32 devices in a mesh: dp: 4 (over z), blk: 2 (over x), ulys: 4 (over y, core).
Axes of the slice: x: 2, y: 2, z: 4, core: 2. Of those that a mesh axis runs over, the one named last changes fastest.
Arguments:
- hidden: float32 [6144, 768], P(('dp', 'blk', 'ulys')), may hold values from -6 to 6
- time_embed: float32 [4, 768], P('dp'), may hold values from -6 to 6
- segment_ids: int32 [4, 1536], P('dp', 'blk'), may hold values from 0 to 7, never falling along the last dimension, each value on 1 to 384 neighbouring positions
- key_valid: int32 [4, 1536], P('dp', 'blk'), may hold values 0 or 1
- out_grad: float32 [6144, 768], P(('dp', 'blk', 'ulys')), may hold values from -6 to 6
- w_query: float32 [768, 768], P(('blk', 'ulys')), may hold values from -0.21875 to 0.21875
- b_query: float32 [768], P(('blk', 'ulys')), may hold values from -3 to 3
- w_key: float32 [768, 768], P(('blk', 'ulys')), may hold values from -0.21875 to 0.21875
- w_value: float32 [768, 768], P(('blk', 'ulys')), may hold values from -0.21875 to 0.21875
- b_value: float32 [768], P(('blk', 'ulys')), may hold values from -3 to 3
- w_out: float32 [768, 768], P(('blk', 'ulys')), may hold values from -3 to 3
- b_out: float32 [768], P(('blk', 'ulys')), may hold values from -3 to 3
- w_up: float32 [768, 3072], P(('blk', 'ulys')), may hold values from -0.21875 to 0.21875
- b_up: float32 [3072], P(('blk', 'ulys')), may hold values from -3 to 3
- w_down: float32 [3072, 768], P(('blk', 'ulys')), may hold values from -0.109375 to 0.109375
- b_down: float32 [768], P(('blk', 'ulys')), may hold values from -3 to 3
- pre_gain: float32 [768], P(('blk', 'ulys')), may hold values from 0.5 to 1.5
- pre_shift: float32 [768], P(('blk', 'ulys')), may hold values from -3 to 3
- mlp_gain: float32 [768], P(('blk', 'ulys')), may hold values from 0.5 to 1.5
- mlp_shift: float32 [768], P(('blk', 'ulys')), may hold values from -3 to 3
Outputs:
- output: float32 [6144, 768], P(('dp', 'blk', 'ulys'))
- hidden_grad: float32 [6144, 768], P(('dp', 'blk', 'ulys'))
- grad_query: float32 [768, 768], P(('blk', 'ulys'))
- grad_qbias: float32 [768], P(('blk', 'ulys'))
- grad_key: float32 [768, 768], P(('blk', 'ulys'))
- grad_value: float32 [768, 768], P(('blk', 'ulys'))
- grad_vbias: float32 [768], P(('blk', 'ulys'))
- grad_outproj: float32 [768, 768], P(('blk', 'ulys'))
- grad_obias: float32 [768], P(('blk', 'ulys'))
- grad_upproj: float32 [768, 3072], P(('blk', 'ulys'))
- grad_upbias: float32 [3072], P(('blk', 'ulys'))
- grad_downproj: float32 [3072, 768], P(('blk', 'ulys'))
- grad_downbias: float32 [768], P(('blk', 'ulys'))
- prenorm_gain_gradient: float32 [768], P(('blk', 'ulys'))
- prenorm_shift_gradient: float32 [768], P(('blk', 'ulys'))
- grad_mlpgain: float32 [768], P(('blk', 'ulys'))
- grad_mlpshift: float32 [768], P(('blk', 'ulys'))
The draws below stay inside these ranges and needn't reach their ends.
Inputs may be any that keep to these rules, and one draw needn't show every extreme that they name: `segment_ids`: segment ids never fall along a sequence; a document holds at most 384 tokens, and some document of each sequence holds exactly that many.
All inputs are finite; a program needn't handle non-finite values. No bound on the sum of `key_valid` on one device may be relied on, other than what follows from the above.
Results may differ from the reference program's by a relative error of at most 0.0003.
Values sent between devices are 32-bit elements; how exact they have to be, the bound alone decides.
No kernel may reach another device: no remote copies, remote signals or barrier semaphores. Data moves between devices by JAX's collectives and lax.ppermute only.
A program may use at most 192 MiB of HBM per device.

```python
import math
import jax
import jax.numpy as jnp
import numpy as np
from jax import lax

D = 768
HEADS = 12
HEAD_DIM = 64
FF = 3072
LEN = 1536
SEQS = 4
TOKENS = 6144


def plant(array, own_key, least, top_value):
    longest = array.shape.index(max(array.shape))
    spots = []
    for shift in (0, 1):
        where = [jax.random.randint(jax.random.fold_in(own_key, axis), (), 0, length) for axis, length in enumerate(array.shape)]
        where[longest] = (where[longest] + shift) % array.shape[longest]
        spots.append(tuple(where))
    return array.at[spots[0]].set(least).at[spots[1]].set(top_value)


def block_levels(key, extent, cuts, least, largest):
    def one(dim, shards_of):
        steps = jax.random.uniform(jax.random.fold_in(jax.random.fold_in(key, 6), dim), (shards_of,), jnp.float32, least / len(cuts), largest / len(cuts))
        return jnp.repeat(jnp.exp(steps), extent[dim] // shards_of).reshape((-1,) + (1,) * (len(extent) - dim - 1))

    factor_of = one(*cuts[0])
    for cut in cuts[1:]:
        factor_of = factor_of * one(*cut)
    return factor_of


def profile(amount, total, limit, lean):
    loads = [(1 << 20) // math.isqrt(grade ** lean) + 1 for grade in range(2, amount + 1)]
    spare, given = total - limit - (amount - 1), [1] * (amount - 1)
    while spare > 0:
        movable = [i for i in range(amount - 1) if given[i] < limit]
        mass, budget = sum([loads[i] for i in movable]), spare
        for i in movable:
            extra = min(limit - given[i], max(1, budget * loads[i] // mass), spare)
            given[i] = given[i] + extra
            spare = spare - extra
    return np.array([limit] + given)


def ragged(key, number_of, total, most, skew):
    if number_of == 2:
        one = jax.random.randint(key, (), max(1, total - most), min(most, total - 1) + 1)
        return jnp.stack([one, total - one])
    lengths = jnp.asarray(profile(number_of, total, most, skew), jnp.int32)
    couples = (number_of - 1) // 2
    giver, sink = lengths[1:1 + 2 * couples:2], lengths[2:2 + 2 * couples:2]
    room = jnp.minimum(giver - 1, most - sink)
    passed = jax.random.randint(jax.random.fold_in(key, 1), (couples,), 0, 1 << 20) % (room + 1)
    lengths = lengths.at[1:1 + 2 * couples:2].set(giver - passed).at[2:2 + 2 * couples:2].set(sink + passed)
    return lengths[jax.random.permutation(jax.random.fold_in(key, 2), number_of)]


def bell_draw(stream_key, shape, spread, bound, pieces=(), kind=jnp.bfloat16):
    entries = spread * jax.random.normal(stream_key, shape, jnp.float32)
    if pieces:
        entries = entries * block_levels(stream_key, shape, pieces, -0.22, 0.18)
    return jnp.clip(entries, -bound, bound).astype(kind)


def setup_inputs(seed: int = 0) -> dict:
    key_of = jax.random.split(jax.random.key(seed), 21)
    return {
        "hidden": bell_draw(key_of[0], (TOKENS, D), 1.0, 6.0, ((0, 32),), jnp.float32),
        "time_embed": bell_draw(key_of[1], (SEQS, D), 1.0, 6.0, ((0, 4),), jnp.float32),
        "segment_ids": jax.vmap(lambda own: jnp.searchsorted(jnp.cumsum(ragged(own, 8, LEN, LEN // 4, 0)), jnp.arange(LEN), side="right"))(jax.random.split(key_of[2], SEQS)).reshape((SEQS, LEN)).astype(jnp.int32),
        "key_valid": plant((jax.random.randint(key_of[3], (SEQS, LEN), 0, 8) < 7).astype(jnp.int32), jax.random.fold_in(key_of[3], 1), 0, 1),
        "out_grad": bell_draw(key_of[4], (TOKENS, D), 1.0, 6.0, ((0, 32),), jnp.float32),
        "w_query": bell_draw(key_of[5], (D, D), D ** -0.5, 0.21875, ((0, 8),), jnp.float32),
        "b_query": bell_draw(key_of[6], (D,), 0.5, 3.0, ((0, 8),), jnp.float32),
        "w_key": bell_draw(key_of[7], (D, D), D ** -0.5, 0.21875, ((0, 8),), jnp.float32),
        "w_value": bell_draw(key_of[8], (D, D), D ** -0.5, 0.21875, ((0, 8),), jnp.float32),
        "b_value": bell_draw(key_of[9], (D,), 0.5, 3.0, ((0, 8),), jnp.float32),
        "w_out": bell_draw(key_of[10], (D, D), (max(1, D * 8 // LEN)) ** -0.5, 3.0, ((0, 8),), jnp.float32),
        "b_out": bell_draw(key_of[11], (D,), 0.5, 3.0, ((0, 8),), jnp.float32),
        "w_up": bell_draw(key_of[12], (D, FF), D ** -0.5, 0.21875, ((0, 8),), jnp.float32),
        "b_up": bell_draw(key_of[13], (FF,), 0.5, 3.0, ((0, 8),), jnp.float32),
        "w_down": bell_draw(key_of[14], (FF, D), FF ** -0.5, 0.109375, ((0, 8),), jnp.float32),
        "b_down": bell_draw(key_of[15], (D,), 0.5, 3.0, ((0, 8),), jnp.float32),
        "pre_gain": jnp.clip(0.5 + 1.0 * jax.random.uniform(key_of[16], (D,), jnp.float32) ** block_levels(key_of[16], (D,), ((0, 8),), -0.2, 0.2), 0.5, 1.5),
        "pre_shift": bell_draw(key_of[17], (D,), 0.5, 3.0, ((0, 8),), jnp.float32),
        "mlp_gain": jnp.clip(0.5 + 1.0 * jax.random.uniform(key_of[18], (D,), jnp.float32) ** block_levels(key_of[18], (D,), ((0, 8),), -0.2, 0.2), 0.5, 1.5),
        "mlp_shift": bell_draw(key_of[19], (D,), 0.5, 3.0, ((0, 8),), jnp.float32),
    }


HIGH = lax.Precision.HIGHEST
floor_score = -1e+30

def layer_normalize(values, gain, shift):
    average = lax.optimization_barrier(jnp.mean(values, axis=-1, keepdims=True))
    centred = values - average
    variance = lax.optimization_barrier(jnp.mean(centred * centred, axis=-1, keepdims=True))
    return centred * lax.rsqrt(variance + 1e-05) * gain + shift

def gelu_tanh(values):
    return 0.5 * values * (1.0 + jnp.tanh(0.7978845608028654 * (values + 0.044715 * values * values * values)))

def attend_sequence(query, keys, values, segments, valid):
    block = math.gcd(LEN, 1024)
    count = LEN // block
    scale = HEAD_DIM ** (-0.5)
    query_blocks = query.reshape(count, block, HEADS, HEAD_DIM)
    key_split = keys.reshape(LEN, HEADS, HEAD_DIM)
    value_split = values.reshape(LEN, HEADS, HEAD_DIM)
    positions = jnp.arange(LEN, dtype=jnp.int32)
    starts = (jnp.arange(count, dtype=jnp.int32) * block).astype(jnp.int32)

    def one_block(item):
        query_block, start = item
        rows = start + jnp.arange(block, dtype=jnp.int32)
        query_segments = lax.dynamic_slice_in_dim(segments, start, block)
        allowed = (query_segments[:, None] == segments[None, :]) & ((valid[None, :] == 1) | (rows[:, None] == positions[None, :]))
        scores = jnp.einsum('qhd,khd->hqk', query_block, key_split, precision=HIGH) * scale
        scores = jnp.where(allowed[None], scores, floor_score)
        weights = jax.nn.softmax(scores, axis=-1)
        return jnp.einsum('hqk,khd->qhd', weights, value_split, precision=HIGH).reshape(block, D)
    return lax.map(jax.checkpoint(one_block), (query_blocks, starts)).reshape(LEN, D)

def reference(hidden, time_embed, segment_ids, key_valid, out_grad, w_query, b_query, w_key, w_value, b_value, w_out, b_out, w_up, b_up, w_down, b_down, pre_gain, pre_shift, mlp_gain, mlp_shift):

    def forward(hidden_in, params):
        proj_query, bias_query, proj_key, proj_value, bias_value, proj_out, bias_out, proj_up, bias_up, proj_down, bias_down, gain_pre, shift_pre, gain_mlp, shift_mlp = params
        residual_input = hidden_in.reshape(SEQS, LEN, D) + time_embed[:, None, :]
        normalized_rows = layer_normalize(residual_input, gain_pre, shift_pre)
        query = jnp.dot(normalized_rows, proj_query, precision=HIGH) + bias_query
        keys = jnp.dot(normalized_rows, proj_key, precision=HIGH)
        values = jnp.dot(normalized_rows, proj_value, precision=HIGH) + bias_value
        attended = lax.map(lambda item: attend_sequence(*item), (query, keys, values, segment_ids, key_valid))
        middle = residual_input + jnp.dot(attended, proj_out, precision=HIGH) + bias_out
        mlp_in = layer_normalize(middle, gain_mlp, shift_mlp)
        activated = gelu_tanh(jnp.dot(mlp_in, proj_up, precision=HIGH) + bias_up)
        result = middle + jnp.dot(activated, proj_down, precision=HIGH) + bias_down
        return result.reshape(TOKENS, D)
    params = (w_query, b_query, w_key, w_value, b_value, w_out, b_out, w_up, b_up, w_down, b_down, pre_gain, pre_shift, mlp_gain, mlp_shift)
    output, backward = jax.vjp(forward, hidden, params)
    hidden_grad, grads = backward(out_grad)
    return (output, hidden_grad, grads[0], grads[1], grads[2], grads[3], grads[4], grads[5], grads[6], grads[7], grads[8], grads[9], grads[10], grads[11], grads[12], grads[13], grads[14])
```

```python
import functools
import math

import jax, jax.numpy as jnp
from jax import lax
from jax.experimental import pallas as pl
from jax.experimental.pallas import tpu as pltpu
from jax.sharding import PartitionSpec as P

HEAD_DIM = 64
FLOOR = -1e30
BF = jnp.bfloat16
F32 = jnp.float32
NT = (((1,), (1,)), ((), ()))
NN = (((1,), (0,)), ((), ()))


def split(x):
    hi = x.astype(BF)
    return hi, (x - hi.astype(F32)).astype(BF)


def mm(a, b, dims=NN):
    return lax.dot_general(a, b, dims, preferred_element_type=F32)


def attend_kernel(tile, heads, seg_ref, qcode_ref, kcode_ref, q_ref, k_ref, v_ref,
                  out_ref, lse_ref, qc, kc, vt, m_s, l_s, acc):
    group, keys = q_ref.shape[0], k_ref.shape[0]
    nq, nk = group // tile, keys // tile
    scale = HEAD_DIM ** -0.5
    for h in range(heads):
        lane = slice(h * HEAD_DIM, (h + 1) * HEAD_DIM)
        hi, lo = split(q_ref[:, lane] * scale)
        qc[h] = jnp.concatenate([hi, hi, lo], axis=1)
        hi, lo = split(k_ref[:, lane])
        kc[h] = jnp.concatenate([hi, lo, hi], axis=1)
    for j in range(nk):
        rows = slice(j * tile, (j + 1) * tile)
        vtile = v_ref[rows, :].T
        for h in range(heads):
            hi, lo = split(vtile[h * HEAD_DIM:(h + 1) * HEAD_DIM])
            vt[h, j] = jnp.concatenate([hi, lo], axis=0)

    def per_q(i, _):
        qrow = pl.ds(pl.multiple_of(i * tile, tile), tile)
        m_s[...] = jnp.full_like(m_s, FLOOR)
        l_s[...] = jnp.zeros_like(l_s)
        acc[...] = jnp.zeros_like(acc)
        first, last = seg_ref[0, 2 * i], seg_ref[0, 2 * i + 1]
        qcode = qcode_ref[:, qrow]

        def per_k(j, _):
            @pl.when((seg_ref[0, 2 * (nq + j) + 1] >= first) & (seg_ref[0, 2 * (nq + j)] <= last))
            def _():
                krow = pl.ds(pl.multiple_of(j * tile, tile), tile)
                kcode = kcode_ref[krow, :]
                gap = (i - j) * tile
                same = (lax.broadcasted_iota(jnp.int32, (tile, tile), 0)
                        - lax.broadcasted_iota(jnp.int32, (tile, tile), 1)) == gap
                allowed = (kcode == qcode) | same
                for h in range(heads):
                    s = mm(kc[h, krow, :], qc[h, qrow, :], NT)
                    s = jnp.where(allowed, s, FLOOR)
                    m_old = m_s[h]
                    m_new = jnp.maximum(m_old, jnp.max(s, axis=0, keepdims=True))
                    p = jnp.where(allowed, jnp.exp(s - m_new), 0.0)
                    factor = jnp.exp(m_old - m_new)
                    m_s[h] = m_new
                    l_s[h] = l_s[h] * factor + jnp.sum(p, axis=0, keepdims=True)
                    hi, lo = split(p)
                    v128 = vt[h, j]
                    acc[h] = acc[h] * factor + mm(v128, hi) + mm(v128, lo)
            return 0

        lax.fori_loop(0, nk, per_k, 0)
        parts = []
        for h in range(heads):
            total = l_s[h]
            parts.append((acc[h, :HEAD_DIM] + acc[h, HEAD_DIM:]) / total)
            lse_ref[h:h + 1, qrow] = m_s[h] + jnp.log(total)
        out_ref[qrow, :] = jnp.concatenate(parts, axis=0).T
        return 0

    lax.fori_loop(0, nq, per_q, 0)


def attend(segs, qcode, kcode, q, k, v, tile):
    group, width = q.shape
    keys = k.shape[0]
    heads = width // HEAD_DIM
    vm = pl.BlockSpec(memory_space=pltpu.VMEM)
    return pl.pallas_call(
        functools.partial(attend_kernel, tile, heads),
        out_shape=(jax.ShapeDtypeStruct((group, width), F32),
                   jax.ShapeDtypeStruct((8, group), F32)),
        in_specs=[pl.BlockSpec(memory_space=pltpu.SMEM)] + [vm] * 5,
        out_specs=(vm, vm),
        scratch_shapes=[
            pltpu.VMEM((heads, group, 3 * HEAD_DIM), BF),
            pltpu.VMEM((heads, keys, 3 * HEAD_DIM), BF),
            pltpu.VMEM((heads, keys // tile, 2 * HEAD_DIM, tile), BF),
            pltpu.VMEM((heads, 1, tile), F32),
            pltpu.VMEM((heads, 1, tile), F32),
            pltpu.VMEM((heads, 2 * HEAD_DIM, tile), F32),
        ],
        compiler_params=pltpu.CompilerParams(vmem_limit_bytes=40 << 20),
        cost_estimate=pl.CostEstimate(flops=4 * group * keys * width * 2, bytes_accessed=4 * width * (2 * group + 2 * keys),
                                      transcendentals=group * keys * heads),
        name="attend",
    )(segs, qcode, kcode, q, k, v)


def attend_back_kernel(tile, heads, seg_ref, qcode_ref, kcode_ref, q_ref, k_ref, v_ref, o_ref, do_ref, lse_ref,
                       dq_ref, dk_ref, dv_ref, qc, kc, vc, dc, q2, d2, kt, dot_s, dqa, dka, dva):
    group, keys = q_ref.shape[0], k_ref.shape[0]
    nq, nk = group // tile, keys // tile
    scale = HEAD_DIM ** -0.5
    for h in range(heads):
        lane = slice(h * HEAD_DIM, (h + 1) * HEAD_DIM)
        hi, lo = split(q_ref[:, lane] * scale)
        qc[h] = jnp.concatenate([hi, hi, lo], axis=1)
        q2[h] = jnp.concatenate([hi, lo], axis=1)
        hi, lo = split(do_ref[:, lane])
        dc[h] = jnp.concatenate([hi, hi, lo], axis=1)
        d2[h] = jnp.concatenate([hi, lo], axis=1)
        hi, lo = split(k_ref[:, lane])
        kc[h] = jnp.concatenate([hi, lo, hi], axis=1)
        hi, lo = split(v_ref[:, lane])
        vc[h] = jnp.concatenate([hi, lo, hi], axis=1)
    for j in range(nk):
        rows = slice(j * tile, (j + 1) * tile)
        ktile = k_ref[rows, :].T
        for h in range(heads):
            hi, lo = split(ktile[h * HEAD_DIM:(h + 1) * HEAD_DIM])
            kt[h, j] = jnp.concatenate([hi, lo], axis=0)
    for i in range(nq):
        rows = slice(i * tile, (i + 1) * tile)
        prod = (o_ref[rows, :] * do_ref[rows, :]).T
        for h in range(heads):
            dot_s[h, :, rows] = jnp.sum(prod[h * HEAD_DIM:(h + 1) * HEAD_DIM], axis=0, keepdims=True)
    dqa[...] = jnp.zeros_like(dqa)

    def per_k(j, _):
        krow = pl.ds(pl.multiple_of(j * tile, tile), tile)
        kcode = kcode_ref[krow, :]
        kfirst, klast = seg_ref[0, 2 * (nq + j)], seg_ref[0, 2 * (nq + j) + 1]
        dka[...] = jnp.zeros_like(dka)
        dva[...] = jnp.zeros_like(dva)

        def per_q(i, _):
            @pl.when((klast >= seg_ref[0, 2 * i]) & (kfirst <= seg_ref[0, 2 * i + 1]))
            def _():
                qrow = pl.ds(pl.multiple_of(i * tile, tile), tile)
                gap = (i - j) * tile
                same = (lax.broadcasted_iota(jnp.int32, (tile, tile), 0)
                        - lax.broadcasted_iota(jnp.int32, (tile, tile), 1)) == gap
                allowed = (kcode == qcode_ref[:, qrow]) | same
                for h in range(heads):
                    s = mm(kc[h, krow, :], qc[h, qrow, :], NT)
                    p = jnp.exp(jnp.where(allowed, s - lse_ref[h:h + 1, qrow], FLOOR))
                    dp = mm(vc[h, krow, :], dc[h, qrow, :], NT)
                    ds = p * (dp - dot_s[h, :, qrow])
                    hi, lo = split(p)
                    d128 = d2[h, qrow, :]
                    dva[h] += mm(hi, d128) + mm(lo, d128)
                    hi, lo = split(ds)
                    q128 = q2[h, qrow, :]
                    dka[h] += mm(hi, q128) + mm(lo, q128)
                    k128 = kt[h, j]
                    dqa[h, i] += mm(k128, hi) + mm(k128, lo)
            return 0

        lax.fori_loop(0, nq, per_q, 0)
        dk_ref[krow, :] = jnp.concatenate([dka[h, :, :HEAD_DIM] + dka[h, :, HEAD_DIM:] for h in range(heads)], axis=1)
        dv_ref[krow, :] = jnp.concatenate([dva[h, :, :HEAD_DIM] + dva[h, :, HEAD_DIM:] for h in range(heads)], axis=1)
        return 0

    lax.fori_loop(0, nk, per_k, 0)
    for i in range(nq):
        parts = [(dqa[h, i, :HEAD_DIM] + dqa[h, i, HEAD_DIM:]) * scale for h in range(heads)]
        dq_ref[i * tile:(i + 1) * tile, :] = jnp.concatenate(parts, axis=0).T


def attend_back(segs, qcode, kcode, q, k, v, o, do, lse, tile):
    group, width = q.shape
    keys = k.shape[0]
    heads = width // HEAD_DIM
    vm = pl.BlockSpec(memory_space=pltpu.VMEM)
    H3, H2 = 3 * HEAD_DIM, 2 * HEAD_DIM
    return pl.pallas_call(
        functools.partial(attend_back_kernel, tile, heads),
        out_shape=(jax.ShapeDtypeStruct((group, width), F32),
                   jax.ShapeDtypeStruct((keys, width), F32),
                   jax.ShapeDtypeStruct((keys, width), F32)),
        in_specs=[pl.BlockSpec(memory_space=pltpu.SMEM)] + [vm] * 8,
        out_specs=(vm, vm, vm),
        scratch_shapes=[
            pltpu.VMEM((heads, group, H3), BF),
            pltpu.VMEM((heads, keys, H3), BF),
            pltpu.VMEM((heads, keys, H3), BF),
            pltpu.VMEM((heads, group, H3), BF),
            pltpu.VMEM((heads, group, H2), BF),
            pltpu.VMEM((heads, group, H2), BF),
            pltpu.VMEM((heads, keys // tile, H2, tile), BF),
            pltpu.VMEM((heads, 1, group), F32),
            pltpu.VMEM((heads, group // tile, H2, tile), F32),
            pltpu.VMEM((heads, tile, H2), F32),
            pltpu.VMEM((heads, tile, H2), F32),
        ],
        compiler_params=pltpu.CompilerParams(vmem_limit_bytes=48 << 20),
        cost_estimate=pl.CostEstimate(flops=10 * group * keys * width * 2, bytes_accessed=4 * width * (4 * group + 4 * keys),
                                      transcendentals=group * keys * heads),
        name="attend_back",
    )(segs, qcode, kcode, q, k, v, o, do, lse)


HIGH = lax.Precision.HIGH
SQRT_2_PI = 0.7978845608028654
CUBIC = 0.044715
TILE = 256


def dot(left, right):
    return jnp.dot(left, right, precision=HIGH)


def dot_left_t(left, right):
    return lax.dot_general(left, right, (((0,), (0,)), ((), ())), precision=HIGH)


def dot_right_t(left, right):
    return lax.dot_general(left, right, (((1,), (1,)), ((), ())), precision=HIGH)


def normalize(values):
    centred = values - jnp.mean(values, axis=-1, keepdims=True)
    inverse = lax.rsqrt(jnp.mean(centred * centred, axis=-1, keepdims=True) + 1e-05)
    return centred * inverse, inverse


def normalize_back(grad, gain, xhat, inverse):
    scaled = grad * gain
    mean = jnp.mean(scaled, axis=-1, keepdims=True)
    lean = jnp.mean(scaled * xhat, axis=-1, keepdims=True)
    return (scaled - mean - xhat * lean) * inverse


def swap(value, axis, mask):
    count = lax.axis_size(axis)
    return lax.ppermute(value, axis, [(i, i ^ mask) for i in range(count)])


def bits_of(axis):
    return lax.axis_size(axis).bit_length() - 1


def gather_axis(value, axis):
    here = lax.axis_index(axis)
    bits = bits_of(axis)
    shape = value.shape
    for level in range(bits):
        bit = bits - 1 - level
        other = swap(value, axis, 1 << bit)
        low = (here >> bit) & 1 == 0
        value = jnp.stack([jnp.where(low, value, other), jnp.where(low, other, value)], axis=level)
    return value.reshape((1 << bits,) + shape)


def scatter_axis(value, axis):
    here = lax.axis_index(axis)
    bits = bits_of(axis)
    shape = value.shape[1:]
    value = value.reshape((2,) * bits + shape)
    for bit in range(bits):
        level = bits - 1 - bit
        zero, one = (lax.index_in_dim(value, i, level, keepdims=False) for i in (0, 1))
        low = (here >> bit) & 1 == 0
        value = jnp.where(low, zero, one) + swap(jnp.where(low, one, zero), axis, 1 << bit)
    return value.reshape(shape)


def sum_half(value, masks):
    here = lax.axis_index("dp")
    sides = {1: (here ^ (here >> 1)) & 1, 3: here >> 1}
    for mask in masks:
        zero, one = jnp.split(value, 2, axis=0)
        low = sides[mask] == 0
        value = jnp.where(low, zero, one) + swap(jnp.where(low, one, zero), "dp", mask)
    for mask in masks[::-1]:
        other = swap(value, "dp", mask)
        low = sides[mask] == 0
        value = jnp.concatenate([jnp.where(low, value, other), jnp.where(low, other, value)], axis=0)
    return value


def sum_sequences(value):
    if lax.axis_size("dp") != 4 or value.shape[0] % 64:
        return lax.psum(value, "dp")
    first, second = jnp.split(value, 2, axis=0)
    return jnp.concatenate([sum_half(first, (1, 3)), sum_half(second, (3, 1))], axis=0)


def halo_moves(group, reach, blocks):
    moves = []
    shift = 1
    while reach > 0 and shift < blocks:
        rows = min(group, reach)
        moves.append((rows, True, [(i, i - shift) for i in range(shift, blocks)]))
        moves.append((rows, False, [(i, i + shift) for i in range(blocks - shift)]))
        reach -= rows
        shift += 1
    return moves


def halo_get(value, reach, axis=0):
    blocks, group = lax.axis_size("blk"), value.shape[axis]
    if blocks == 2 and reach <= group:
        first = lax.slice_in_dim(value, 0, reach, axis=axis)
        last = lax.slice_in_dim(value, group - reach, group, axis=axis)
        return swap(jnp.where(lax.axis_index("blk") == 0, last, first), "blk", 1)
    parts = []
    for rows, right, moves in halo_moves(group, reach, blocks):
        start = 0 if right else group - rows
        parts.append(lax.ppermute(lax.slice_in_dim(value, start, start + rows, axis=axis), "blk", moves))
    return jnp.concatenate(parts, axis=axis)


def halo_add(value, halo, reach):
    blocks, group = lax.axis_size("blk"), value.shape[0]
    if blocks == 2 and reach <= group:
        back = swap(halo, "blk", 1)
        spare = ((0, group - reach), (0, 0))
        return value + jnp.where(lax.axis_index("blk") == 0, jnp.pad(back, ((group - reach, 0), (0, 0))), jnp.pad(back, spare))
    start = 0
    for rows, right, moves in halo_moves(group, reach, blocks):
        back = lax.ppermute(halo[start:start + rows], "blk", [(j, i) for i, j in moves])
        start += rows
        room = group - rows
        value = value + jnp.pad(back, ((0, room), (0, 0)) if right else ((room, 0), (0, 0)))
    return value


def local(
    hidden,
    time_embed,
    segment_ids,
    key_valid,
    out_grad,
    w_query,
    b_query,
    w_key,
    w_value,
    b_value,
    w_out,
    b_out,
    w_up,
    b_up,
    w_down,
    b_down,
    pre_gain,
    pre_shift,
    mlp_gain,
    mlp_shift,
):
    blocks, splits = lax.axis_size("blk"), lax.axis_size("ulys")
    here_b, here_u = lax.axis_index("blk"), lax.axis_index("ulys")
    both = ("blk", "ulys")
    owners = blocks * splits
    tokens, width = hidden.shape
    group = tokens * splits
    part = width // splits
    rows = w_query.shape[0]
    units = w_up.shape[1]
    unit_rows = w_down.shape[0]
    share = units // splits
    reach = group * blocks // 4

    def mine(value):
        return lax.dynamic_slice_in_dim(value, here_u * tokens, tokens, 0)

    small = jnp.concatenate([b_query, b_value, b_out, b_down, pre_gain, pre_shift, mlp_gain, mlp_shift, b_up])
    small_rows = -(-small.shape[0] // (3 * part))
    small_rows += -small_rows % 8
    small_pad = jnp.pad(small, (0, small_rows * 3 * part - small.shape[0])).reshape(1, small_rows, 3 * part)
    qkv_cut = jnp.stack([w_query, w_key, w_value], axis=1).reshape(rows, 3, splits, part)
    qkv_cut = qkv_cut.transpose(2, 0, 1, 3).reshape(splits, rows, 3 * part)
    message = jnp.concatenate([qkv_cut, jnp.broadcast_to(small_pad, (splits, small_rows, 3 * part))], axis=1)
    message = jnp.broadcast_to(message[None], (blocks,) + message.shape).reshape(owners, rows + small_rows, 3 * part)
    message = lax.all_to_all(message, both, 0, 0, tiled=True)
    base = gather_axis(hidden + time_embed, "ulys").reshape(group, width)
    own_segments = segment_ids[0] + 1
    own_codes = jnp.stack([own_segments, jnp.where(key_valid[0] == 1, own_segments, 0)]).astype(jnp.float32)
    halo_codes = halo_get(own_codes, reach, axis=1)
    w_qkv = message[:, :rows].reshape(width, 3 * part)
    smalls = message[:, rows:].reshape(owners, -1)
    vectors = [smalls[:, i * rows:(i + 1) * rows].reshape(width) for i in range(8)]
    full_qbias, full_vbias, full_obias, full_downbias, gain1, shift1, gain2, shift2 = vectors
    up_bias = smalls[:, 8 * rows:8 * rows + unit_rows].reshape(blocks, splits, unit_rows)
    up_bias = lax.dynamic_index_in_dim(up_bias, here_u, 1, keepdims=False).reshape(share)

    xhat1, inverse1 = normalize(base)
    normed = xhat1 * gain1 + shift1
    bias_here = jnp.concatenate(
        [
            lax.dynamic_slice_in_dim(full_qbias, here_u * part, part),
            jnp.zeros((part,), jnp.float32),
            lax.dynamic_slice_in_dim(full_vbias, here_u * part, part),
        ]
    )
    qkv = dot(normed, w_qkv) + bias_here
    query, key_value = qkv[:, :part], qkv[:, part:]

    window = group + halo_codes.shape[1]
    spare = -window % TILE
    halo = halo_get(key_value, reach)
    all_kv = jnp.pad(jnp.concatenate([key_value, halo], axis=0), ((0, spare), (0, 0)))
    all_codes = jnp.pad(jnp.concatenate([own_codes, halo_codes], axis=1), ((0, 0), (0, spare)))
    all_keys, all_values = all_kv[:, :part], all_kv[:, part:]
    window_segments = all_codes[0].astype(jnp.int32).reshape(-1, TILE)
    query_segments = own_segments.reshape(-1, TILE)
    bounds = jnp.concatenate(
        [
            jnp.stack([query_segments[:, 0], query_segments[:, -1]], axis=1),
            jnp.stack(
                [
                    jnp.min(jnp.where(window_segments == 0, 1 << 20, window_segments), axis=1),
                    jnp.max(window_segments, axis=1),
                ],
                axis=1,
            ),
        ],
        axis=0,
    ).reshape(1, -1)
    query_codes = own_codes[:1]
    key_codes = all_codes[1][:, None]
    attended, normalizer = attend(bounds, query_codes, key_codes, query, all_keys, all_values, TILE)

    full_out = lax.all_gather(w_out, both, axis=0, tiled=True)
    up_cut = w_up.reshape(rows, blocks, splits, unit_rows).transpose(2, 0, 1, 3).reshape(splits, rows, share)
    up_cut = jnp.broadcast_to(up_cut[None], (blocks,) + up_cut.shape).reshape(owners, rows, share)
    up_here = lax.all_to_all(up_cut, both, 0, 0, tiled=True).reshape(width, share)
    down_here = gather_axis(w_down, "blk").reshape(share, width)
    out_grads = gather_axis(out_grad, "ulys").reshape(group, width)

    attended_all = gather_axis(attended, "ulys")
    middle = base + full_obias
    for i in range(splits):
        middle = middle + dot(attended_all[i], full_out[i * part:(i + 1) * part])
    xhat2, inverse2 = normalize(middle)
    mlp_in = xhat2 * gain2 + shift2
    pre_act = dot(mlp_in, up_here) + up_bias
    curve = jnp.tanh(SQRT_2_PI * (pre_act + CUBIC * pre_act * pre_act * pre_act))
    activated = 0.5 * pre_act * (1.0 + curve)
    slope = 0.5 * (1.0 + curve) + 0.5 * pre_act * (1.0 - curve * curve) * SQRT_2_PI * (
        1.0 + 3.0 * CUBIC * pre_act * pre_act
    )
    pre_grad = dot_right_t(out_grads, down_here) * slope
    mlp_in_grads = dot_right_t(pre_grad, up_here)
    mlp_in_grad = scatter_axis(mlp_in_grads.reshape(splits, tokens, width), "ulys")
    grad_down = dot_left_t(activated, out_grads)
    grad_up = dot_left_t(mlp_in, pre_grad)
    output = scatter_axis(dot(activated, down_here).reshape(splits, tokens, width), "ulys")
    output = output + mine(middle) + full_downbias

    feed_grads = jnp.concatenate(
        [grad_down.reshape(blocks, unit_rows, width), grad_up.reshape(blocks, splits * rows, share)], axis=1
    )
    feed_grads = lax.psum_scatter(feed_grads, "blk", scatter_dimension=0, tiled=False)
    feed_grads = lax.psum(feed_grads, "dp")
    total_down = feed_grads[:unit_rows]
    total_up = lax.all_to_all(feed_grads[unit_rows:].reshape(splits, rows, share), "ulys", 0, 0, tiled=True)
    total_up = total_up.reshape(splits, rows, blocks, unit_rows).transpose(1, 2, 0, 3).reshape(rows, units)

    middle_grad = out_grad + normalize_back(mlp_in_grad, gain2, mine(xhat2), mine(inverse2))
    middle_grads = gather_axis(middle_grad, "ulys").reshape(group, width)
    out_here = lax.dynamic_slice_in_dim(full_out, here_u * part, part, 0)
    attended_grad = dot_right_t(middle_grads, out_here)
    grad_out = dot_left_t(attended, middle_grads)

    query_grad, keys_grad, values_grad = attend_back(
        bounds, query_codes, key_codes, query, all_keys, all_values, attended, attended_grad, normalizer, TILE
    )
    pair_grad = jnp.concatenate([keys_grad, values_grad], axis=1)
    pair_grad = halo_add(pair_grad[:group], pair_grad[group:window], reach)
    qkv_grad = jnp.concatenate([query_grad, pair_grad], axis=1)
    grad_qkv = dot_left_t(normed, qkv_grad)
    normed_grads = dot_right_t(qkv_grad, w_qkv)
    normed_grad = scatter_axis(normed_grads.reshape(splits, tokens, width), "ulys")
    hidden_grad = middle_grad + normalize_back(normed_grad, gain1, mine(xhat1), mine(inverse1))

    column_sums = jnp.sum(qkv_grad, axis=0)
    place = lambda piece: lax.dynamic_update_slice_in_dim(jnp.zeros((width,), jnp.float32), piece, here_u * part, 0)
    terms = [
        place(column_sums[:part]),
        place(column_sums[2 * part:]),
        jnp.sum(middle_grad, axis=0),
        jnp.sum(out_grad, axis=0),
        jnp.sum(normed_grads * xhat1, axis=0),
        jnp.sum(normed_grads, axis=0),
        jnp.sum(mlp_in_grads * xhat2, axis=0),
        jnp.sum(mlp_in_grads, axis=0),
    ]
    up_terms = lax.dynamic_update_slice_in_dim(
        jnp.zeros((blocks, splits, unit_rows), jnp.float32),
        jnp.sum(pre_grad, axis=0).reshape(blocks, 1, unit_rows),
        here_u,
        1,
    ).reshape(owners, unit_rows)
    terms = jnp.concatenate([term.reshape(owners, rows) for term in terms] + [up_terms], axis=1)
    terms = jnp.pad(terms, ((0, 0), (0, small_rows * 3 * part - terms.shape[1])))
    terms = terms.reshape(blocks, splits, small_rows, 3 * part)
    tail = jnp.concatenate([grad_qkv.reshape(blocks, splits, rows, 3 * part), terms], axis=2)
    tail = tail.reshape(blocks, splits * (rows + small_rows), 3 * part)
    tail = jnp.concatenate([tail, grad_out.reshape(blocks, -1, 3 * part)], axis=1)
    tail_rows = tail.shape[1]
    tail = jnp.pad(tail, ((0, 0), (0, -tail_rows % 64), (0, 0)))
    if blocks == 2:
        tail = scatter_axis(tail, "blk")
    else:
        tail = lax.psum_scatter(tail, "blk", scatter_dimension=0, tiled=False)
    tail = sum_sequences(tail)
    cut = splits * (rows + small_rows)
    total_out = tail[cut:tail_rows].reshape(rows, width)
    total_out = lax.ppermute(
        total_out, both, [(i * splits + j, j * blocks + i) for i in range(blocks) for j in range(splits)]
    )
    tail = lax.all_to_all(tail[:cut].reshape(splits, rows + small_rows, 3 * part), "ulys", 0, 0, tiled=True)
    total_qkv = tail[:, :rows].reshape(splits, rows, 3, part).transpose(2, 1, 0, 3).reshape(3, rows, width)
    sums = jnp.sum(tail[:, rows:], axis=0).reshape(-1)
    vector = [sums[i * rows:(i + 1) * rows] for i in range(8)]
    return (
        output,
        hidden_grad,
        total_qkv[0],
        vector[0],
        total_qkv[1],
        total_qkv[2],
        vector[1],
        total_out,
        vector[2],
        total_up,
        sums[8 * rows:8 * rows + unit_rows],
        total_down,
        vector[3],
        vector[4],
        vector[5],
        vector[6],
        vector[7],
    )


def solution(mesh):
    tokens = P(("dp", "blk", "ulys"), None)
    matrix = P(("blk", "ulys"), None)
    vector = P(("blk", "ulys"))
    return jax.shard_map(
        local,
        mesh=mesh,
        in_specs=(
            tokens,
            P("dp", None),
            P("dp", "blk"),
            P("dp", "blk"),
            tokens,
            matrix,
            vector,
            matrix,
            matrix,
            vector,
            matrix,
            vector,
            matrix,
            vector,
            matrix,
            vector,
            vector,
            vector,
            vector,
            vector,
        ),
        out_specs=(
            tokens,
            tokens,
            matrix,
            vector,
            matrix,
            matrix,
            vector,
            matrix,
            vector,
            matrix,
            vector,
            matrix,
            vector,
            vector,
            vector,
            vector,
            vector,
        ),
        check_vma=False,
    )
```

```python
import functools
import math

import jax
import jax.numpy as jnp
from jax import lax
from jax.experimental import pallas as pl
from jax.experimental.pallas import tpu as pltpu
from jax.sharding import PartitionSpec as P

HEAD_DIM = 64
FLOOR = -1e30
SQRT_2_PI = 0.7978845608028654
CUBIC = 0.044715
EXTRA = 16
TILE = 256
EDGE = 128
BF = jnp.bfloat16
F32 = jnp.float32
NN = (((1,), (0,)), ((), ()))
NT = (((1,), (1,)), ((), ()))
TN = (((0,), (0,)), ((), ()))
VM = pl.BlockSpec(memory_space=pltpu.VMEM)
SM = pl.BlockSpec(memory_space=pltpu.SMEM)
LIMITS = {"attend_own": 10, "attend_edge": 10, "back_edge": 12, "back_own": 12, "act": 14, "weights": 16, "feed_grads": 12, "place": 8, "hidden": 6, "middle": 6, "last_grads": 16, "pack": 8}


def split(x):
    hi = x.astype(BF)
    return hi, (x - hi.astype(F32)).astype(BF)


def mm(a, b, dims=NN):
    return lax.dot_general(a, b, dims, preferred_element_type=F32)


def mm3(a, b, dims=NN):
    return mm(a[0], b[0], dims) + (mm(a[0], b[1], dims) + mm(a[1], b[0], dims))


def at(start, size, step=8):
    return pl.ds(pl.multiple_of(start, step), size)


def call(kernel, name, outs, ins, scratch=(), flops=0, smem=1, limit=16, wide=False):
    size = sum(math.prod(x.shape) * x.dtype.itemsize for x in list(outs) + list(ins[smem:]))
    return pl.pallas_call(
        kernel,
        out_shape=tuple(outs),
        in_specs=[SM] * smem + [VM] * (len(ins) - smem),
        out_specs=tuple(VM for _ in outs),
        scratch_shapes=list(scratch),
        compiler_params=pltpu.CompilerParams(vmem_limit_bytes=(48 if wide else LIMITS.get(name, limit)) << 20),
        cost_estimate=pl.CostEstimate(flops=3 * flops, bytes_accessed=size, transcendentals=0),
        name=name,
    )(*ins)


def arr(shape, dtype=F32):
    return jax.ShapeDtypeStruct(tuple(shape), dtype)


def norm(x):
    centred = x - jnp.mean(x, axis=-1, keepdims=True)
    inverse = lax.rsqrt(jnp.mean(centred * centred, axis=-1, keepdims=True) + 1e-05)
    return centred * inverse, inverse


def norm_back(grad, gain, xhat, inverse):
    scaled = grad * gain
    mean = jnp.mean(scaled, axis=-1, keepdims=True)
    lean = jnp.mean(scaled * xhat, axis=-1, keepdims=True)
    return (scaled - mean - xhat * lean) * inverse


def pick(index, choices):
    value = choices[0]
    for i in range(1, len(choices)):
        value = jnp.where(index == i, choices[i], value)
    return value


def pack_kernel(blocks, idx, wq, wk, wv, wup, wout, near, far, near2, far2):
    part, share = near.shape[2] // 3, near2.shape[2]
    splits = wq.shape[1] // part
    unit = share // blocks
    for r in range(splits):
        first, second, k = (near, near2, r) if r < 2 else (far, far2, r - 2)
        for u in range(splits):

            @pl.when(idx[0, r] == u)
            def _():
                for i, w in enumerate((wq, wk, wv)):
                    first[k, :, i * part:(i + 1) * part] = w[:, u * part:(u + 1) * part]
                for b in range(blocks):
                    lane = (b * splits + u) * unit
                    second[k, :, b * unit:(b + 1) * unit] = wup[:, lane:lane + unit]
    near2[2] = wout[...]
    far2[2] = wout[...]


def qkv_kernel(pieces, splits, edge, idx, *refs):
    base, rest = refs[:splits], refs[splits:]
    count = max(p[0] for p in pieces) + 1
    weights = rest[:count]
    (q_ref, kv_ref, edge_ref, base_ref, small_ref, wh, wl, w32, nh, nl) = rest[count:count + 10]
    got = base + weights
    tokens = base[0].shape[0] - EXTRA
    part = q_ref.shape[1]
    rows = w32.shape[0] // len(pieces)
    small = None
    for r in range(splits):
        rest = got[r][tokens:, :]
        small = rest if small is None else small + rest
    small_ref[...] = small
    gain, shift = small[4:5], small[5:6]
    for r in range(splits):
        row = at(idx[0, r] * tokens, tokens, 16)
        x = got[r][:tokens, :]
        base_ref[row, :] = x
        xhat, _ = norm(x)
        nh[row, :], nl[row, :] = split(xhat * gain + shift)
    for i, (n, lead) in enumerate(pieces):
        w32[at(idx[0, splits + i] * rows, rows), :] = got[splits + n][lead, :rows, :]
    wh[...], wl[...] = split(w32[...])
    u = idx[0, 0]
    qb = pick(u, [small[0:1, i * part:(i + 1) * part] for i in range(splits)])
    vb = pick(u, [small[1:2, i * part:(i + 1) * part] for i in range(splits)])
    bias = jnp.concatenate([qb, jnp.zeros_like(qb), vb], axis=1)
    step = nh.shape[0] // 2

    def rows_of(i, _):
        row = at(i * step, step, 16)
        out = mm3((nh[row, :], nl[row, :]), (wh[...], wl[...])) + bias
        q_ref[row, :] = out[:, :part]
        kv_ref[row, :] = out[:, part:]
        return 0

    lax.fori_loop(0, 2, rows_of, 0)
    reach = edge_ref.shape[0]
    edge_ref[...] = kv_ref[at(idx[0, edge], reach), :]


def span_hits(seg, i, j):
    return (seg[0, 2 * j + 1] >= seg[0, 2 * i]) & (seg[0, 2 * j] <= seg[0, 2 * i + 1])


def prepare(src, width, first, count, size, pairs, flipped):
    heads = width // HEAD_DIM
    for scratch, start in pairs:
        for h in range(heads):
            hi, lo = split(src[:, start + h * HEAD_DIM:start + (h + 1) * HEAD_DIM])
            scratch[h] = jnp.concatenate([hi, lo, hi], axis=1)
    for j in range(count):
        turned = src[j * size:(j + 1) * size, first:first + width].T
        for h in range(heads):
            hi, lo = split(turned[h * HEAD_DIM:(h + 1) * HEAD_DIM])
            flipped[h, j] = jnp.concatenate([hi, lo], axis=0)


def columns(codes, out, size):
    for j in range(out.shape[0] // size):
        row = codes[:, j * size:(j + 1) * size]
        out[j * size:(j + 1) * size, :] = jnp.broadcast_to(row, (128, size)).T


def same_row(i, j):
    return (lax.broadcasted_iota(jnp.int32, (TILE, TILE), 0)
            - lax.broadcasted_iota(jnp.int32, (TILE, TILE), 1)) == (i - j) * TILE


def attend_add(heads, qc, keys, flipped, m_s, l_s, acc, i, j, size, allowed):
    qrow = at(i * TILE, TILE, TILE)
    krow = at(j * size, size, size)
    for h in range(heads):
        s = jnp.where(allowed, mm(keys[h, krow, :], qc[h, qrow, :], NT), FLOOR)
        m_old = m_s[h, i]
        m_new = jnp.maximum(m_old, jnp.max(s, axis=0, keepdims=True))
        p = jnp.where(allowed, jnp.exp(s - m_new), 0.0)
        factor = jnp.exp(m_old - m_new)
        m_s[h, i] = m_new
        l_s[h, i] = l_s[h, i] * factor + jnp.sum(p, axis=0, keepdims=True)
        hi, lo = split(p)
        v128 = flipped[h, j]
        acc[h, i] = acc[h, i] * factor + mm(v128, hi) + mm(v128, lo)


def attend_own_kernel(heads, seg_ref, qcode_ref, kcode_ref, q_ref, kv_ref, qc, m_s, l_s, acc, kc, vt, kcol):
    group, width = q_ref.shape
    nq = group // TILE
    for h in range(heads):
        hi, lo = split(q_ref[:, h * HEAD_DIM:(h + 1) * HEAD_DIM] * HEAD_DIM ** -0.5)
        qc[h] = jnp.concatenate([hi, hi, lo], axis=1)
    prepare(kv_ref, width, width, nq, TILE, [(kc, 0)], vt)
    columns(kcode_ref, kcol, TILE)
    m_s[...] = jnp.full_like(m_s, FLOOR)
    l_s[...] = jnp.zeros_like(l_s)
    acc[...] = jnp.zeros_like(acc)

    def per_q(i, _):
        def per_k(j, _):
            @pl.when(span_hits(seg_ref, i, j))
            def _():
                allowed = kcol[at(j * TILE, TILE, TILE), :1] == qcode_ref[:, at(i * TILE, TILE, TILE)]
                attend_add(heads, qc, kc, vt, m_s, l_s, acc, i, j, TILE, allowed | same_row(i, j))
            return 0

        lax.fori_loop(0, nq, per_k, 0)
        return 0

    lax.fori_loop(0, nq, per_q, 0)


def attend_edge_kernel(heads, seg_ref, qcode_ref, hcode_ref, halo_ref, qc, m_in, l_in, acc_in,
                       out_ref, wide_ref, lse_ref, kh, vh, hcol, m_s, l_s, acc):
    group, width = out_ref.shape
    nq, nh = group // TILE, halo_ref.shape[0] // EDGE
    m_s[...] = m_in[...]
    l_s[...] = l_in[...]
    acc[...] = acc_in[...]
    if nh:
        prepare(halo_ref, width, width, nh, EDGE, [(kh, 0)], vh)
        columns(hcode_ref, hcol, EDGE)

    def per_q(i, _):
        qrow = at(i * TILE, TILE, TILE)

        def per_edge(j, _):
            @pl.when(span_hits(seg_ref, i, nq + j))
            def _():
                allowed = hcol[at(j * EDGE, EDGE, EDGE), :1] == qcode_ref[:, qrow]
                attend_add(heads, qc, kh, vh, m_s, l_s, acc, i, j, EDGE, allowed)
            return 0

        if nh:
            lax.fori_loop(0, nh, per_edge, 0)
        parts = []
        for h in range(heads):
            total = l_s[h, i]
            parts.append((acc[h, i, :HEAD_DIM] + acc[h, i, HEAD_DIM:]) / total)
            lse_ref[h:h + 1, qrow] = m_s[h, i] + jnp.log(total)
        out_ref[qrow, :] = jnp.concatenate(parts, axis=0).T
        return 0

    lax.fori_loop(0, nq, per_q, 0)
    wide_ref[:, :width] = out_ref[:group // 2, :]
    wide_ref[:, width:] = out_ref[group // 2:, :]


def attend_own(segs, qcode, kcode, q, kv):
    group, width = q.shape
    heads, nq = width // HEAD_DIM, group // TILE
    return call(
        functools.partial(attend_own_kernel, heads), "attend_own",
        [arr((heads, group, 3 * HEAD_DIM), BF), arr((heads, nq, 1, TILE)), arr((heads, nq, 1, TILE)),
         arr((heads, nq, 2 * HEAD_DIM, TILE))],
        [segs, qcode, kcode, q, kv],
        [pltpu.VMEM((heads, group, 3 * HEAD_DIM), BF), pltpu.VMEM((heads, nq, 2 * HEAD_DIM, TILE), BF),
         pltpu.VMEM((group, 128), F32)],
        flops=4 * group * group * width)


def attend_edge(segs, qcode, hcode, halo, state):
    heads, group, _ = state[0].shape
    reach, width = halo.shape[0], halo.shape[1] // 2
    nq, nh = group // TILE, reach // EDGE
    return call(
        functools.partial(attend_edge_kernel, heads), "attend_edge",
        [arr((group, width)), arr((group // 2, 2 * width)), arr((8, group))],
        [segs, qcode, hcode, halo, *state],
        [pltpu.VMEM((heads, reach, 3 * HEAD_DIM), BF), pltpu.VMEM((heads, nh, 2 * HEAD_DIM, EDGE), BF),
         pltpu.VMEM((reach, 128), F32)]
        + [pltpu.VMEM(x.shape, x.dtype) for x in state[1:]],
        flops=2 * group * reach * width, wide=reach > group)


def back_add(heads, qc, q2, dc, d2, dot_s, lse_ref, keys, values, flipped, dqa, dka, dva, i, j, size, allowed):
    qrow = at(i * TILE, TILE, TILE)
    krow = at(j * size, size, size)
    for h in range(heads):
        s = mm(keys[h, krow, :], qc[h, qrow, :], NT)
        p = jnp.exp(jnp.where(allowed, s - lse_ref[h:h + 1, qrow], FLOOR))
        dp = mm(values[h, krow, :], dc[h, qrow, :], NT)
        ds = p * (dp - dot_s[h, :, qrow])
        hi, lo = split(p)
        d128 = d2[h, qrow, :]
        dva[h] += mm(hi, d128) + mm(lo, d128)
        hi, lo = split(ds)
        q128 = q2[h, qrow, :]
        dka[h] += mm(hi, q128) + mm(lo, q128)
        k128 = flipped[h, j]
        dqa[h, i] += mm(k128, hi) + mm(k128, lo)


def back_over(heads, seg_ref, nq, count, size, first, out, dka, dva, visit):
    width = heads * HEAD_DIM

    def folded(acc):
        return jnp.concatenate([acc[h, :, :HEAD_DIM] + acc[h, :, HEAD_DIM:] for h in range(heads)], axis=1)

    def per_k(j, _):
        dka[...] = jnp.zeros_like(dka)
        dva[...] = jnp.zeros_like(dva)

        def per_q(i, _):
            @pl.when(span_hits(seg_ref, i, first + j))
            def _():
                visit(i, j)
            return 0

        lax.fori_loop(0, nq, per_q, 0)
        krow = at(j * size, size, size)
        out[krow, :width] = folded(dka)
        out[krow, width:] = folded(dva)
        return 0

    lax.fori_loop(0, count, per_k, 0)


def back_edge_kernel(heads, splits, idx, seg_ref, qcode_ref, hcode_ref, q_ref, halo_ref, o_ref, lse_ref, qc,
                     oh_ref, ol_ref, *refs):
    mg, (dhalo_ref, q2, dc, d2, dot_s, dqa, gh, gl, kh, vh, kth, hcol, prod_s, dka, dva) = (
        refs[:splits], refs[splits:])
    group, width = q_ref.shape
    nq, nh = group // TILE, halo_ref.shape[0] // EDGE
    tokens = group // splits
    if nh:
        prepare(halo_ref, width, 0, nh, EDGE, [(kh, 0), (vh, width)], kth)
        columns(hcode_ref, hcol, EDGE)
    for h in range(heads):
        hi, lo = split(q_ref[:, h * HEAD_DIM:(h + 1) * HEAD_DIM] * HEAD_DIM ** -0.5)
        q2[h] = jnp.concatenate([hi, lo], axis=1)
    dqa[...] = jnp.zeros_like(dqa)
    wrow = at(idx[0, 0] * width, width, 16)
    w_pair = (oh_ref[wrow, :], ol_ref[wrow, :])
    for r in range(splits):
        row = at(idx[0, r] * tokens, tokens, 16)
        gh[row, :], gl[row, :] = split(mg[r][...])
    step = group // 2
    for i in range(2):
        row = slice(i * step, (i + 1) * step)
        grad = mm3((gh[row, :], gl[row, :]), w_pair, NT)
        prod_s[row, :] = grad * o_ref[row, :]
        for h in range(heads):
            hi, lo = split(grad[:, h * HEAD_DIM:(h + 1) * HEAD_DIM])
            dc[h, row, :] = jnp.concatenate([hi, hi, lo], axis=1)
            d2[h, row, :] = jnp.concatenate([hi, lo], axis=1)
    for i in range(nq):
        rows = slice(i * TILE, (i + 1) * TILE)
        prod = prod_s[rows, :].T
        for h in range(heads):
            dot_s[h, :, rows] = jnp.sum(prod[h * HEAD_DIM:(h + 1) * HEAD_DIM], axis=0, keepdims=True)

    def visit(i, j):
        allowed = hcol[at(j * EDGE, EDGE, EDGE), :1] == qcode_ref[:, at(i * TILE, TILE, TILE)]
        back_add(heads, qc, q2, dc, d2, dot_s, lse_ref, kh, vh, kth, dqa, dka, dva, i, j, EDGE, allowed)

    if nh:
        back_over(heads, seg_ref, nq, nh, EDGE, nq, dhalo_ref, dka, dva, visit)


def back_own_kernel(heads, seg_ref, qcode_ref, kcode_ref, kv_ref, lse_ref, qc, q2, dc, d2, dot_s, dq_in,
                    dq_ref, dkv_ref, kc, vc, kt, kcol, dqa, dka, dva):
    group, width = dq_ref.shape
    nq = group // TILE
    prepare(kv_ref, width, 0, nq, TILE, [(kc, 0), (vc, width)], kt)
    columns(kcode_ref, kcol, TILE)
    dqa[...] = dq_in[...]

    def visit(i, j):
        allowed = kcol[at(j * TILE, TILE, TILE), :1] == qcode_ref[:, at(i * TILE, TILE, TILE)]
        back_add(heads, qc, q2, dc, d2, dot_s, lse_ref, kc, vc, kt, dqa, dka, dva, i, j, TILE, allowed | same_row(i, j))

    back_over(heads, seg_ref, nq, nq, TILE, 0, dkv_ref, dka, dva, visit)
    for i in range(nq):
        parts = [(dqa[h, i, :HEAD_DIM] + dqa[h, i, HEAD_DIM:]) * HEAD_DIM ** -0.5 for h in range(heads)]
        dq_ref[i * TILE:(i + 1) * TILE, :] = jnp.concatenate(parts, axis=0).T


def attend_back_edge(idx, segs, qcode, hcode, q, halo, o, lse, qc, oh, ol, mg):
    group, width = q.shape
    reach = halo.shape[0]
    heads = width // HEAD_DIM
    nq, nh = group // TILE, reach // EDGE
    full = oh.shape[1]
    H3, H2 = 3 * HEAD_DIM, 2 * HEAD_DIM
    return call(
        functools.partial(back_edge_kernel, heads, len(mg)), "back_edge",
        [arr((reach, 2 * width)), arr((heads, group, H2), BF), arr((heads, group, H3), BF), arr((heads, group, H2), BF),
         arr((heads, 1, group)), arr((heads, nq, H2, TILE)), arr((group, full), BF), arr((group, full), BF)],
        [idx, segs, qcode, hcode, q, halo, o, lse, qc, oh, ol, *mg],
        [
            pltpu.VMEM((heads, reach, H3), BF),
            pltpu.VMEM((heads, reach, H3), BF),
            pltpu.VMEM((heads, nh, H2, EDGE), BF),
            pltpu.VMEM((reach, 128), F32),
            pltpu.VMEM((group, width), F32),
            pltpu.VMEM((heads, EDGE, H2), F32),
            pltpu.VMEM((heads, EDGE, H2), F32),
        ],
        flops=2 * group * full * width, smem=2, wide=reach > group)


def attend_back_own(segs, qcode, kcode, kv, lse, qc, q2, dc, d2, dot_s, dqa):
    heads, group, _ = qc.shape
    width = kv.shape[1] // 2
    nq = group // TILE
    H3, H2 = 3 * HEAD_DIM, 2 * HEAD_DIM
    return call(
        functools.partial(back_own_kernel, heads), "back_own",
        [arr((group, width)), arr((group, 2 * width))],
        [segs, qcode, kcode, kv, lse, qc, q2, dc, d2, dot_s, dqa],
        [
            pltpu.VMEM((heads, group, H3), BF),
            pltpu.VMEM((heads, group, H3), BF),
            pltpu.VMEM((heads, nq, H2, TILE), BF),
            pltpu.VMEM((group, 128), F32),
            pltpu.VMEM((heads, nq, H2, TILE), F32),
            pltpu.VMEM((heads, TILE, H2), F32),
            pltpu.VMEM((heads, TILE, H2), F32),
        ],
        flops=10 * group * group * width)


def weights_kernel(full, splits, idx, *refs):
    count = max([p[0] for p in full]) + 1
    weights, (uh, ul, oh, ol, u32, o32) = refs[:count], refs[count:count + 6]
    got = weights
    owners = len(full)
    rows = u32.shape[0] // owners
    for i, (n, lead) in enumerate(full):
        row = at(idx[0, splits + i] * rows, rows)
        u32[row, :] = got[n][lead]
        o32[row, :] = got[n][2]
    uh[...], ul[...] = split(u32[...])
    oh[...], ol[...] = split(o32[...])


def act_kernel(splits, whole, first, place, idx, *refs):
    got, (gh, gl, dh, dl, act_ref) = refs[:-5], refs[-5:]
    tokens = got[0].shape[0]
    down = got[splits:]
    unit = down[0].shape[0]
    blocks = dh.shape[0] // unit
    for r in range(splits):
        row = at(idx[0, r] * tokens, tokens, 16)
        gh[row, :], gl[row, :] = split(got[r][...])
    for i in range(blocks):
        if i < whole:
            row = at(idx[0, first + i] * unit, unit, 16)
            dh[row, :], dl[row, :] = split(down[i][...])
            continue
        size = unit // 4
        for z in range(4):
            quarter = idx[0, place] ^ (0, 3, 1, 2)[z]
            row = at(idx[0, first + i] * unit + quarter * size, size, 16)
            dh[row, :], dl[row, :] = split(down[whole + 4 * (i - whole) + z][...])
    step = gh.shape[0] // 2

    def rows_of(i, _):
        row = at(i * step, step, 16)
        act_ref[row, :] = mm3((gh[row, :], gl[row, :]), (dh[...], dl[...]), NT)
        return 0

    lax.fori_loop(0, 2, rows_of, 0)


def feed_kernel(splits, idx, small, base, *refs):
    (oh, ol, uh, ul, act, keep, send, mine, inv_ref, ah, al, ph, plo, mh, ml, vec, b32, x2, g32, r32) = (
        refs[splits:splits + 20])
    att = refs[:splits]
    tokens = keep.shape[1]
    group = b32.shape[0]
    part = att[0].shape[1] // 2
    gain, shift = small[6:7, :], small[7:8, :]
    up_bias = small[pl.ds(8 + idx[0, 0], 1), :]
    vec[...] = jnp.zeros_like(vec)
    step = group // 2

    def rows_of(i, _):
        row = at(i * step, step, 16)
        middle = base[row, :] + small[2:3, :]
        for s in range(splits):
            wrow = at(idx[0, s] * part, part, 16)
            piece = jnp.where(i == 0, att[s][:, :part], att[s][:, part:])
            middle = middle + mm3(split(piece), (oh[wrow, :], ol[wrow, :]))
        b32[row, :] = middle
        xhat, inverse = norm(middle)
        x2[row, :] = xhat
        g32[row, :] = jnp.broadcast_to(inverse, g32[row, :].shape)
        pair = split(xhat * gain + shift)
        mh[row, :], ml[row, :] = pair
        pre = mm3(pair, (uh[...], ul[...])) + up_bias
        square = pre * pre
        curve = jnp.tanh(SQRT_2_PI * (pre + CUBIC * square * pre))
        half = 0.5 * (1.0 + curve)
        ah[row, :], al[row, :] = split(pre * half)
        slope = half + 0.5 * pre * (1.0 - curve * curve) * SQRT_2_PI * (1.0 + 3.0 * CUBIC * square)
        grad = act[row, :] * slope
        pair = split(grad)
        ph[row, :], plo[row, :] = pair
        back = mm3(pair, (uh[...], ul[...]), NT)
        vec[0:1, :] += jnp.sum(grad, axis=0, keepdims=True)
        vec[1:2, :] += jnp.sum(back * xhat, axis=0, keepdims=True)
        vec[2:3, :] += jnp.sum(back, axis=0, keepdims=True)
        r32[row, :] = back
        return 0

    lax.fori_loop(0, 2, rows_of, 0)
    for r in range(splits):
        row = at(idx[0, r] * tokens, tokens)
        target = send if r % 2 else keep
        target[r // 2] = r32[row, :]
    row = at(idx[0, 0] * tokens, tokens)
    mine[0] = b32[row, :]
    mine[1] = x2[row, :]
    inv_ref[...] = g32[row, :]


def feed_grads_kernel(splits, first, down_rows, up_rows, idx, ah, al, ph, plo, mh, ml, gh, gl, dh, dl,
                      keep, send, *refs):
    outs, r32 = refs[:-1], refs[-1]
    downs, ups = outs[:len(outs) // 2], outs[len(outs) // 2:]
    tokens = keep.shape[1]
    step = r32.shape[0] // 2

    def left(a, b):
        def rows_of(i, _):
            lane = at(i * step, step, 128)
            r32[at(i * step, step), :] = mm3((a[0][:, lane], a[1][:, lane]), (b[0][...], b[1][...]), TN)
            return 0

        lax.fori_loop(0, 2, rows_of, 0)

    def deal(targets, rows, place):
        for target in targets:
            for c in range(target.shape[0]):
                target[c] = r32[at(idx[0, place + c], rows), :]
            place += target.shape[0]
        return place

    left((ah, al), (gh, gl))
    place = deal(downs, down_rows, first)
    left((mh, ml), (ph, plo))
    deal(ups, up_rows, place)

    def rows_of(i, _):
        row = at(i * step, step, 16)
        r32[row, :] = mm3((ah[row, :], al[row, :]), (dh[...], dl[...]))
        return 0

    lax.fori_loop(0, 2, rows_of, 0)
    for r in range(splits):
        target = send if r % 2 else keep
        target[r // 2] = r32[at(idx[0, r] * tokens, tokens), :]


def middle_kernel(small, keep, core, far, og, mine, inv, mg_ref, vec_ref):
    grad = keep[0] + core[0] + far[...]
    out = og[...] + norm_back(grad, small[6:7, :], mine[1], inv[:, :1])
    mg_ref[...] = out
    vec_ref[...] = jnp.zeros_like(vec_ref)
    vec_ref[0:1, :] = jnp.sum(out, axis=0, keepdims=True)
    vec_ref[1:2, :] = jnp.sum(og[...], axis=0, keepdims=True)


def last_grads_kernel(splits, first, edge, rows, idx, small, dq, dkv, back, base, att, vec1, vec2, gh, gl, wh, wl,
                      keep, send, *refs):
    tails, (qh, ql, xhat, r32, o32, s32, n32, vec) = refs[:-8], refs[-8:]
    part = dq.shape[1]
    width = xhat.shape[1]
    tokens = keep.shape[1]
    gain, shift = small[4:5, :], small[5:6, :]
    u = idx[0, 0]
    s32[:, :part] = dq[...]
    s32[:, part:] = dkv[...]
    s32[at(idx[0, edge], back.shape[0]), part:] += back[...]
    qkv = s32[...]
    qh[...], ql[...] = split(qkv)
    sums = jnp.sum(qkv, axis=0, keepdims=True)
    xhat[...], _ = norm(base[...])
    vec[...] = jnp.zeros_like(vec)
    step = n32.shape[0] // 2

    def rows_of(i, _):
        row = at(i * step, step, 16)
        grad = mm3((qh[row, :], ql[row, :]), (wh[...], wl[...]), NT)
        n32[row, :] = grad
        vec[4:5, :] += jnp.sum(grad * xhat[row, :], axis=0, keepdims=True)
        vec[5:6, :] += jnp.sum(grad, axis=0, keepdims=True)
        return 0

    lax.fori_loop(0, 2, rows_of, 0)
    for r in range(splits):
        target = send if r % 2 else keep
        target[r // 2] = n32[at(idx[0, r] * tokens, tokens), :]
    step = width // 2
    for i in range(2):
        lane = slice(i * step, (i + 1) * step)
        pair = split(xhat[:, lane] * gain[:, lane] + shift[:, lane])
        r32[lane, :] = mm3(pair, (qh[...], ql[...]), TN)
    o32[...] = mm3(split(att[...]), (gh[...], gl[...]), TN)
    for i in range(splits):

        @pl.when(u == i)
        def _():
            vec[0:1, i * part:(i + 1) * part] = sums[:, :part]
            vec[1:2, i * part:(i + 1) * part] = sums[:, 2 * part:]

    vec[2:4, :] = vec2[0:2, :]
    vec[6:8, :] = vec1[1:3, :]
    vec[pl.ds(8 + u, 1), :] = vec1[0:1, :]
    wide = r32.shape[1]
    outs = width // 128
    vecs = outs * EXTRA // rows
    lane_blocks = -(-wide // 128)
    spare = lane_blocks * 128 - wide
    near = 2 * lane_blocks
    total = sum(t.shape[0] for t in tails)
    spot = 0
    for t in tails:
        for c in range(t.shape[0]):
            for j in range(splits):
                row = at(idx[0, first + spot * splits + j], rows)
                start = j * lane_blocks + (outs + vecs if j >= 2 else 0)
                for k in range(lane_blocks - 1):
                    t[c, start + k] = r32[row, k * 128:(k + 1) * 128]
                k = lane_blocks - 1
                t[c, start + k, :, :128 - spare] = r32[row, k * 128:]
                t[c, start + k, :, 128 - spare:] = jnp.zeros((rows, spare), F32)
            row = at(idx[0, first + total * splits + spot], rows)
            for k in range(outs):
                t[c, near + k] = o32[row, k * 128:(k + 1) * 128]
            for k in range(outs * EXTRA // 8):
                block, low = divmod(8 * k, rows)
                lane, high = divmod(8 * k, EXTRA)
                t[c, near + outs + block, low:low + 8, :] = vec[high:high + 8, lane * 128:(lane + 1) * 128]
            spot += 1


def hidden_kernel(idx, small, base, keep, core, far, mg, out):
    tokens = mg.shape[0]
    xhat, inverse = norm(base[at(idx[0, 0] * tokens, tokens), :])
    out[...] = mg[...] + norm_back(keep[0] + core[0] + far[...], small[4:5, :], xhat, inverse)


def place_kernel(splits, first, rows, idx, *refs):
    pieces, (gq, gk, gv, go) = refs[:-4], refs[-4:]
    part = gq.shape[1] // splits
    for z, piece in enumerate(pieces):
        row = at(idx[0, first + z] * rows, rows)
        count = gq.shape[1] // 128
        for k in range(count):
            go[row, k * 128:(k + 1) * 128] = piece[5 * splits + k]
        for r in range(splits):
            whole = jnp.concatenate([piece[5 * r + k] for k in range(5)], axis=1)
            for i in range(splits):

                @pl.when(idx[0, r] == i)
                def _():
                    for n, out in enumerate((gq, gk, gv)):
                        out[row, i * part:(i + 1) * part] = whole[:, n * part:(n + 1) * part]


def place_feed_kernel(splits, blocks, unit, first, idx, *refs):
    pieces, (gd, gu) = refs[:-2], refs[-2:]
    downs, ups = pieces[:len(pieces) // 2], pieces[len(pieces) // 2:]
    for z, (down, up) in enumerate(zip(downs, ups)):
        gd[at(idx[0, first + z] * down.shape[0], down.shape[0]), :] = down[...]
        rows = up.shape[1]
        row = at(idx[0, first + z] * rows, rows)
        for r in range(splits):
            for i in range(splits):

                @pl.when(idx[0, r] == i)
                def _():
                    for n in range(blocks):
                        start = (n * splits + i) * unit
                        gu[row, start:start + unit] = up[r, :, n * unit:(n + 1) * unit]


def swap(value, axis, mask):
    count = lax.axis_size(axis)
    return lax.ppermute(value, axis, [(i, i ^ mask) for i in range(count)])


def across(value):
    return swap(value, "ulys", 2)


def beside(value):
    return swap(value, "ulys", 1)


def over(value):
    return swap(value, "blk", 1)


def gather_splits(value):
    far = across(value)
    return [value, beside(value), far, beside(far)]


def after(value, *marks):
    return lax.optimization_barrier((value,) + marks)[0]


def corner(value):
    return lax.slice(value, (0,) * value.ndim, (1,) * (value.ndim - 2) + (8, 128))


def collect(value):
    near = swap(value, "dp", 3)
    return [value, near, swap(value, "dp", 1), swap(near, "dp", 1)]


def halo_moves(group, reach, blocks):
    moves = []
    shift = 1
    while reach > 0 and shift < blocks:
        rows = min(group, reach)
        moves.append((rows, True, [(i, i - shift) for i in range(shift, blocks)]))
        moves.append((rows, False, [(i, i + shift) for i in range(blocks - shift)]))
        reach -= rows
        shift += 1
    return moves


def halo_get(value, reach, axis=0):
    blocks, group = lax.axis_size("blk"), value.shape[axis]
    parts = []
    for rows, right, moves in halo_moves(group, reach, blocks):
        start = 0 if right else group - rows
        parts.append(lax.ppermute(lax.slice_in_dim(value, start, start + rows, axis=axis), "blk", moves))
    return jnp.concatenate(parts, axis=axis)


def halo_add(value, halo, reach):
    blocks, group = lax.axis_size("blk"), value.shape[0]
    start = 0
    for rows, right, moves in halo_moves(group, reach, blocks):
        back = lax.ppermute(halo[start:start + rows], "blk", [(j, i) for i, j in moves])
        start += rows
        room = group - rows
        value = value + jnp.pad(back, ((0, room), (0, 0)) if right else ((room, 0), (0, 0)))
    return value


def local(
    hidden,
    time_embed,
    segment_ids,
    key_valid,
    out_grad,
    w_query,
    b_query,
    w_key,
    w_value,
    b_value,
    w_out,
    b_out,
    w_up,
    b_up,
    w_down,
    b_down,
    pre_gain,
    pre_shift,
    mlp_gain,
    mlp_shift,
):
    blocks, splits = lax.axis_size("blk"), lax.axis_size("ulys")
    b, u, d = (lax.axis_index(name) for name in ("blk", "ulys", "dp"))
    both = ("blk", "ulys")
    owners = blocks * splits
    tokens, width = hidden.shape
    group = tokens * splits
    part = width // splits
    rows = w_query.shape[0]
    unit = w_down.shape[0]
    units = unit * owners
    share = units // splits
    reach = group * blocks // 4
    fast = blocks == 2 and splits == 4 and lax.axis_size("dp") == 4 and reach <= group and group == width

    if fast:
        f1, f3 = (d ^ (d >> 1)) & 1, d >> 1
        quarters = [2 * (f1 ^ s) + (f3 ^ t) for s in range(2) for t in range(2)]
        owner_list = [(b ^ x) * splits + (u ^ r) for x in range(2) for r in range(4)]
        block_list = [b, b ^ 1]
        edge_row = jnp.where(b == 0, group - reach, 0)
        down_rows, up_rows, tail_rows = unit // 4, rows // 4, rows // 4
        down_table = [(b ^ x) * unit + q * down_rows for x in range(2) for q in quarters]
        up_table = [
            ((b ^ x) * splits + (u ^ r)) * rows + q * up_rows for q in quarters for x in range(2) for r in range(4)
        ]
        tail_table = [
            ((b ^ x) * splits + (u ^ r)) * rows + q * tail_rows for x in range(2) for q in quarters for r in range(4)
        ] + [(b ^ x) * rows + q * tail_rows for x in range(2) for q in quarters]
        chunks = 8
    else:
        quarters = []
        owner_list = list(range(owners))
        block_list = list(range(blocks))
        edge_row = 0
        down_rows, up_rows, tail_rows = unit, rows, rows
        down_table = [i * unit for i in range(blocks)]
        up_table = [i * rows for i in range(owners)]
        tail_table = up_table + [i * rows for i in range(blocks)]
        chunks = blocks
    entries, spots = [], []
    for values in (
        [u ^ r for r in range(splits)], owner_list, block_list, [d], [edge_row], down_table + up_table, tail_table,
        quarters,
    ):
        spots.append(len(entries))
        entries += values
    _, _, at_block, at_d, at_edge, at_feed, at_tail, at_quarter = spots
    idx = jnp.stack([jnp.asarray(v, jnp.int32) for v in entries]).reshape(1, -1)

    segments = segment_ids[0] + 1
    codes = jnp.stack([segments, jnp.where(key_valid[0] == 1, segments, 0)]).astype(F32)
    small = jnp.stack([b_query, b_value, b_out, b_down, pre_gain, pre_shift, mlp_gain, mlp_shift])
    small = lax.dynamic_update_slice(jnp.zeros((EXTRA, width), F32), small, (0, (b * splits + u) * rows))
    small = lax.dynamic_update_slice(small, b_up[None], (8 + u, b * unit))
    if fast:
        small = lax.dynamic_update_slice(small, codes, (12, 0))
        other = over(small)
        small = small + other
        halo_codes = jnp.where(b == 0, other[12:14, :reach], other[12:14, group - reach:group])
    else:
        small = lax.psum(small, "blk")
        halo_codes = halo_get(codes, reach, axis=1)
    tiles = codes[0].reshape(-1, TILE)
    edges = halo_codes[0].reshape(-1, EDGE)
    bounds = jnp.concatenate(
        [
            jnp.stack([tiles[:, 0], tiles[:, -1]], axis=1).reshape(-1),
            jnp.stack([jnp.min(jnp.where(edges == 0, 1e6, edges), axis=1), jnp.max(edges, axis=1)], axis=1).reshape(-1),
        ]
    ).astype(jnp.int32).reshape(1, -1)
    query_codes, key_codes, edge_codes = codes[:1], codes[1:], halo_codes[1:]
    idx, bounds, query_codes, key_codes, edge_codes, small = lax.optimization_barrier(
        (idx, bounds, query_codes, key_codes, edge_codes, small)
    )
    base = jnp.concatenate([hidden + time_embed, small], axis=0)

    if fast:
        near, far, near2, far2 = call(
            functools.partial(pack_kernel, blocks), "pack",
            [arr((2, rows, 3 * part))] * 2 + [arr((3, rows, share))] * 2,
            [idx, w_query, w_key, w_value, w_up, w_out])
        pieces = [(i, i % 2) for i in range(8)]
        far = across(far)
        far_base = across(after(base, corner(far)))
        qkv_arrays = [near, beside(near), far, beside(far)]
        near = over(near)
        far = over(far)
        qkv_arrays += [near, beside(near), far, beside(far)]
        base_all = [base, beside(base), far_base, beside(far_base)]

        far2 = across(after(far2, corner(far_base)))
        feed_arrays = [near2, beside(near2), far2, beside(far2)]
        near2 = over(after(near2, corner(far)))
        feed_arrays += [near2, beside(near2)]
        whole = 1
        down_quarter = lax.dynamic_slice_in_dim(w_down, d * (unit // 4), unit // 4, 0)
        down_quarter = over(after(down_quarter, corner(far)))
    else:
        cut = jnp.stack([w_query, w_key, w_value], axis=1).reshape(rows, 3, splits, part)
        cut = cut.transpose(2, 0, 1, 3).reshape(splits, rows, 3 * part)
        cut = jnp.broadcast_to(cut[None], (blocks,) + cut.shape).reshape(owners, rows, 3 * part)
        got = lax.all_to_all(cut, both, 0, 0, tiled=True)
        qkv_arrays = [got[i:i + 1] for i in range(owners)]
        cut = w_up.reshape(rows, blocks, splits, unit).transpose(2, 0, 1, 3).reshape(splits, rows, share)
        cut = jnp.broadcast_to(cut[None], (blocks,) + cut.shape).reshape(owners, rows, share)
        got = lax.all_to_all(cut, both, 0, 0, tiled=True)
        outs = lax.all_gather(w_out, both, axis=0, tiled=False)
        feed_arrays = [jnp.stack([got[i], got[i], outs[i]]) for i in range(owners)]
        pieces = [(i, 0) for i in range(owners)]
        whole = blocks
        base_all = gather_splits(base)
        gathered = lax.all_gather(w_down, "blk", axis=0, tiled=False)
        down = [gathered[i] for i in range(blocks)]

    query, key_value, edge_kv, base, small, qkv_hi, qkv_lo = call(
        functools.partial(qkv_kernel, pieces, splits, at_edge), "qkv",
        [arr((group, part)), arr((group, 2 * part)), arr((reach if fast else 8, 2 * part)), arr((group, width)),
         arr((EXTRA, width)), arr((width, 3 * part), BF), arr((width, 3 * part), BF)],
        [idx, *base_all, *qkv_arrays],
        [pltpu.VMEM((width, 3 * part), F32), pltpu.VMEM((group, width), BF), pltpu.VMEM((group, width), BF)],
        flops=2 * group * width * 3 * part)
    halo = over(edge_kv) if fast else halo_get(key_value, reach)
    state = attend_own(bounds, query_codes, key_codes, query, key_value)
    attended, attended_wide, lse = attend_edge(bounds, query_codes, edge_codes, halo, state)

    grads = gather_splits(after(out_grad, corner(edge_kv)))
    if fast:
        down = [w_down] + collect(after(down_quarter, corner(state[3])))
        far2 = over(after(far2, corner(halo)))
    og_hi, og_lo, down_hi, down_lo, act_grad = call(
        functools.partial(act_kernel, splits, whole, at_block, at_d), "act",
        [arr((group, width), BF)] * 2 + [arr((share, width), BF)] * 2 + [arr((group, share))],
        [idx, *grads, *down],
        flops=2 * group * width * share)
    if fast:
        far2 = after(far2, corner(act_grad))
        feed_arrays += [far2, beside(far2)]
    up_hi, up_lo, out_hi, out_lo = call(
        functools.partial(weights_kernel, pieces, splits), "weights",
        [arr((width, share), BF)] * 2 + [arr((width, width), BF)] * 2,
        [idx, *feed_arrays],
        [pltpu.VMEM((width, share), F32), pltpu.VMEM((width, width), F32)])

    attended_all = gather_splits(attended_wide)
    pair = [arr((group, share), BF)] * 2
    keep, send, mine, inverse2, act_hi, act_lo, pre_hi, pre_lo, in_hi, in_lo, vec_feed = call(
        functools.partial(feed_kernel, splits), "feed",
        [arr((2, tokens, width))] * 2 + [arr((2, tokens, width)), arr((tokens, 128))] + pair * 2
        + [arr((group, width), BF)] * 2 + [arr((8, width))],
        [idx, small, base, *attended_all, out_hi, out_lo, up_hi, up_lo, act_grad],
        [pltpu.VMEM((group, width), F32), pltpu.VMEM((group, width), F32), pltpu.VMEM((group, 128), F32),
         pltpu.VMEM((group, width), F32)],
        flops=2 * group * width * (width + 2 * share))
    core = beside(send)
    near_sum = keep[1] + core[1]
    far_sum = across(near_sum)

    if fast:
        feed_outs = [arr((4, down_rows, width))] * 2 + [arr((8 * splits // 2, up_rows, share))] * 2
    else:
        feed_outs = [arr((blocks, down_rows, width)), arr((owners, up_rows, share))]
    keep_out, send_out, *feed_grads = call(
        functools.partial(feed_grads_kernel, splits, at_feed, down_rows, up_rows), "feed_grads",
        [arr((2, tokens, width))] * 2 + feed_outs,
        [idx, after(act_hi, corner(near_sum)), act_lo, pre_hi, pre_lo, in_hi, in_lo, og_hi, og_lo, down_hi, down_lo],
        [pltpu.VMEM((group, width), F32)],
        flops=6 * group * width * share)
    if fast:
        down_keep, down_send, up_keep, up_send = feed_grads
        down_got = over(down_send)
        up_got = swap(up_send, "dp", 1)

    middle_grad, vec_middle = call(
        middle_kernel, "middle",
        [arr((tokens, width)), arr((8, width))],
        [small, keep, core, after(far_sum, corner(keep_out)), out_grad, mine, inverse2], smem=0)
    middle_all = gather_splits(middle_grad)

    halo_grad, q2, dc, d2, dots, dq_part, mg_hi, mg_lo = attend_back_edge(
        idx, bounds, query_codes, edge_codes, query, halo, attended, lse, state[0], out_hi, out_lo, middle_all)
    query_grad, kv_grad = attend_back_own(
        bounds, query_codes, key_codes, key_value, lse, state[0], q2, dc, d2, dots, dq_part)
    if fast:
        returned = over(halo_grad)
        mark = corner(halo_grad)
        part_down = down_keep + after(down_got, mark)
        part_up = up_keep.reshape(2, 2, splits, up_rows, share) + after(up_got, mark).reshape(
            2, 2, splits, up_rows, share)
        down_got = swap(part_down[2:], "dp", 1)
        up_got = swap(part_up[1], "dp", 3)
    else:
        kv_grad = halo_add(kv_grad, halo_grad, reach)
        returned = jnp.zeros((8, 2 * part), F32)

    lane_blocks = -(-3 * part // 128)
    outs, vecs = width // 128, width // 128 * EXTRA // tail_rows
    total_blocks = splits * lane_blocks + outs + vecs
    tail_outs = [arr((4, total_blocks, tail_rows, 128))] * 2 if fast else [arr((blocks, total_blocks, tail_rows, 128))]
    keep_in, send_in, *tail = call(
        functools.partial(last_grads_kernel, splits, at_tail, at_edge, tail_rows), "last_grads",
        [arr((2, tokens, width))] * 2 + tail_outs,
        [idx, small, query_grad, kv_grad, returned, base, attended, vec_feed, vec_middle, mg_hi, mg_lo, qkv_hi, qkv_lo],
        [pltpu.VMEM((group, 3 * part), BF), pltpu.VMEM((group, 3 * part), BF), pltpu.VMEM((group, width), F32),
         pltpu.VMEM((width, 3 * part), F32), pltpu.VMEM((part, width), F32), pltpu.VMEM((group, 3 * part), F32),
         pltpu.VMEM((group, width), F32), pltpu.VMEM((EXTRA, width), F32)],
        flops=2 * group * width * 7 * part)
    to_owner = [(i * splits + j, j * blocks + i) for i in range(blocks) for j in range(splits)]
    near = 2 * lane_blocks
    if fast:
        tail_got = over(tail[1])
        core_in = beside(send_in)
        far_in = across(keep_in[1] + core_in[1])

        mark = corner(keep_in)
        part_down = part_down[:2] + after(down_got, mark)
        part_up = part_up[0] + after(up_got, mark)
        down_got = swap(part_down[1], "dp", 3)
        up_got = over(part_up[1])
        part_down = part_down[0] + down_got
        part_up = part_up[0] + up_got

        part_tail = tail[0] + tail_got
        mark = corner(part_tail)
        part_tail = part_tail[:2] + swap(part_tail[2:], "dp", 1)
        far_up = across(after(part_up[2:], mark))
        core_up = beside(jnp.stack([part_up[1], far_up[1]]))
        part_tail = part_tail[0] + swap(part_tail[1], "dp", 3)
        part_up = jnp.stack([part_up[0], core_up[0], far_up[0], core_up[1]])

        all_down = collect(after(part_down, mark))
        far_tail = across(part_tail[near + outs:])
        core_tail = beside(
            jnp.concatenate([
                part_tail[lane_blocks:near], part_tail[near + outs:near + outs + vecs] + far_tail[:vecs],
                far_tail[vecs + lane_blocks:]])
        )
        vec = part_tail[near + outs:near + outs + vecs] + far_tail[:vecs] + core_tail[lane_blocks:lane_blocks + vecs]
        owned = lax.ppermute(part_tail[near:near + outs], both, to_owner)
        part_tail = jnp.concatenate([
            part_tail[:lane_blocks], core_tail[:lane_blocks], far_tail[vecs:vecs + lane_blocks],
            core_tail[lane_blocks + vecs:], owned])
        all_tail = collect(part_tail)
        all_up = collect(part_up)
        total_down, total_up = call(
            functools.partial(place_feed_kernel, splits, blocks, unit, at_quarter), "place_feed",
            [arr((unit, width)), arr((rows, units))],
            [idx, *all_down, *all_up])
        total_query, total_key, total_value, total_out = call(
            functools.partial(place_kernel, splits, at_quarter, tail_rows), "place",
            [arr((rows, width))] * 4,
            [idx, *all_tail])
    else:
        core_in = beside(send_in)
        far_in = across(keep_in[1] + core_in[1])
        total_down, total_up, tail = [
            lax.psum(lax.psum_scatter(g.reshape((blocks, -1) + g.shape[1:]), "blk", scatter_dimension=0, tiled=False), "dp")
            for g in (*feed_grads, *tail)
        ]
        total_down = total_down.reshape(unit, width)
        total_up = lax.all_to_all(total_up, "ulys", 0, 0, tiled=True)
        total_up = total_up.reshape(splits, rows, blocks, unit).transpose(1, 2, 0, 3).reshape(rows, units)
        tail = tail[0]
        total_out = lax.ppermute(tail[near:near + outs], both, to_owner).transpose(1, 0, 2).reshape(rows, width)
        vec = lax.psum(tail[near + outs:near + outs + vecs], "ulys")
        got = jnp.concatenate([tail[:near], tail[near + outs + vecs:]]).reshape(splits, lane_blocks, rows, 128)
        got = lax.all_to_all(got, "ulys", 0, 0, tiled=True).transpose(2, 0, 1, 3).reshape(rows, splits, lane_blocks * 128)
        total_query, total_key, total_value = (
            got[:, :, i * part:(i + 1) * part].reshape(rows, width) for i in range(3)
        )
    (hidden_grad,) = call(
        hidden_kernel, "hidden",
        [arr((tokens, width))],
        [idx, small, base, keep_in, core_in, far_in, middle_grad])

    core_out = beside(after(send_out, corner(keep_in)))
    far_out = across(keep_out[1] + core_out[1])
    output = mine[0] + small[3:4] + keep_out[0] + core_out[0] + far_out

    vec = vec.reshape(outs, EXTRA, 128).transpose(1, 0, 2).reshape(EXTRA, width)
    vector = lax.dynamic_slice(vec, (0, (b * splits + u) * rows), (8, rows))
    up_vector = lax.dynamic_slice(vec, (8 + u, b * unit), (1, unit))[0]
    return (
        output,
        hidden_grad,
        total_query,
        vector[0],
        total_key,
        total_value,
        vector[1],
        total_out,
        vector[2],
        total_up,
        up_vector,
        total_down,
        vector[3],
        vector[4],
        vector[5],
        vector[6],
        vector[7],
    )


def solution(mesh):
    tokens = P(("dp", "blk", "ulys"), None)
    matrix = P(("blk", "ulys"), None)
    vector = P(("blk", "ulys"))
    return jax.shard_map(
        local,
        mesh=mesh,
        in_specs=(
            tokens,
            P("dp", None),
            P("dp", "blk"),
            P("dp", "blk"),
            tokens,
            matrix,
            vector,
            matrix,
            matrix,
            vector,
            matrix,
            vector,
            matrix,
            vector,
            matrix,
            vector,
            vector,
            vector,
            vector,
            vector,
        ),
        out_specs=(
            tokens,
            tokens,
            matrix,
            vector,
            matrix,
            matrix,
            vector,
            matrix,
            vector,
            matrix,
            vector,
            matrix,
            vector,
            vector,
            vector,
            vector,
            vector,
        ),
        check_vma=False,
    )
```

```python
import functools
import math

import jax
import jax.numpy as jnp
from jax import lax
from jax.experimental import pallas as pl
from jax.experimental.pallas import tpu as pltpu
from jax.sharding import PartitionSpec as P

HEAD_DIM = 64
FLOOR = -1e30
SQRT_2_PI = 0.7978845608028654
CUBIC = 0.044715
EXTRA = 16
TILE = 256
EDGE = 128
BF = jnp.bfloat16
F32 = jnp.float32
NN = (((1,), (0,)), ((), ()))
NT = (((1,), (1,)), ((), ()))
TN = (((0,), (0,)), ((), ()))
VM = pl.BlockSpec(memory_space=pltpu.VMEM)
SM = pl.BlockSpec(memory_space=pltpu.SMEM)
LIMITS = {"attend_own": 10, "attend_edge": 10, "back_edge": 12, "back_own": 12, "act": 14, "weights": 16, "feed_grads": 12, "place": 8, "hidden": 6, "middle": 6, "last_grads": 16, "fold": 10, "base": 6, "pack_qkv": 8, "pack_feed": 10}


def split(x):
    hi = x.astype(BF)
    return hi, (x - hi.astype(F32)).astype(BF)


def mm(a, b, dims=NN):
    return lax.dot_general(a, b, dims, preferred_element_type=F32)


def mm3(a, b, dims=NN):
    return mm(a[0], b[0], dims) + (mm(a[0], b[1], dims) + mm(a[1], b[0], dims))


def at(start, size, step=8):
    return pl.ds(pl.multiple_of(start, step), size)


def call(kernel, name, outs, ins, scratch=(), flops=0, smem=1, limit=16, wide=False, marks=()):
    inner, count, ins = kernel, len(ins), list(ins) + list(marks)

    def kernel(*refs):
        return inner(*refs[:count], *refs[len(ins):])

    size = sum(math.prod(x.shape) * x.dtype.itemsize for x in list(outs) + list(ins[smem:count]))
    return pl.pallas_call(
        kernel,
        out_shape=tuple(outs),
        in_specs=[SM] * smem + [VM] * (count - smem) + [pl.BlockSpec(memory_space=pl.ANY)] * len(marks),
        out_specs=tuple(SM if x.dtype == jnp.int32 else VM for x in outs),
        scratch_shapes=list(scratch),
        compiler_params=pltpu.CompilerParams(vmem_limit_bytes=(48 if wide else LIMITS.get(name, limit)) << 20),
        cost_estimate=pl.CostEstimate(flops=1, bytes_accessed=1, transcendentals=0),
        name=name,
    )(*ins)


def arr(shape, dtype=F32):
    return jax.ShapeDtypeStruct(tuple(shape), dtype)


def norm(x):
    centred = x - jnp.mean(x, axis=-1, keepdims=True)
    inverse = lax.rsqrt(jnp.mean(centred * centred, axis=-1, keepdims=True) + 1e-05)
    return centred * inverse, inverse


def norm_back(grad, gain, xhat, inverse):
    scaled = grad * gain
    mean = jnp.mean(scaled, axis=-1, keepdims=True)
    lean = jnp.mean(scaled * xhat, axis=-1, keepdims=True)
    return (scaled - mean - xhat * lean) * inverse


def pick(index, choices):
    value = choices[0]
    for i in range(1, len(choices)):
        value = jnp.where(index == i, choices[i], value)
    return value


def first_kernel(count, numbers, *refs):
    for source, target in zip((numbers,) + refs[:count], refs[count:]):
        if target.dtype == jnp.int32:
            for i in range(target.shape[1]):
                target[0, i] = source[0, i]
        else:
            target[...] = source[...]


def pack_qkv_kernel(idx, bounds, codes, halo_codes, small, wq, wk, wv, near, far, *outs):
    first_kernel(4, idx, bounds, codes, halo_codes, small, *outs)
    part = near.shape[2] // 3
    splits = wq.shape[1] // part
    for r in range(splits):
        target, k = (near, r) if r < 2 else (far, r - 2)
        for u in range(splits):

            @pl.when(idx[0, r] == u)
            def _():
                for i, w in enumerate((wq, wk, wv)):
                    target[k, :, i * part:(i + 1) * part] = w[:, u * part:(u + 1) * part]


def pack_feed_kernel(splits, blocks, idx, wup, wout, near, far):
    unit = near.shape[2] // blocks
    for r in range(splits):
        target, k = (near, r) if r < 2 else (far, r - 2)
        for u in range(splits):

            @pl.when(idx[0, r] == u)
            def _():
                for b in range(blocks):
                    lane = (b * splits + u) * unit
                    target[k, :, b * unit:(b + 1) * unit] = wup[:, lane:lane + unit]
    near[2] = wout[...]
    far[2] = wout[...]


def base_kernel(place, idx, hidden, embed, small, wdown, out, quarter):
    tokens, size = hidden.shape[0], quarter.shape[0]
    quarter[...] = wdown[at(idx[0, place] * size, size), :]
    out[:tokens, :] = hidden[...] + embed[...]
    out[tokens:, :] = small[...]


def qkv_kernel(pieces, splits, edge, idx, og, *refs):
    base, rest = refs[:splits], refs[splits:]
    count = max(p[0] for p in pieces) + 1
    weights = rest[:count]
    (q_ref, kv_ref, edge_ref, base_ref, small_ref, wh, wl, og_ref, w32, nh, nl) = rest[count:count + 11]
    got = base + weights
    tokens = base[0].shape[0] - EXTRA
    part = q_ref.shape[1]
    rows = w32.shape[0] // len(pieces)
    small = None
    for r in range(splits):
        rest = got[r][tokens:, :]
        small = rest if small is None else small + rest
    small_ref[...] = small
    gain, shift = small[4:5], small[5:6]
    for r in range(splits):
        row = at(idx[0, r] * tokens, tokens, 16)
        x = got[r][:tokens, :]
        base_ref[row, :] = x
        xhat, _ = norm(x)
        nh[row, :], nl[row, :] = split(xhat * gain + shift)
    for i, (n, lead) in enumerate(pieces):
        w32[at(idx[0, splits + i] * rows, rows), :] = got[splits + n][lead, :rows, :]
    wh[...], wl[...] = split(w32[...])
    u = idx[0, 0]
    qb = pick(u, [small[0:1, i * part:(i + 1) * part] for i in range(splits)])
    vb = pick(u, [small[1:2, i * part:(i + 1) * part] for i in range(splits)])
    bias = jnp.concatenate([qb, jnp.zeros_like(qb), vb], axis=1)
    step = nh.shape[0] // 2

    def rows_of(i, _):
        row = at(i * step, step, 16)
        out = mm3((nh[row, :], nl[row, :]), (wh[...], wl[...])) + bias
        q_ref[row, :] = out[:, :part]
        kv_ref[row, :] = out[:, part:]
        return 0

    lax.fori_loop(0, 2, rows_of, 0)
    reach = edge_ref.shape[0]
    edge_ref[...] = kv_ref[at(idx[0, edge], reach), :]
    og_ref[...] = og[...]


def span_hits(seg, i, j):
    return (seg[0, 2 * j + 1] >= seg[0, 2 * i]) & (seg[0, 2 * j] <= seg[0, 2 * i + 1])


def prepare(src, width, first, count, size, pairs, flipped):
    heads = width // HEAD_DIM
    for scratch, start in pairs:
        for h in range(heads):
            hi, lo = split(src[:, start + h * HEAD_DIM:start + (h + 1) * HEAD_DIM])
            scratch[h] = jnp.concatenate([hi, lo, hi], axis=1)
    for j in range(count):
        turned = src[j * size:(j + 1) * size, first:first + width].T
        for h in range(heads):
            hi, lo = split(turned[h * HEAD_DIM:(h + 1) * HEAD_DIM])
            flipped[h, j] = jnp.concatenate([hi, lo], axis=0)


def columns(codes, out, size):
    for j in range(out.shape[0] // size):
        row = codes[1:2, j * size:(j + 1) * size]
        out[j * size:(j + 1) * size, :] = jnp.broadcast_to(row, (128, size)).T


def same_row(i, j):
    return (lax.broadcasted_iota(jnp.int32, (TILE, TILE), 0)
            - lax.broadcasted_iota(jnp.int32, (TILE, TILE), 1)) == (i - j) * TILE


def attend_add(heads, qc, keys, flipped, m_s, l_s, acc, i, j, size, allowed):
    qrow = at(i * TILE, TILE, TILE)
    krow = at(j * size, size, size)
    for h in range(heads):
        s = jnp.where(allowed, mm(keys[h, krow, :], qc[h, qrow, :], NT), FLOOR)
        m_old = m_s[h, i]
        m_new = jnp.maximum(m_old, jnp.max(s, axis=0, keepdims=True))
        p = jnp.where(allowed, jnp.exp(s - m_new), 0.0)
        factor = jnp.exp(m_old - m_new)
        m_s[h, i] = m_new
        l_s[h, i] = l_s[h, i] * factor + jnp.sum(p, axis=0, keepdims=True)
        hi, lo = split(p)
        v128 = flipped[h, j]
        acc[h, i] = acc[h, i] * factor + mm(v128, hi) + mm(v128, lo)


def attend_own_kernel(heads, seg_ref, qcode_ref, kcode_ref, q_ref, kv_ref, qc, m_s, l_s, acc, kc, vt, kcol):
    group, width = q_ref.shape
    nq = group // TILE
    for h in range(heads):
        hi, lo = split(q_ref[:, h * HEAD_DIM:(h + 1) * HEAD_DIM] * HEAD_DIM ** -0.5)
        qc[h] = jnp.concatenate([hi, hi, lo], axis=1)
    prepare(kv_ref, width, width, nq, TILE, [(kc, 0)], vt)
    columns(kcode_ref, kcol, TILE)
    m_s[...] = jnp.full_like(m_s, FLOOR)
    l_s[...] = jnp.zeros_like(l_s)
    acc[...] = jnp.zeros_like(acc)

    def per_q(i, _):
        def per_k(j, _):
            @pl.when(span_hits(seg_ref, i, j))
            def _():
                allowed = kcol[at(j * TILE, TILE, TILE), :1] == qcode_ref[:1, at(i * TILE, TILE, TILE)]
                attend_add(heads, qc, kc, vt, m_s, l_s, acc, i, j, TILE, allowed | same_row(i, j))
            return 0

        lax.fori_loop(0, nq, per_k, 0)
        return 0

    lax.fori_loop(0, nq, per_q, 0)


def attend_edge_kernel(heads, extra, seg_ref, qcode_ref, hcode_ref, halo_ref, qc, m_in, l_in, acc_in, *refs):
    out_ref, wide_ref, lse_ref = refs[extra:extra + 3]
    for source, target in zip(refs[:extra], refs[extra + 3:2 * extra + 3]):
        target[...] = source[...]
    kh, vh, hcol, m_s, l_s, acc = refs[2 * extra + 3:]
    group, width = out_ref.shape
    nq, nh = group // TILE, halo_ref.shape[0] // EDGE
    m_s[...] = m_in[...]
    l_s[...] = l_in[...]
    acc[...] = acc_in[...]
    if nh:
        prepare(halo_ref, width, width, nh, EDGE, [(kh, 0)], vh)
        columns(hcode_ref, hcol, EDGE)

    def per_q(i, _):
        qrow = at(i * TILE, TILE, TILE)

        def per_edge(j, _):
            @pl.when(span_hits(seg_ref, i, nq + j))
            def _():
                allowed = hcol[at(j * EDGE, EDGE, EDGE), :1] == qcode_ref[:1, qrow]
                attend_add(heads, qc, kh, vh, m_s, l_s, acc, i, j, EDGE, allowed)
            return 0

        if nh:
            lax.fori_loop(0, nh, per_edge, 0)
        parts = []
        for h in range(heads):
            total = l_s[h, i]
            parts.append((acc[h, i, :HEAD_DIM] + acc[h, i, HEAD_DIM:]) / total)
            lse_ref[h:h + 1, qrow] = m_s[h, i] + jnp.log(total)
        out_ref[qrow, :] = jnp.concatenate(parts, axis=0).T
        return 0

    lax.fori_loop(0, nq, per_q, 0)
    wide_ref[:, :width] = out_ref[:group // 2, :]
    wide_ref[:, width:] = out_ref[group // 2:, :]


def attend_own(segs, qcode, kcode, q, kv):
    group, width = q.shape
    heads, nq = width // HEAD_DIM, group // TILE
    return call(
        functools.partial(attend_own_kernel, heads), "attend_own",
        [arr((heads, group, 3 * HEAD_DIM), BF), arr((heads, nq, 1, TILE)), arr((heads, nq, 1, TILE)),
         arr((heads, nq, 2 * HEAD_DIM, TILE))],
        [segs, qcode, kcode, q, kv],
        [pltpu.VMEM((heads, group, 3 * HEAD_DIM), BF), pltpu.VMEM((heads, nq, 2 * HEAD_DIM, TILE), BF),
         pltpu.VMEM((group, 128), F32)],
        flops=4 * group * group * width)


def attend_edge(segs, qcode, hcode, halo, state, passed=(), marks=()):
    heads, group, _ = state[0].shape
    reach, width = halo.shape[0], halo.shape[1] // 2
    nq, nh = group // TILE, reach // EDGE
    return call(
        functools.partial(attend_edge_kernel, heads, len(passed)), "attend_edge",
        [arr((group, width)), arr((group // 2, 2 * width)), arr((8, group))] + [arr(x.shape) for x in passed],
        [segs, qcode, hcode, halo, *state, *passed],
        [pltpu.VMEM((heads, reach, 3 * HEAD_DIM), BF), pltpu.VMEM((heads, nh, 2 * HEAD_DIM, EDGE), BF),
         pltpu.VMEM((reach, 128), F32)]
        + [pltpu.VMEM(x.shape, x.dtype) for x in state[1:]],
        flops=2 * group * reach * width, wide=reach > group, marks=marks)


def back_add(heads, qc, q2, dc, d2, dot_s, lse_ref, keys, values, flipped, dqa, dka, dva, i, j, size, allowed):
    qrow = at(i * TILE, TILE, TILE)
    krow = at(j * size, size, size)
    for h in range(heads):
        s = mm(keys[h, krow, :], qc[h, qrow, :], NT)
        p = jnp.exp(jnp.where(allowed, s - lse_ref[h:h + 1, qrow], FLOOR))
        dp = mm(values[h, krow, :], dc[h, qrow, :], NT)
        ds = p * (dp - dot_s[h, :, qrow])
        hi, lo = split(p)
        d128 = d2[h, qrow, :]
        dva[h] += mm(hi, d128) + mm(lo, d128)
        hi, lo = split(ds)
        q128 = q2[h, qrow, :]
        dka[h] += mm(hi, q128) + mm(lo, q128)
        k128 = flipped[h, j]
        dqa[h, i] += mm(k128, hi) + mm(k128, lo)


def back_over(heads, seg_ref, nq, count, size, first, out, dka, dva, visit):
    width = heads * HEAD_DIM

    def folded(acc):
        return jnp.concatenate([acc[h, :, :HEAD_DIM] + acc[h, :, HEAD_DIM:] for h in range(heads)], axis=1)

    def per_k(j, _):
        dka[...] = jnp.zeros_like(dka)
        dva[...] = jnp.zeros_like(dva)

        def per_q(i, _):
            @pl.when(span_hits(seg_ref, i, first + j))
            def _():
                visit(i, j)
            return 0

        lax.fori_loop(0, nq, per_q, 0)
        krow = at(j * size, size, size)
        out[krow, :width] = folded(dka)
        out[krow, width:] = folded(dva)
        return 0

    lax.fori_loop(0, count, per_k, 0)


def back_edge_kernel(heads, splits, idx, seg_ref, qcode_ref, hcode_ref, q_ref, halo_ref, o_ref, lse_ref, qc,
                     oh_ref, ol_ref, *refs):
    mg, (dhalo_ref, q2, dc, d2, dot_s, dqa, gh, gl, kh, vh, kth, hcol, prod_s, dka, dva) = (
        refs[:splits], refs[splits:])
    group, width = q_ref.shape
    nq, nh = group // TILE, halo_ref.shape[0] // EDGE
    tokens = group // splits
    if nh:
        prepare(halo_ref, width, 0, nh, EDGE, [(kh, 0), (vh, width)], kth)
        columns(hcode_ref, hcol, EDGE)
    for h in range(heads):
        hi, lo = split(q_ref[:, h * HEAD_DIM:(h + 1) * HEAD_DIM] * HEAD_DIM ** -0.5)
        q2[h] = jnp.concatenate([hi, lo], axis=1)
    dqa[...] = jnp.zeros_like(dqa)
    wrow = at(idx[0, 0] * width, width, 16)
    w_pair = (oh_ref[wrow, :], ol_ref[wrow, :])
    for r in range(splits):
        row = at(idx[0, r] * tokens, tokens, 16)
        gh[row, :], gl[row, :] = split(mg[r][...])
    step = group // 2
    for i in range(2):
        row = slice(i * step, (i + 1) * step)
        grad = mm3((gh[row, :], gl[row, :]), w_pair, NT)
        prod_s[row, :] = grad * o_ref[row, :]
        for h in range(heads):
            hi, lo = split(grad[:, h * HEAD_DIM:(h + 1) * HEAD_DIM])
            dc[h, row, :] = jnp.concatenate([hi, hi, lo], axis=1)
            d2[h, row, :] = jnp.concatenate([hi, lo], axis=1)
    for i in range(nq):
        rows = slice(i * TILE, (i + 1) * TILE)
        prod = prod_s[rows, :].T
        for h in range(heads):
            dot_s[h, :, rows] = jnp.sum(prod[h * HEAD_DIM:(h + 1) * HEAD_DIM], axis=0, keepdims=True)

    def visit(i, j):
        allowed = hcol[at(j * EDGE, EDGE, EDGE), :1] == qcode_ref[:1, at(i * TILE, TILE, TILE)]
        back_add(heads, qc, q2, dc, d2, dot_s, lse_ref, kh, vh, kth, dqa, dka, dva, i, j, EDGE, allowed)

    if nh:
        back_over(heads, seg_ref, nq, nh, EDGE, nq, dhalo_ref, dka, dva, visit)


def back_own_kernel(heads, seg_ref, qcode_ref, kcode_ref, kv_ref, lse_ref, qc, q2, dc, d2, dot_s, dq_in,
                    dq_ref, dkv_ref, kc, vc, kt, kcol, dqa, dka, dva):
    group, width = dq_ref.shape
    nq = group // TILE
    prepare(kv_ref, width, 0, nq, TILE, [(kc, 0), (vc, width)], kt)
    columns(kcode_ref, kcol, TILE)
    dqa[...] = dq_in[...]

    def visit(i, j):
        allowed = kcol[at(j * TILE, TILE, TILE), :1] == qcode_ref[:1, at(i * TILE, TILE, TILE)]
        back_add(heads, qc, q2, dc, d2, dot_s, lse_ref, kc, vc, kt, dqa, dka, dva, i, j, TILE, allowed | same_row(i, j))

    back_over(heads, seg_ref, nq, nq, TILE, 0, dkv_ref, dka, dva, visit)
    for i in range(nq):
        parts = [(dqa[h, i, :HEAD_DIM] + dqa[h, i, HEAD_DIM:]) * HEAD_DIM ** -0.5 for h in range(heads)]
        dq_ref[i * TILE:(i + 1) * TILE, :] = jnp.concatenate(parts, axis=0).T


def attend_back_edge(idx, segs, qcode, hcode, q, halo, o, lse, qc, oh, ol, mg):
    group, width = q.shape
    reach = halo.shape[0]
    heads = width // HEAD_DIM
    nq, nh = group // TILE, reach // EDGE
    full = oh.shape[1]
    H3, H2 = 3 * HEAD_DIM, 2 * HEAD_DIM
    return call(
        functools.partial(back_edge_kernel, heads, len(mg)), "back_edge",
        [arr((reach, 2 * width)), arr((heads, group, H2), BF), arr((heads, group, H3), BF), arr((heads, group, H2), BF),
         arr((heads, 1, group)), arr((heads, nq, H2, TILE)), arr((group, full), BF), arr((group, full), BF)],
        [idx, segs, qcode, hcode, q, halo, o, lse, qc, oh, ol, *mg],
        [
            pltpu.VMEM((heads, reach, H3), BF),
            pltpu.VMEM((heads, reach, H3), BF),
            pltpu.VMEM((heads, nh, H2, EDGE), BF),
            pltpu.VMEM((reach, 128), F32),
            pltpu.VMEM((group, width), F32),
            pltpu.VMEM((heads, EDGE, H2), F32),
            pltpu.VMEM((heads, EDGE, H2), F32),
        ],
        flops=2 * group * full * width, smem=2, wide=reach > group)


def attend_back_own(segs, qcode, kcode, kv, lse, qc, q2, dc, d2, dot_s, dqa, marks):
    heads, group, _ = qc.shape
    width = kv.shape[1] // 2
    nq = group // TILE
    H3, H2 = 3 * HEAD_DIM, 2 * HEAD_DIM
    return call(
        functools.partial(back_own_kernel, heads), "back_own",
        [arr((group, width)), arr((group, 2 * width))],
        [segs, qcode, kcode, kv, lse, qc, q2, dc, d2, dot_s, dqa],
        [
            pltpu.VMEM((heads, group, H3), BF),
            pltpu.VMEM((heads, group, H3), BF),
            pltpu.VMEM((heads, nq, H2, TILE), BF),
            pltpu.VMEM((group, 128), F32),
            pltpu.VMEM((heads, nq, H2, TILE), F32),
            pltpu.VMEM((heads, TILE, H2), F32),
            pltpu.VMEM((heads, TILE, H2), F32),
        ],
        flops=10 * group * group * width, marks=marks)


def weights_kernel(full, splits, idx, *refs):
    count = max([p[0] for p in full]) + 1
    weights, (uh, ul, oh, ol, u32, o32) = refs[:count], refs[count:count + 6]
    got = weights
    owners = len(full)
    rows = u32.shape[0] // owners
    for i, (n, lead) in enumerate(full):
        row = at(idx[0, splits + i] * rows, rows)
        u32[row, :] = got[n][lead]
        o32[row, :] = got[n][2]
    uh[...], ul[...] = split(u32[...])
    oh[...], ol[...] = split(o32[...])


def act_kernel(splits, whole, first, place, idx, *refs):
    got, (gh, gl, dh, dl, act_ref) = refs[:-5], refs[-5:]
    tokens = got[0].shape[0]
    down = got[splits:]
    unit = down[0].shape[0]
    blocks = dh.shape[0] // unit
    for r in range(splits):
        row = at(idx[0, r] * tokens, tokens, 16)
        gh[row, :], gl[row, :] = split(got[r][...])
    for i in range(blocks):
        if i < whole:
            row = at(idx[0, first + i] * unit, unit, 16)
            dh[row, :], dl[row, :] = split(down[i][...])
            continue
        size = unit // 4
        for z in range(4):
            quarter = idx[0, place] ^ (0, 3, 1, 2)[z]
            row = at(idx[0, first + i] * unit + quarter * size, size, 16)
            dh[row, :], dl[row, :] = split(down[whole + 4 * (i - whole) + z][...])
    step = gh.shape[0] // 2

    def rows_of(i, _):
        row = at(i * step, step, 16)
        act_ref[row, :] = mm3((gh[row, :], gl[row, :]), (dh[...], dl[...]), NT)
        return 0

    lax.fori_loop(0, 2, rows_of, 0)


def feed_kernel(splits, idx, small, base, *refs):
    (oh, ol, uh, ul, act, keep, send, mine, inv_ref, ah, al, ph, plo, mh, ml, vec, b32, x2, g32, r32) = (
        refs[splits:splits + 20])
    att = refs[:splits]
    tokens = keep.shape[1]
    group = b32.shape[0]
    part = att[0].shape[1] // 2
    gain, shift = small[6:7, :], small[7:8, :]
    up_bias = small[pl.ds(8 + idx[0, 0], 1), :]
    vec[...] = jnp.zeros_like(vec)
    step = group // 2

    def rows_of(i, _):
        row = at(i * step, step, 16)
        middle = base[row, :] + small[2:3, :]
        for s in range(splits):
            wrow = at(idx[0, s] * part, part, 16)
            piece = jnp.where(i == 0, att[s][:, :part], att[s][:, part:])
            middle = middle + mm3(split(piece), (oh[wrow, :], ol[wrow, :]))
        b32[row, :] = middle
        xhat, inverse = norm(middle)
        x2[row, :] = xhat
        g32[row, :] = jnp.broadcast_to(inverse, g32[row, :].shape)
        pair = split(xhat * gain + shift)
        mh[row, :], ml[row, :] = pair
        pre = mm3(pair, (uh[...], ul[...])) + up_bias
        square = pre * pre
        curve = jnp.tanh(SQRT_2_PI * (pre + CUBIC * square * pre))
        half = 0.5 * (1.0 + curve)
        ah[row, :], al[row, :] = split(pre * half)
        slope = half + 0.5 * pre * (1.0 - curve * curve) * SQRT_2_PI * (1.0 + 3.0 * CUBIC * square)
        grad = act[row, :] * slope
        pair = split(grad)
        ph[row, :], plo[row, :] = pair
        back = mm3(pair, (uh[...], ul[...]), NT)
        vec[0:1, :] += jnp.sum(grad, axis=0, keepdims=True)
        vec[1:2, :] += jnp.sum(back * xhat, axis=0, keepdims=True)
        vec[2:3, :] += jnp.sum(back, axis=0, keepdims=True)
        r32[row, :] = back
        return 0

    lax.fori_loop(0, 2, rows_of, 0)
    for r in range(splits):
        row = at(idx[0, r] * tokens, tokens)
        target = send if r % 2 else keep
        target[r // 2] = r32[row, :]
    row = at(idx[0, 0] * tokens, tokens)
    mine[0] = b32[row, :]
    mine[1] = x2[row, :]
    inv_ref[...] = g32[row, :]


def feed_grads_kernel(splits, first, down_rows, up_rows, idx, ah, al, ph, plo, mh, ml, gh, gl, dh, dl,
                      keep, send, *refs):
    outs, r32 = refs[:-1], refs[-1]
    downs, ups = outs[:len(outs) // 2], outs[len(outs) // 2:]
    tokens = keep.shape[1]
    step = r32.shape[0] // 2

    def left(a, b):
        def rows_of(i, _):
            lane = at(i * step, step, 128)
            r32[at(i * step, step), :] = mm3((a[0][:, lane], a[1][:, lane]), (b[0][...], b[1][...]), TN)
            return 0

        lax.fori_loop(0, 2, rows_of, 0)

    def deal(targets, rows, place):
        for target in targets:
            for c in range(target.shape[0]):
                target[c] = r32[at(idx[0, place + c], rows), :]
            place += target.shape[0]
        return place

    left((ah, al), (gh, gl))
    place = deal(downs, down_rows, first)
    left((mh, ml), (ph, plo))
    deal(ups, up_rows, place)

    def rows_of(i, _):
        row = at(i * step, step, 16)
        r32[row, :] = mm3((ah[row, :], al[row, :]), (dh[...], dl[...]))
        return 0

    lax.fori_loop(0, 2, rows_of, 0)
    for r in range(splits):
        target = send if r % 2 else keep
        target[r // 2] = r32[at(idx[0, r] * tokens, tokens), :]


def middle_kernel(small, keep, core, far, og, mine, inv, mg_ref, vec_ref):
    grad = keep[0] + core[0] + far[...]
    out = og[...] + norm_back(grad, small[6:7, :], mine[1], inv[:, :1])
    mg_ref[...] = out
    vec_ref[...] = jnp.zeros_like(vec_ref)
    vec_ref[0:1, :] = jnp.sum(out, axis=0, keepdims=True)
    vec_ref[1:2, :] = jnp.sum(og[...], axis=0, keepdims=True)


def last_grads_kernel(splits, first, edge, rows, idx, small, dq, dkv, back, base, att, vec1, vec2, gh, gl, wh, wl,
                      keep, send, *refs):
    tails, (qh, ql, xhat, r32, o32, s32, n32, vec) = refs[:-8], refs[-8:]
    part = dq.shape[1]
    width = xhat.shape[1]
    tokens = keep.shape[1]
    gain, shift = small[4:5, :], small[5:6, :]
    u = idx[0, 0]
    s32[:, :part] = dq[...]
    s32[:, part:] = dkv[...]
    s32[at(idx[0, edge], back.shape[0]), part:] += back[...]
    qkv = s32[...]
    qh[...], ql[...] = split(qkv)
    sums = jnp.sum(qkv, axis=0, keepdims=True)
    xhat[...], _ = norm(base[...])
    vec[...] = jnp.zeros_like(vec)
    step = n32.shape[0] // 2

    def rows_of(i, _):
        row = at(i * step, step, 16)
        grad = mm3((qh[row, :], ql[row, :]), (wh[...], wl[...]), NT)
        n32[row, :] = grad
        vec[4:5, :] += jnp.sum(grad * xhat[row, :], axis=0, keepdims=True)
        vec[5:6, :] += jnp.sum(grad, axis=0, keepdims=True)
        return 0

    lax.fori_loop(0, 2, rows_of, 0)
    for r in range(splits):
        target = send if r % 2 else keep
        target[r // 2] = n32[at(idx[0, r] * tokens, tokens), :]
    step = width // 2
    for i in range(2):
        lane = slice(i * step, (i + 1) * step)
        pair = split(xhat[:, lane] * gain[:, lane] + shift[:, lane])
        r32[lane, :] = mm3(pair, (qh[...], ql[...]), TN)
    o32[...] = mm3(split(att[...]), (gh[...], gl[...]), TN)
    for i in range(splits):

        @pl.when(u == i)
        def _():
            vec[0:1, i * part:(i + 1) * part] = sums[:, :part]
            vec[1:2, i * part:(i + 1) * part] = sums[:, 2 * part:]

    vec[2:4, :] = vec2[0:2, :]
    vec[6:8, :] = vec1[1:3, :]
    vec[pl.ds(8 + u, 1), :] = vec1[0:1, :]
    wide = r32.shape[1]
    outs = width // 128
    vecs = outs * EXTRA // rows
    lane_blocks = -(-wide // 128)
    spare = lane_blocks * 128 - wide
    near = 2 * lane_blocks
    total = sum(t.shape[0] for t in tails)
    spot = 0
    for t in tails:
        for c in range(t.shape[0]):
            for j in range(splits):
                row = at(idx[0, first + spot * splits + j], rows)
                start = j * lane_blocks + (outs + vecs if j >= 2 else 0)
                for k in range(lane_blocks - 1):
                    t[c, start + k] = r32[row, k * 128:(k + 1) * 128]
                k = lane_blocks - 1
                t[c, start + k, :, :128 - spare] = r32[row, k * 128:]
                t[c, start + k, :, 128 - spare:] = jnp.zeros((rows, spare), F32)
            row = at(idx[0, first + total * splits + spot], rows)
            for k in range(outs):
                t[c, near + k] = o32[row, k * 128:(k + 1) * 128]
            for k in range(outs * EXTRA // 8):
                block, low = divmod(8 * k, rows)
                lane, high = divmod(8 * k, EXTRA)
                t[c, near + outs + block, low:low + 8, :] = vec[high:high + 8, lane * 128:(lane + 1) * 128]
            spot += 1


def hidden_kernel(idx, small, base, keep, core, far, mg, out):
    tokens = mg.shape[0]
    xhat, inverse = norm(base[at(idx[0, 0] * tokens, tokens), :])
    out[...] = mg[...] + norm_back(keep[0] + core[0] + far[...], small[4:5, :], xhat, inverse)


def fold_kernel(count, *refs):
    keeps, gots, outs = refs[:count], refs[count:2 * count], refs[2 * count:]
    for i in range(count):
        stay, go = outs[2 * i:2 * i + 2]
        half = stay.shape[0]
        stay[...] = keeps[i][:half] + gots[i][:half]
        go[...] = keeps[i][half:] + gots[i][half:]


def fold(keeps, gots, marks=()):
    outs = []
    for keep in keeps:
        outs += [arr((keep.shape[0] // 2,) + keep.shape[1:])] * 2
    got = call(functools.partial(fold_kernel, len(keeps)), "fold", outs, [*keeps, *gots], smem=0, marks=marks)
    return got[::2], got[1::2]


def message_kernel(near, stop, vecs, part, far, out):
    blocks = near // 2
    out[:blocks] = part[blocks:near]
    out[blocks:blocks + vecs] = part[stop:stop + vecs] + far[:vecs]
    out[blocks + vecs:] = far[vecs + blocks:]


def place_kernel(splits, first, rows, idx, *refs):
    pieces, (gq, gk, gv, go) = refs[:-4], refs[-4:]
    part = gq.shape[1] // splits
    for z, piece in enumerate(pieces):
        row = at(idx[0, first + z] * rows, rows)
        count = gq.shape[1] // 128
        for k in range(count):
            go[row, k * 128:(k + 1) * 128] = piece[5 * splits + k]
        for r in range(splits):
            whole = jnp.concatenate([piece[5 * r + k] for k in range(5)], axis=1)
            for i in range(splits):

                @pl.when(idx[0, r] == i)
                def _():
                    for n, out in enumerate((gq, gk, gv)):
                        out[row, i * part:(i + 1) * part] = whole[:, n * part:(n + 1) * part]


def place_feed_kernel(splits, blocks, unit, first, idx, *refs):
    pieces, (gd, gu) = refs[:-2], refs[-2:]
    downs, ups = pieces[:len(pieces) // 2], pieces[len(pieces) // 2:]
    for z, (down, up) in enumerate(zip(downs, ups)):
        gd[at(idx[0, first + z] * down.shape[0], down.shape[0]), :] = down[...]
        rows = up.shape[1]
        row = at(idx[0, first + z] * rows, rows)
        for r in range(splits):
            for i in range(splits):

                @pl.when(idx[0, r] == i)
                def _():
                    for n in range(blocks):
                        start = (n * splits + i) * unit
                        gu[row, start:start + unit] = up[r, :, n * unit:(n + 1) * unit]


def swap(value, axis, mask):
    count = lax.axis_size(axis)
    return lax.ppermute(value, axis, [(i, i ^ mask) for i in range(count)])


def across(value):
    return swap(value, "ulys", 2)


def beside(value):
    return swap(value, "ulys", 1)


def over(value):
    return swap(value, "blk", 1)


def gather_splits(value):
    far = across(value)
    return [value, beside(value), far, beside(far)]


def collect(value):
    near = swap(value, "dp", 3)
    return [value, near, swap(value, "dp", 1), swap(near, "dp", 1)]


def halo_moves(group, reach, blocks):
    moves = []
    shift = 1
    while reach > 0 and shift < blocks:
        rows = min(group, reach)
        moves.append((rows, True, [(i, i - shift) for i in range(shift, blocks)]))
        moves.append((rows, False, [(i, i + shift) for i in range(blocks - shift)]))
        reach -= rows
        shift += 1
    return moves


def halo_get(value, reach, axis=0):
    blocks, group = lax.axis_size("blk"), value.shape[axis]
    parts = []
    for rows, right, moves in halo_moves(group, reach, blocks):
        start = 0 if right else group - rows
        parts.append(lax.ppermute(lax.slice_in_dim(value, start, start + rows, axis=axis), "blk", moves))
    return jnp.concatenate(parts, axis=axis)


def halo_add(value, halo, reach):
    blocks, group = lax.axis_size("blk"), value.shape[0]
    start = 0
    for rows, right, moves in halo_moves(group, reach, blocks):
        back = lax.ppermute(halo[start:start + rows], "blk", [(j, i) for i, j in moves])
        start += rows
        room = group - rows
        value = value + jnp.pad(back, ((0, room), (0, 0)) if right else ((room, 0), (0, 0)))
    return value


def local(
    hidden,
    time_embed,
    segment_ids,
    key_valid,
    out_grad,
    w_query,
    b_query,
    w_key,
    w_value,
    b_value,
    w_out,
    b_out,
    w_up,
    b_up,
    w_down,
    b_down,
    pre_gain,
    pre_shift,
    mlp_gain,
    mlp_shift,
):
    blocks, splits = lax.axis_size("blk"), lax.axis_size("ulys")
    b, u, d = (lax.axis_index(name) for name in ("blk", "ulys", "dp"))
    both = ("blk", "ulys")
    owners = blocks * splits
    tokens, width = hidden.shape
    group = tokens * splits
    part = width // splits
    rows = w_query.shape[0]
    unit = w_down.shape[0]
    units = unit * owners
    share = units // splits
    reach = group * blocks // 4
    fast = blocks == 2 and splits == 4 and lax.axis_size("dp") == 4 and reach <= group and group == width

    if fast:
        f1, f3 = (d ^ (d >> 1)) & 1, d >> 1
        quarters = [2 * (f1 ^ s) + (f3 ^ t) for s in range(2) for t in range(2)]
        owner_list = [(b ^ x) * splits + (u ^ r) for x in range(2) for r in range(4)]
        block_list = [b, b ^ 1]
        edge_row = jnp.where(b == 0, group - reach, 0)
        down_rows, up_rows, tail_rows = unit // 4, rows // 4, rows // 4
        down_table = [(b ^ x) * unit + q * down_rows for x in range(2) for q in quarters]
        up_table = [
            ((b ^ x) * splits + (u ^ r)) * rows + q * up_rows for q in quarters for x in range(2) for r in range(4)
        ]
        tail_table = [
            ((b ^ x) * splits + (u ^ r)) * rows + q * tail_rows for x in range(2) for q in quarters for r in range(4)
        ] + [(b ^ x) * rows + q * tail_rows for x in range(2) for q in quarters]
        chunks = 8
    else:
        quarters = []
        owner_list = list(range(owners))
        block_list = list(range(blocks))
        edge_row = 0
        down_rows, up_rows, tail_rows = unit, rows, rows
        down_table = [i * unit for i in range(blocks)]
        up_table = [i * rows for i in range(owners)]
        tail_table = up_table + [i * rows for i in range(blocks)]
        chunks = blocks
    entries, spots = [], []
    for values in (
        [u ^ r for r in range(splits)], owner_list, block_list, [d], [edge_row], down_table + up_table, tail_table,
        quarters,
    ):
        spots.append(len(entries))
        entries += values
    _, _, at_block, at_d, at_edge, at_feed, at_tail, at_quarter = spots
    idx = jnp.stack([jnp.asarray(v, jnp.int32) for v in entries]).reshape(1, -1)

    segments = segment_ids[0] + 1
    codes = jnp.stack([segments, jnp.where(key_valid[0] == 1, segments, 0)]).astype(F32)
    small = jnp.stack([b_query, b_value, b_out, b_down, pre_gain, pre_shift, mlp_gain, mlp_shift])
    small = lax.dynamic_update_slice(jnp.zeros((EXTRA, width), F32), small, (0, (b * splits + u) * rows))
    small = lax.dynamic_update_slice(small, b_up[None], (8 + u, b * unit))
    if fast:
        small = lax.dynamic_update_slice(small, codes, (12, 0))
        other = over(small)
        small = small + other
        halo_codes = jnp.where(b == 0, other[12:14, :reach], other[12:14, group - reach:group])
    else:
        small = lax.psum(small, "blk")
        halo_codes = halo_get(codes, reach, axis=1)
    tiles = codes[0].reshape(-1, TILE)
    edges = halo_codes[0].reshape(-1, EDGE)
    bounds = jnp.concatenate(
        [
            jnp.stack([tiles[:, 0], tiles[:, -1]], axis=1).reshape(-1),
            jnp.stack([jnp.min(jnp.where(edges == 0, 1e6, edges), axis=1), jnp.max(edges, axis=1)], axis=1).reshape(-1),
        ]
    ).astype(jnp.int32).reshape(1, -1)
    def make_base(marks):
        return call(
            functools.partial(base_kernel, at_d), "base",
            [arr((tokens + EXTRA, width)), arr((unit // 4 if fast else 8, width))],
            [idx, hidden, time_embed, small, w_down], marks=marks)

    if fast:
        tables = [idx, bounds, codes, halo_codes, small]
        near, far, *tables = call(
            pack_qkv_kernel, "pack_qkv",
            [arr((2, rows, 3 * part))] * 2 + [arr(x.shape, x.dtype) for x in tables],
            [*tables, w_query, w_key, w_value], smem=2)
        idx, bounds, codes, halo_codes, small = tables
        pieces = [(i, i % 2) for i in range(8)]
        far = across(far)
        near_over = over(near)
        base, down_quarter = make_base([far, near_over])
        far_base = across(base)
        qkv_arrays = [near, beside(near), far, beside(far)]
        near = near_over
        far = over(far)
        down_quarter = over(down_quarter)
        qkv_arrays += [near, beside(near), far, beside(far)]
        base_all = [base, beside(base), far_base, beside(far_base)]
        near2, far2 = call(
            functools.partial(pack_feed_kernel, splits, blocks), "pack_feed", [arr((3, rows, share))] * 2,
            [idx, w_up, w_out], marks=[far])
        far2 = across(far2)
        feed_arrays = [near2, beside(near2), far2, beside(far2)]
        near2 = over(near2)
        feed_arrays += [near2, beside(near2)]
        whole = 1
    else:
        cut = jnp.stack([w_query, w_key, w_value], axis=1).reshape(rows, 3, splits, part)
        cut = cut.transpose(2, 0, 1, 3).reshape(splits, rows, 3 * part)
        cut = jnp.broadcast_to(cut[None], (blocks,) + cut.shape).reshape(owners, rows, 3 * part)
        got = lax.all_to_all(cut, both, 0, 0, tiled=True)
        qkv_arrays = [got[i:i + 1] for i in range(owners)]
        cut = w_up.reshape(rows, blocks, splits, unit).transpose(2, 0, 1, 3).reshape(splits, rows, share)
        cut = jnp.broadcast_to(cut[None], (blocks,) + cut.shape).reshape(owners, rows, share)
        got = lax.all_to_all(cut, both, 0, 0, tiled=True)
        outs = lax.all_gather(w_out, both, axis=0, tiled=False)
        feed_arrays = [jnp.stack([got[i], got[i], outs[i]]) for i in range(owners)]
        pieces = [(i, 0) for i in range(owners)]
        whole = blocks
        base, down_quarter = make_base([])
        base_all = gather_splits(base)
        gathered = lax.all_gather(w_down, "blk", axis=0, tiled=False)
        down = [gathered[i] for i in range(blocks)]

    query_codes, key_codes, edge_codes = codes, codes, halo_codes
    query, key_value, edge_kv, base, small, qkv_hi, qkv_lo, own_grad = call(
        functools.partial(qkv_kernel, pieces, splits, at_edge), "qkv",
        [arr((group, part)), arr((group, 2 * part)), arr((reach if fast else 8, 2 * part)), arr((group, width)),
         arr((EXTRA, width)), arr((width, 3 * part), BF), arr((width, 3 * part), BF), arr((tokens, width))],
        [idx, out_grad, *base_all, *qkv_arrays],
        [pltpu.VMEM((width, 3 * part), F32), pltpu.VMEM((group, width), BF), pltpu.VMEM((group, width), BF)],
        flops=2 * group * width * 3 * part)
    halo = over(edge_kv) if fast else halo_get(key_value, reach)
    state = attend_own(bounds, query_codes, key_codes, query, key_value)
    grads = gather_splits(own_grad)
    if fast:
        down = [w_down, down_quarter] + [swap(down_quarter, "dp", mask) for mask in (3, 1, 2)]
        attended, attended_wide, lse, far2 = attend_edge(bounds, query_codes, edge_codes, halo, state, (far2,), [*down[2:], grads[2], near2])
        far2 = over(far2)
        feed_arrays += [far2, beside(far2)]
    else:
        attended, attended_wide, lse = attend_edge(bounds, query_codes, edge_codes, halo, state)
    attended_all = gather_splits(attended_wide)
    og_hi, og_lo, down_hi, down_lo, act_grad = call(
        functools.partial(act_kernel, splits, whole, at_block, at_d), "act",
        [arr((group, width), BF)] * 2 + [arr((share, width), BF)] * 2 + [arr((group, share))],
        [idx, *grads, *down],
        flops=2 * group * width * share, marks=[attended_all[2]])
    up_hi, up_lo, out_hi, out_lo = call(
        functools.partial(weights_kernel, pieces, splits), "weights",
        [arr((width, share), BF)] * 2 + [arr((width, width), BF)] * 2,
        [idx, *feed_arrays],
        [pltpu.VMEM((width, share), F32), pltpu.VMEM((width, width), F32)], marks=[act_grad])

    pair = [arr((group, share), BF)] * 2
    keep, send, mine, inverse2, act_hi, act_lo, pre_hi, pre_lo, in_hi, in_lo, vec_feed = call(
        functools.partial(feed_kernel, splits), "feed",
        [arr((2, tokens, width))] * 2 + [arr((2, tokens, width)), arr((tokens, 128))] + pair * 2
        + [arr((group, width), BF)] * 2 + [arr((8, width))],
        [idx, small, base, *attended_all, out_hi, out_lo, up_hi, up_lo, act_grad],
        [pltpu.VMEM((group, width), F32), pltpu.VMEM((group, width), F32), pltpu.VMEM((group, 128), F32),
         pltpu.VMEM((group, width), F32)],
        flops=2 * group * width * (width + 2 * share))
    core = beside(send)
    near_sum = keep[1] + core[1]
    far_sum = across(near_sum)

    if fast:
        feed_outs = [arr((4, down_rows, width))] * 2 + [arr((8 * splits // 2, up_rows, share))] * 2
    else:
        feed_outs = [arr((blocks, down_rows, width)), arr((owners, up_rows, share))]
    keep_out, send_out, *feed_grads = call(
        functools.partial(feed_grads_kernel, splits, at_feed, down_rows, up_rows), "feed_grads",
        [arr((2, tokens, width))] * 2 + feed_outs,
        [idx, act_hi, act_lo, pre_hi, pre_lo, in_hi, in_lo, og_hi, og_lo, down_hi, down_lo],
        [pltpu.VMEM((group, width), F32)],
        flops=6 * group * width * share, marks=[near_sum])
    if fast:
        down_keep, down_send, up_keep, up_send = feed_grads
        down_got = over(down_send)
        up_got = swap(up_send, "dp", 1)

    middle_grad, vec_middle = call(
        middle_kernel, "middle",
        [arr((tokens, width)), arr((8, width))],
        [small, keep, core, far_sum, out_grad, mine, inverse2], smem=0, marks=[keep_out])
    middle_all = gather_splits(middle_grad)

    halo_grad, q2, dc, d2, dots, dq_part, mg_hi, mg_lo = attend_back_edge(
        idx, bounds, query_codes, edge_codes, query, halo, attended, lse, state[0], out_hi, out_lo, middle_all)
    if fast:
        returned = over(halo_grad)
        (down_keep, up_keep), (down_send, up_send) = fold((down_keep, up_keep), (down_got, up_got), [halo_grad])
        down_got = swap(down_send, "dp", 1)
        up_got = swap(up_send, "dp", 3)
        own_marks = [down_keep]
    else:
        own_marks = []
    query_grad, kv_grad = attend_back_own(
        bounds, query_codes, key_codes, key_value, lse, state[0], q2, dc, d2, dots, dq_part, own_marks)
    if not fast:
        kv_grad = halo_add(kv_grad, halo_grad, reach)
        returned = jnp.zeros((8, 2 * part), F32)

    lane_blocks = -(-3 * part // 128)
    outs, vecs = width // 128, width // 128 * EXTRA // tail_rows
    total_blocks = splits * lane_blocks + outs + vecs
    tail_outs = [arr((2, total_blocks, tail_rows, 128))] * 4 if fast else [arr((blocks, total_blocks, tail_rows, 128))]
    keep_in, send_in, *tail = call(
        functools.partial(last_grads_kernel, splits, at_tail, at_edge, tail_rows), "last_grads",
        [arr((2, tokens, width))] * 2 + tail_outs,
        [idx, small, query_grad, kv_grad, returned, base, attended, vec_feed, vec_middle, mg_hi, mg_lo, qkv_hi, qkv_lo],
        [pltpu.VMEM((group, 3 * part), BF), pltpu.VMEM((group, 3 * part), BF), pltpu.VMEM((group, width), F32),
         pltpu.VMEM((width, 3 * part), F32), pltpu.VMEM((part, width), F32), pltpu.VMEM((group, 3 * part), F32),
         pltpu.VMEM((group, width), F32), pltpu.VMEM((EXTRA, width), F32)],
        flops=2 * group * width * 7 * part, marks=[])
    to_owner = [(i * splits + j, j * blocks + i) for i in range(blocks) for j in range(splits)]
    near = 2 * lane_blocks
    if fast:
        tail_near, tail_far, send_near, send_far = tail
        got_far = over(send_far)
        got_near = over(send_near)
        core_in = beside(send_in)
        far_in = across(keep_in[1] + core_in[1])

        (down_keep, up_keep), (down_send, up_send) = fold((down_keep, up_keep), (down_got, up_got), [keep_in])
        down_got = swap(down_send, "dp", 3)
        up_got = over(up_send)
        tail_got = swap(tail_far + got_far, "dp", 1)
        tail_near = tail_near + got_near
        part_down = (down_keep + down_got)[0]
        part_up = up_keep + up_got
        far_up = across(part_up[2:])
        core_up = beside(jnp.stack([part_up[1], far_up[1]]))
        part_up = jnp.stack([part_up[0], core_up[0], far_up[0], core_up[1]])
        all_down = collect(part_down)
        all_up = collect(part_up)
        (tail_keep,), (tail_send,) = fold((tail_near,), (tail_got,), all_down)
        part_tail = (tail_keep + swap(tail_send, "dp", 3))[0]

        far_tail = across(part_tail[near + outs:])
        message, = call(
            functools.partial(message_kernel, near, near + outs, vecs), "message", [arr(far_tail.shape)],
            [part_tail, far_tail], smem=0, marks=all_up)
        core_tail = beside(message)
        vec = part_tail[near + outs:near + outs + vecs] + far_tail[:vecs] + core_tail[lane_blocks:lane_blocks + vecs]
        owned = lax.ppermute(part_tail[near:near + outs], both, to_owner)
        part_tail = jnp.concatenate([
            part_tail[:lane_blocks], core_tail[:lane_blocks], far_tail[vecs:vecs + lane_blocks],
            core_tail[lane_blocks + vecs:], owned])
        all_tail = collect(part_tail)
        total_down, total_up = call(
            functools.partial(place_feed_kernel, splits, blocks, unit, at_quarter), "place_feed",
            [arr((unit, width)), arr((rows, units))],
            [idx, *all_down, *all_up])
        total_query, total_key, total_value, total_out = call(
            functools.partial(place_kernel, splits, at_quarter, tail_rows), "place",
            [arr((rows, width))] * 4,
            [idx, *all_tail])
    else:
        core_in = beside(send_in)
        far_in = across(keep_in[1] + core_in[1])
        total_down, total_up, tail = [
            lax.psum(lax.psum_scatter(g.reshape((blocks, -1) + g.shape[1:]), "blk", scatter_dimension=0, tiled=False), "dp")
            for g in (*feed_grads, *tail)
        ]
        total_down = total_down.reshape(unit, width)
        total_up = lax.all_to_all(total_up, "ulys", 0, 0, tiled=True)
        total_up = total_up.reshape(splits, rows, blocks, unit).transpose(1, 2, 0, 3).reshape(rows, units)
        tail = tail[0]
        total_out = lax.ppermute(tail[near:near + outs], both, to_owner).transpose(1, 0, 2).reshape(rows, width)
        vec = lax.psum(tail[near + outs:near + outs + vecs], "ulys")
        got = jnp.concatenate([tail[:near], tail[near + outs + vecs:]]).reshape(splits, lane_blocks, rows, 128)
        got = lax.all_to_all(got, "ulys", 0, 0, tiled=True).transpose(2, 0, 1, 3).reshape(rows, splits, lane_blocks * 128)
        total_query, total_key, total_value = (
            got[:, :, i * part:(i + 1) * part].reshape(rows, width) for i in range(3)
        )
    (hidden_grad,) = call(
        hidden_kernel, "hidden",
        [arr((tokens, width))],
        [idx, small, base, keep_in, core_in, far_in, middle_grad])

    core_out = beside(send_out)
    far_out = across(keep_out[1] + core_out[1])
    output = mine[0] + small[3:4] + keep_out[0] + core_out[0] + far_out

    vec = vec.reshape(outs, EXTRA, 128).transpose(1, 0, 2).reshape(EXTRA, width)
    vector = lax.dynamic_slice(vec, (0, (b * splits + u) * rows), (8, rows))
    up_vector = lax.dynamic_slice(vec, (8 + u, b * unit), (1, unit))[0]
    return (
        output,
        hidden_grad,
        total_query,
        vector[0],
        total_key,
        total_value,
        vector[1],
        total_out,
        vector[2],
        total_up,
        up_vector,
        total_down,
        vector[3],
        vector[4],
        vector[5],
        vector[6],
        vector[7],
    )


def solution(mesh):
    tokens = P(("dp", "blk", "ulys"), None)
    matrix = P(("blk", "ulys"), None)
    vector = P(("blk", "ulys"))
    return jax.shard_map(
        local,
        mesh=mesh,
        in_specs=(
            tokens,
            P("dp", None),
            P("dp", "blk"),
            P("dp", "blk"),
            tokens,
            matrix,
            vector,
            matrix,
            matrix,
            vector,
            matrix,
            vector,
            matrix,
            vector,
            matrix,
            vector,
            vector,
            vector,
            vector,
            vector,
        ),
        out_specs=(
            tokens,
            tokens,
            matrix,
            vector,
            matrix,
            matrix,
            vector,
            matrix,
            vector,
            matrix,
            vector,
            matrix,
            vector,
            vector,
            vector,
            vector,
            vector,
        ),
        check_vma=False,
    )
```

```python
import functools
import math

import jax
import jax.numpy as jnp
from jax import lax
from jax.experimental import pallas as pl
from jax.experimental.pallas import tpu as pltpu
from jax.sharding import PartitionSpec as P

HEAD_DIM = 64
FLOOR = -1e30
SQRT_2_PI = 0.7978845608028654
CUBIC = 0.044715
EXTRA = 16
TILE = 256
EDGE = 128
BF = jnp.bfloat16
F32 = jnp.float32
NN = (((1,), (0,)), ((), ()))
NT = (((1,), (1,)), ((), ()))
TN = (((0,), (0,)), ((), ()))
VM = pl.BlockSpec(memory_space=pltpu.VMEM)
SM = pl.BlockSpec(memory_space=pltpu.SMEM)
LIMITS = {"attend_own": 10, "attend_edge": 10, "back_edge": 12, "back_own": 12, "act": 14, "weights": 16, "feed_grads": 12, "place": 8, "hidden": 6, "middle": 6, "last_grads": 16, "fold": 10, "base": 6, "pack_qkv": 8, "pack_feed": 10}


def split(x):
    hi = x.astype(BF)
    return hi, (x - hi.astype(F32)).astype(BF)


def mm(a, b, dims=NN):
    return lax.dot_general(a, b, dims, preferred_element_type=F32)


def mm3(a, b, dims=NN):
    return mm(a[0], b[0], dims) + (mm(a[0], b[1], dims) + mm(a[1], b[0], dims))


def at(start, size, step=8):
    return pl.ds(pl.multiple_of(start, step), size)


def call(kernel, name, outs, ins, scratch=(), flops=0, smem=1, limit=16, wide=False, marks=()):
    inner, count, ins = kernel, len(ins), list(ins) + list(marks)

    def kernel(*refs):
        return inner(*refs[:count], *refs[len(ins):])

    size = sum(math.prod(x.shape) * x.dtype.itemsize for x in list(outs) + list(ins[smem:count]))
    return pl.pallas_call(
        kernel,
        out_shape=tuple(outs),
        in_specs=[SM] * smem + [VM] * (count - smem) + [pl.BlockSpec(memory_space=pl.ANY)] * len(marks),
        out_specs=tuple(SM if x.dtype == jnp.int32 else VM for x in outs),
        scratch_shapes=list(scratch),
        compiler_params=pltpu.CompilerParams(vmem_limit_bytes=(48 if wide else LIMITS.get(name, limit)) << 20),
        cost_estimate=pl.CostEstimate(flops=1, bytes_accessed=1, transcendentals=0),
        name=name,
    )(*ins)


def arr(shape, dtype=F32):
    return jax.ShapeDtypeStruct(tuple(shape), dtype)


def norm(x):
    centred = x - jnp.mean(x, axis=-1, keepdims=True)
    inverse = lax.rsqrt(jnp.mean(centred * centred, axis=-1, keepdims=True) + 1e-05)
    return centred * inverse, inverse


def norm_back(grad, gain, xhat, inverse):
    scaled = grad * gain
    mean = jnp.mean(scaled, axis=-1, keepdims=True)
    lean = jnp.mean(scaled * xhat, axis=-1, keepdims=True)
    return (scaled - mean - xhat * lean) * inverse


def pick(index, choices):
    value = choices[0]
    for i in range(1, len(choices)):
        value = jnp.where(index == i, choices[i], value)
    return value


def first_kernel(count, numbers, *refs):
    for source, target in zip((numbers,) + refs[:count], refs[count:]):
        if target.dtype == jnp.int32:
            for i in range(target.shape[1]):
                target[0, i] = source[0, i]
        else:
            target[...] = source[...]


def pack_qkv_kernel(idx, bounds, codes, halo_codes, small, wq, wk, wv, near, far, *outs):
    first_kernel(4, idx, bounds, codes, halo_codes, small, *outs)
    part = near.shape[2] // 3
    splits = wq.shape[1] // part
    for r in range(splits):
        target, k = (near, r) if r < 2 else (far, r - 2)
        for u in range(splits):

            @pl.when(idx[0, r] == u)
            def _():
                for i, w in enumerate((wq, wk, wv)):
                    target[k, :, i * part:(i + 1) * part] = w[:, u * part:(u + 1) * part]


def pack_feed_kernel(splits, blocks, place, idx, wup, wout, wdown, near, far, down_quarter):
    unit = near.shape[2] // blocks
    for r in range(splits):
        target, k = (near, r) if r < 2 else (far, r - 2)
        for u in range(splits):

            @pl.when(idx[0, r] == u)
            def _():
                for b in range(blocks):
                    lane = (b * splits + u) * unit
                    target[k, :, b * unit:(b + 1) * unit] = wup[:, lane:lane + unit]
    near[2] = wout[...]
    far[2] = wout[...]
    size = down_quarter.shape[0]
    down_quarter[...] = wdown[at(idx[0, place] * size, size), :]


def base_kernel(hidden, embed, small, out):
    tokens = hidden.shape[0]
    out[:tokens, :] = hidden[...] + embed[...]
    out[tokens:, :] = small[...]


def qkv_kernel(pieces, splits, edge, idx, og, *refs):
    base, rest = refs[:splits], refs[splits:]
    count = max(p[0] for p in pieces) + 1
    weights = rest[:count]
    (q_ref, kv_ref, edge_ref, base_ref, small_ref, wh, wl, og_ref, w32, nh, nl) = rest[count:count + 11]
    got = base + weights
    tokens = base[0].shape[0] - EXTRA
    part = q_ref.shape[1]
    rows = w32.shape[0] // len(pieces)
    small = None
    for r in range(splits):
        rest = got[r][tokens:, :]
        small = rest if small is None else small + rest
    small_ref[...] = small
    gain, shift = small[4:5], small[5:6]
    for r in range(splits):
        row = at(idx[0, r] * tokens, tokens, 16)
        x = got[r][:tokens, :]
        base_ref[row, :] = x
        xhat, _ = norm(x)
        nh[row, :], nl[row, :] = split(xhat * gain + shift)
    for i, (n, lead) in enumerate(pieces):
        w32[at(idx[0, splits + i] * rows, rows), :] = got[splits + n][lead, :rows, :]
    wh[...], wl[...] = split(w32[...])
    u = idx[0, 0]
    qb = pick(u, [small[0:1, i * part:(i + 1) * part] for i in range(splits)])
    vb = pick(u, [small[1:2, i * part:(i + 1) * part] for i in range(splits)])
    bias = jnp.concatenate([qb, jnp.zeros_like(qb), vb], axis=1)
    step = nh.shape[0] // 2

    def rows_of(i, _):
        row = at(i * step, step, 16)
        out = mm3((nh[row, :], nl[row, :]), (wh[...], wl[...])) + bias
        q_ref[row, :] = out[:, :part]
        kv_ref[row, :] = out[:, part:]
        return 0

    lax.fori_loop(0, 2, rows_of, 0)
    reach = edge_ref.shape[0]
    edge_ref[...] = kv_ref[at(idx[0, edge], reach), :]
    og_ref[...] = og[...]


def span_hits(seg, i, j):
    return (seg[0, 2 * j + 1] >= seg[0, 2 * i]) & (seg[0, 2 * j] <= seg[0, 2 * i + 1])


def prepare(src, width, first, count, size, pairs, flipped):
    heads = width // HEAD_DIM
    for scratch, start in pairs:
        for h in range(heads):
            hi, lo = split(src[:, start + h * HEAD_DIM:start + (h + 1) * HEAD_DIM])
            scratch[h] = jnp.concatenate([hi, lo, hi], axis=1)
    for j in range(count):
        turned = src[j * size:(j + 1) * size, first:first + width].T
        for h in range(heads):
            hi, lo = split(turned[h * HEAD_DIM:(h + 1) * HEAD_DIM])
            flipped[h, j] = jnp.concatenate([hi, lo], axis=0)


def columns(codes, out, size):
    for j in range(out.shape[0] // size):
        row = codes[1:2, j * size:(j + 1) * size]
        out[j * size:(j + 1) * size, :] = jnp.broadcast_to(row, (128, size)).T


def same_row(i, j):
    return (lax.broadcasted_iota(jnp.int32, (TILE, TILE), 0)
            - lax.broadcasted_iota(jnp.int32, (TILE, TILE), 1)) == (i - j) * TILE


def attend_add(heads, qc, keys, flipped, m_s, l_s, acc, i, j, size, allowed):
    qrow = at(i * TILE, TILE, TILE)
    krow = at(j * size, size, size)
    for h in range(heads):
        s = jnp.where(allowed, mm(keys[h, krow, :], qc[h, qrow, :], NT), FLOOR)
        m_old = m_s[h, i]
        m_new = jnp.maximum(m_old, jnp.max(s, axis=0, keepdims=True))
        p = jnp.where(allowed, jnp.exp(s - m_new), 0.0)
        factor = jnp.exp(m_old - m_new)
        m_s[h, i] = m_new
        l_s[h, i] = l_s[h, i] * factor + jnp.sum(p, axis=0, keepdims=True)
        hi, lo = split(p)
        v128 = flipped[h, j]
        acc[h, i] = acc[h, i] * factor + mm(v128, hi) + mm(v128, lo)


def attend_own_kernel(heads, seg_ref, qcode_ref, kcode_ref, q_ref, kv_ref, qc, m_s, l_s, acc, kc, vt, kcol):
    group, width = q_ref.shape
    nq = group // TILE
    for h in range(heads):
        hi, lo = split(q_ref[:, h * HEAD_DIM:(h + 1) * HEAD_DIM] * HEAD_DIM ** -0.5)
        qc[h] = jnp.concatenate([hi, hi, lo], axis=1)
    prepare(kv_ref, width, width, nq, TILE, [(kc, 0)], vt)
    columns(kcode_ref, kcol, TILE)
    m_s[...] = jnp.full_like(m_s, FLOOR)
    l_s[...] = jnp.zeros_like(l_s)
    acc[...] = jnp.zeros_like(acc)

    def per_q(i, _):
        def per_k(j, _):
            @pl.when(span_hits(seg_ref, i, j))
            def _():
                allowed = kcol[at(j * TILE, TILE, TILE), :1] == qcode_ref[:1, at(i * TILE, TILE, TILE)]
                attend_add(heads, qc, kc, vt, m_s, l_s, acc, i, j, TILE, allowed | same_row(i, j))
            return 0

        lax.fori_loop(0, nq, per_k, 0)
        return 0

    lax.fori_loop(0, nq, per_q, 0)


def attend_edge_kernel(heads, extra, seg_ref, qcode_ref, hcode_ref, halo_ref, qc, m_in, l_in, acc_in, *refs):
    out_ref, wide_ref, lse_ref = refs[extra:extra + 3]
    for source, target in zip(refs[:extra], refs[extra + 3:2 * extra + 3]):
        target[...] = source[...]
    kh, vh, hcol, m_s, l_s, acc = refs[2 * extra + 3:]
    group, width = out_ref.shape
    nq, nh = group // TILE, halo_ref.shape[0] // EDGE
    m_s[...] = m_in[...]
    l_s[...] = l_in[...]
    acc[...] = acc_in[...]
    if nh:
        prepare(halo_ref, width, width, nh, EDGE, [(kh, 0)], vh)
        columns(hcode_ref, hcol, EDGE)

    def per_q(i, _):
        qrow = at(i * TILE, TILE, TILE)

        def per_edge(j, _):
            @pl.when(span_hits(seg_ref, i, nq + j))
            def _():
                allowed = hcol[at(j * EDGE, EDGE, EDGE), :1] == qcode_ref[:1, qrow]
                attend_add(heads, qc, kh, vh, m_s, l_s, acc, i, j, EDGE, allowed)
            return 0

        if nh:
            lax.fori_loop(0, nh, per_edge, 0)
        parts = []
        for h in range(heads):
            total = l_s[h, i]
            parts.append((acc[h, i, :HEAD_DIM] + acc[h, i, HEAD_DIM:]) / total)
            lse_ref[h:h + 1, qrow] = m_s[h, i] + jnp.log(total)
        out_ref[qrow, :] = jnp.concatenate(parts, axis=0).T
        return 0

    lax.fori_loop(0, nq, per_q, 0)
    wide_ref[:, :width] = out_ref[:group // 2, :]
    wide_ref[:, width:] = out_ref[group // 2:, :]


def attend_own(segs, qcode, kcode, q, kv):
    group, width = q.shape
    heads, nq = width // HEAD_DIM, group // TILE
    return call(
        functools.partial(attend_own_kernel, heads), "attend_own",
        [arr((heads, group, 3 * HEAD_DIM), BF), arr((heads, nq, 1, TILE)), arr((heads, nq, 1, TILE)),
         arr((heads, nq, 2 * HEAD_DIM, TILE))],
        [segs, qcode, kcode, q, kv],
        [pltpu.VMEM((heads, group, 3 * HEAD_DIM), BF), pltpu.VMEM((heads, nq, 2 * HEAD_DIM, TILE), BF),
         pltpu.VMEM((group, 128), F32)],
        flops=4 * group * group * width)


def attend_edge(segs, qcode, hcode, halo, state, passed=(), marks=()):
    heads, group, _ = state[0].shape
    reach, width = halo.shape[0], halo.shape[1] // 2
    nq, nh = group // TILE, reach // EDGE
    return call(
        functools.partial(attend_edge_kernel, heads, len(passed)), "attend_edge",
        [arr((group, width)), arr((group // 2, 2 * width)), arr((8, group))] + [arr(x.shape) for x in passed],
        [segs, qcode, hcode, halo, *state, *passed],
        [pltpu.VMEM((heads, reach, 3 * HEAD_DIM), BF), pltpu.VMEM((heads, nh, 2 * HEAD_DIM, EDGE), BF),
         pltpu.VMEM((reach, 128), F32)]
        + [pltpu.VMEM(x.shape, x.dtype) for x in state[1:]],
        flops=2 * group * reach * width, wide=reach > group, marks=marks)


def back_add(heads, qc, q2, dc, d2, dot_s, lse_ref, keys, values, flipped, dqa, dka, dva, i, j, size, allowed):
    qrow = at(i * TILE, TILE, TILE)
    krow = at(j * size, size, size)
    for h in range(heads):
        s = mm(keys[h, krow, :], qc[h, qrow, :], NT)
        p = jnp.exp(jnp.where(allowed, s - lse_ref[h:h + 1, qrow], FLOOR))
        dp = mm(values[h, krow, :], dc[h, qrow, :], NT)
        ds = p * (dp - dot_s[h, :, qrow])
        hi, lo = split(p)
        d128 = d2[h, qrow, :]
        dva[h] += mm(hi, d128) + mm(lo, d128)
        hi, lo = split(ds)
        q128 = q2[h, qrow, :]
        dka[h] += mm(hi, q128) + mm(lo, q128)
        k128 = flipped[h, j]
        dqa[h, i] += mm(k128, hi) + mm(k128, lo)


def back_over(heads, seg_ref, nq, count, size, first, out, dka, dva, visit):
    width = heads * HEAD_DIM

    def folded(acc):
        return jnp.concatenate([acc[h, :, :HEAD_DIM] + acc[h, :, HEAD_DIM:] for h in range(heads)], axis=1)

    def per_k(j, _):
        dka[...] = jnp.zeros_like(dka)
        dva[...] = jnp.zeros_like(dva)

        def per_q(i, _):
            @pl.when(span_hits(seg_ref, i, first + j))
            def _():
                visit(i, j)
            return 0

        lax.fori_loop(0, nq, per_q, 0)
        krow = at(j * size, size, size)
        out[krow, :width] = folded(dka)
        out[krow, width:] = folded(dva)
        return 0

    lax.fori_loop(0, count, per_k, 0)


def back_edge_kernel(heads, splits, idx, seg_ref, qcode_ref, hcode_ref, q_ref, halo_ref, o_ref, lse_ref, qc,
                     oh_ref, ol_ref, *refs):
    mg, (dhalo_ref, q2, dc, d2, dot_s, dqa, gh, gl, kh, vh, kth, hcol, prod_s, dka, dva) = (
        refs[:splits], refs[splits:])
    group, width = q_ref.shape
    nq, nh = group // TILE, halo_ref.shape[0] // EDGE
    tokens = group // splits
    if nh:
        prepare(halo_ref, width, 0, nh, EDGE, [(kh, 0), (vh, width)], kth)
        columns(hcode_ref, hcol, EDGE)
    for h in range(heads):
        hi, lo = split(q_ref[:, h * HEAD_DIM:(h + 1) * HEAD_DIM] * HEAD_DIM ** -0.5)
        q2[h] = jnp.concatenate([hi, lo], axis=1)
    dqa[...] = jnp.zeros_like(dqa)
    wrow = at(idx[0, 0] * width, width, 16)
    w_pair = (oh_ref[wrow, :], ol_ref[wrow, :])
    for r in range(splits):
        row = at(idx[0, r] * tokens, tokens, 16)
        gh[row, :], gl[row, :] = split(mg[r][...])
    step = group // 3

    def rows_of(i, _):
        row = at(i * step, step, 16)
        grad = mm3((gh[row, :], gl[row, :]), w_pair, NT)
        prod_s[row, :] = grad * o_ref[row, :]
        for h in range(heads):
            hi, lo = split(grad[:, h * HEAD_DIM:(h + 1) * HEAD_DIM])
            dc[h, row, :] = jnp.concatenate([hi, hi, lo], axis=1)
            d2[h, row, :] = jnp.concatenate([hi, lo], axis=1)
        return 0

    lax.fori_loop(0, 3, rows_of, 0)
    for i in range(nq):
        rows = slice(i * TILE, (i + 1) * TILE)
        prod = prod_s[rows, :].T
        for h in range(heads):
            dot_s[h, :, rows] = jnp.sum(prod[h * HEAD_DIM:(h + 1) * HEAD_DIM], axis=0, keepdims=True)

    def visit(i, j):
        allowed = hcol[at(j * EDGE, EDGE, EDGE), :1] == qcode_ref[:1, at(i * TILE, TILE, TILE)]
        back_add(heads, qc, q2, dc, d2, dot_s, lse_ref, kh, vh, kth, dqa, dka, dva, i, j, EDGE, allowed)

    if nh:
        back_over(heads, seg_ref, nq, nh, EDGE, nq, dhalo_ref, dka, dva, visit)


def back_own_kernel(heads, seg_ref, qcode_ref, kcode_ref, kv_ref, lse_ref, qc, q2, dc, d2, dot_s, dq_in,
                    dq_ref, dkv_ref, kc, vc, kt, kcol, dqa, dka, dva):
    group, width = dq_ref.shape
    nq = group // TILE
    prepare(kv_ref, width, 0, nq, TILE, [(kc, 0), (vc, width)], kt)
    columns(kcode_ref, kcol, TILE)
    dqa[...] = dq_in[...]

    def visit(i, j):
        allowed = kcol[at(j * TILE, TILE, TILE), :1] == qcode_ref[:1, at(i * TILE, TILE, TILE)]
        back_add(heads, qc, q2, dc, d2, dot_s, lse_ref, kc, vc, kt, dqa, dka, dva, i, j, TILE, allowed | same_row(i, j))

    back_over(heads, seg_ref, nq, nq, TILE, 0, dkv_ref, dka, dva, visit)
    for i in range(nq):
        parts = [(dqa[h, i, :HEAD_DIM] + dqa[h, i, HEAD_DIM:]) * HEAD_DIM ** -0.5 for h in range(heads)]
        dq_ref[i * TILE:(i + 1) * TILE, :] = jnp.concatenate(parts, axis=0).T


def attend_back_edge(idx, segs, qcode, hcode, q, halo, o, lse, qc, oh, ol, mg):
    group, width = q.shape
    reach = halo.shape[0]
    heads = width // HEAD_DIM
    nq, nh = group // TILE, reach // EDGE
    full = oh.shape[1]
    H3, H2 = 3 * HEAD_DIM, 2 * HEAD_DIM
    return call(
        functools.partial(back_edge_kernel, heads, len(mg)), "back_edge",
        [arr((reach, 2 * width)), arr((heads, group, H2), BF), arr((heads, group, H3), BF), arr((heads, group, H2), BF),
         arr((heads, 1, group)), arr((heads, nq, H2, TILE)), arr((group, full), BF), arr((group, full), BF)],
        [idx, segs, qcode, hcode, q, halo, o, lse, qc, oh, ol, *mg],
        [
            pltpu.VMEM((heads, reach, H3), BF),
            pltpu.VMEM((heads, reach, H3), BF),
            pltpu.VMEM((heads, nh, H2, EDGE), BF),
            pltpu.VMEM((reach, 128), F32),
            pltpu.VMEM((group, width), F32),
            pltpu.VMEM((heads, EDGE, H2), F32),
            pltpu.VMEM((heads, EDGE, H2), F32),
        ],
        flops=2 * group * full * width, smem=2, wide=reach > group)


def attend_back_own(segs, qcode, kcode, kv, lse, qc, q2, dc, d2, dot_s, dqa, marks):
    heads, group, _ = qc.shape
    width = kv.shape[1] // 2
    nq = group // TILE
    H3, H2 = 3 * HEAD_DIM, 2 * HEAD_DIM
    return call(
        functools.partial(back_own_kernel, heads), "back_own",
        [arr((group, width)), arr((group, 2 * width))],
        [segs, qcode, kcode, kv, lse, qc, q2, dc, d2, dot_s, dqa],
        [
            pltpu.VMEM((heads, group, H3), BF),
            pltpu.VMEM((heads, group, H3), BF),
            pltpu.VMEM((heads, nq, H2, TILE), BF),
            pltpu.VMEM((group, 128), F32),
            pltpu.VMEM((heads, nq, H2, TILE), F32),
            pltpu.VMEM((heads, TILE, H2), F32),
            pltpu.VMEM((heads, TILE, H2), F32),
        ],
        flops=10 * group * group * width, marks=marks)


def weights_kernel(full, splits, idx, *refs):
    count = max([p[0] for p in full]) + 1
    weights, (uh, ul, oh, ol, u32, o32) = refs[:count], refs[count:count + 6]
    got = weights
    owners = len(full)
    rows = u32.shape[0] // owners
    for i, (n, lead) in enumerate(full):
        row = at(idx[0, splits + i] * rows, rows)
        u32[row, :] = got[n][lead]
        o32[row, :] = got[n][2]
    uh[...], ul[...] = split(u32[...])
    oh[...], ol[...] = split(o32[...])


def act_kernel(splits, whole, first, place, idx, *refs):
    got, (gh, gl, dh, dl, act_ref) = refs[:-5], refs[-5:]
    tokens = got[0].shape[0]
    down = got[splits:]
    unit = down[0].shape[0]
    blocks = dh.shape[0] // unit
    for r in range(splits):
        row = at(idx[0, r] * tokens, tokens, 16)
        gh[row, :], gl[row, :] = split(got[r][...])
    for i in range(blocks):
        if i < whole:
            row = at(idx[0, first + i] * unit, unit, 16)
            dh[row, :], dl[row, :] = split(down[i][...])
            continue
        size = unit // 4
        for z in range(4):
            quarter = idx[0, place] ^ (0, 3, 1, 2)[z]
            row = at(idx[0, first + i] * unit + quarter * size, size, 16)
            dh[row, :], dl[row, :] = split(down[whole + 4 * (i - whole) + z][...])
    step = gh.shape[0] // 2

    def rows_of(i, _):
        row = at(i * step, step, 16)
        act_ref[row, :] = mm3((gh[row, :], gl[row, :]), (dh[...], dl[...]), NT)
        return 0

    lax.fori_loop(0, 2, rows_of, 0)


def feed_kernel(splits, idx, small, base, *refs):
    (oh, ol, uh, ul, act, keep, send, mine, inv_ref, ah, al, ph, plo, mh, ml, vec, b32, x2, g32, r32) = (
        refs[splits:splits + 20])
    att = refs[:splits]
    tokens = keep.shape[1]
    group = b32.shape[0]
    part = att[0].shape[1] // 2
    gain, shift = small[6:7, :], small[7:8, :]
    up_bias = small[pl.ds(8 + idx[0, 0], 1), :]
    vec[...] = jnp.zeros_like(vec)
    step = group // 2

    def rows_of(i, _):
        row = at(i * step, step, 16)
        middle = base[row, :] + small[2:3, :]
        for s in range(splits):
            wrow = at(idx[0, s] * part, part, 16)
            piece = jnp.where(i == 0, att[s][:, :part], att[s][:, part:])
            middle = middle + mm3(split(piece), (oh[wrow, :], ol[wrow, :]))
        b32[row, :] = middle
        xhat, inverse = norm(middle)
        x2[row, :] = xhat
        g32[row, :] = jnp.broadcast_to(inverse, g32[row, :].shape)
        pair = split(xhat * gain + shift)
        mh[row, :], ml[row, :] = pair
        pre = mm3(pair, (uh[...], ul[...])) + up_bias
        square = pre * pre
        curve = jnp.tanh(SQRT_2_PI * (pre + CUBIC * square * pre))
        half = 0.5 * (1.0 + curve)
        ah[row, :], al[row, :] = split(pre * half)
        slope = half + 0.5 * pre * (1.0 - curve * curve) * SQRT_2_PI * (1.0 + 3.0 * CUBIC * square)
        grad = act[row, :] * slope
        pair = split(grad)
        ph[row, :], plo[row, :] = pair
        back = mm3(pair, (uh[...], ul[...]), NT)
        vec[0:1, :] += jnp.sum(grad, axis=0, keepdims=True)
        vec[1:2, :] += jnp.sum(back * xhat, axis=0, keepdims=True)
        vec[2:3, :] += jnp.sum(back, axis=0, keepdims=True)
        r32[row, :] = back
        return 0

    lax.fori_loop(0, 2, rows_of, 0)

    def pairs_of(h, _):
        keep[h] = r32[at(idx[0, 2 * h] * tokens, tokens), :]
        send[h] = r32[at(idx[0, 2 * h + 1] * tokens, tokens), :]
        return 0

    lax.fori_loop(0, splits // 2, pairs_of, 0)
    row = at(idx[0, 0] * tokens, tokens)
    mine[0] = b32[row, :]
    mine[1] = x2[row, :]
    inv_ref[...] = g32[row, :]


def feed_grads_kernel(splits, first, down_rows, up_rows, idx, ah, al, ph, plo, mh, ml, gh, gl, dh, dl,
                      keep, send, *refs):
    outs, r32 = refs[:-1], refs[-1]
    downs, ups = outs[:len(outs) // 2], outs[len(outs) // 2:]
    tokens = keep.shape[1]
    step = r32.shape[0] // 2

    third = r32.shape[0] // 3

    def left(a, b):
        def rows_of(i, _):
            lane = at(i * third, third, 128)
            r32[at(i * third, third), :] = mm3((a[0][:, lane], a[1][:, lane]), (b[0][...], b[1][...]), TN)
            return 0

        lax.fori_loop(0, 3, rows_of, 0)

    def deal(targets, rows, place):
        for target in targets:
            def one(c, _, target=target, place=place):
                target[c] = r32[at(idx[0, place + c], rows), :]
                return 0

            lax.fori_loop(0, target.shape[0], one, 0)
            place += target.shape[0]
        return place

    left((ah, al), (gh, gl))
    place = deal(downs, down_rows, first)
    left((mh, ml), (ph, plo))
    deal(ups, up_rows, place)

    def rows_of(i, _):
        row = at(i * step, step, 16)
        r32[row, :] = mm3((ah[row, :], al[row, :]), (dh[...], dl[...]))
        return 0

    lax.fori_loop(0, 2, rows_of, 0)

    def pairs_of(h, _):
        keep[h] = r32[at(idx[0, 2 * h] * tokens, tokens), :]
        send[h] = r32[at(idx[0, 2 * h + 1] * tokens, tokens), :]
        return 0

    lax.fori_loop(0, splits // 2, pairs_of, 0)


def middle_kernel(small, keep, core, far, og, mine, inv, mg_ref, vec_ref):
    grad = keep[0] + core[0] + far[...]
    out = og[...] + norm_back(grad, small[6:7, :], mine[1], inv[:, :1])
    mg_ref[...] = out
    vec_ref[...] = jnp.zeros_like(vec_ref)
    vec_ref[0:1, :] = jnp.sum(out, axis=0, keepdims=True)
    vec_ref[1:2, :] = jnp.sum(og[...], axis=0, keepdims=True)


def last_grads_kernel(splits, first, edge, rows, idx, small, dq, dkv, back, base, att, vec1, vec2, gh, gl, wh, wl,
                      keep, send, *refs):
    tails, (qh, ql, xhat, r32, o32, s32, n32, vec) = refs[:-8], refs[-8:]
    part = dq.shape[1]
    width = xhat.shape[1]
    tokens = keep.shape[1]
    u = idx[0, 0]
    s32[:, :part] = dq[...]
    s32[:, part:] = dkv[...]
    s32[at(idx[0, edge], back.shape[0]), part:] += back[...]
    qkv = s32[...]
    qh[...], ql[...] = split(qkv)
    sums = jnp.sum(qkv, axis=0, keepdims=True)
    xhat[...], _ = norm(base[...])
    vec[...] = jnp.zeros_like(vec)
    step = n32.shape[0] // 2

    def rows_of(i, _):
        row = at(i * step, step, 16)
        grad = mm3((qh[row, :], ql[row, :]), (wh[...], wl[...]), NT)
        n32[row, :] = grad
        vec[4:5, :] += jnp.sum(grad * xhat[row, :], axis=0, keepdims=True)
        vec[5:6, :] += jnp.sum(grad, axis=0, keepdims=True)
        return 0

    lax.fori_loop(0, 2, rows_of, 0)

    def pairs_of(h, _):
        keep[h] = n32[at(idx[0, 2 * h] * tokens, tokens), :]
        send[h] = n32[at(idx[0, 2 * h + 1] * tokens, tokens), :]
        return 0

    lax.fori_loop(0, splits // 2, pairs_of, 0)
    step = width // 3

    def lanes_of(i, _):
        lane = at(i * step, step, 128)
        pair = split(xhat[:, lane] * small[4:5, lane] + small[5:6, lane])
        r32[lane, :] = mm3(pair, (qh[...], ql[...]), TN)
        return 0

    lax.fori_loop(0, 3, lanes_of, 0)
    o32[...] = mm3(split(att[...]), (gh[...], gl[...]), TN)
    for i in range(splits):

        @pl.when(u == i)
        def _():
            vec[0:1, i * part:(i + 1) * part] = sums[:, :part]
            vec[1:2, i * part:(i + 1) * part] = sums[:, 2 * part:]

    vec[2:4, :] = vec2[0:2, :]
    vec[6:8, :] = vec1[1:3, :]
    vec[pl.ds(8 + u, 1), :] = vec1[0:1, :]
    wide = r32.shape[1]
    outs = width // 128
    vecs = outs * EXTRA // rows
    lane_blocks = -(-wide // 128)
    spare = lane_blocks * 128 - wide
    near = 2 * lane_blocks
    total = sum(t.shape[0] for t in tails)
    spot = 0
    for t in tails:
        def one(c, _, t=t, spot=spot):
            for j in range(splits):
                row = at(idx[0, first + (spot + c) * splits + j], rows)
                start = j * lane_blocks + (outs + vecs if j >= 2 else 0)
                for k in range(lane_blocks - 1):
                    t[c, start + k] = r32[row, k * 128:(k + 1) * 128]
                k = lane_blocks - 1
                t[c, start + k, :, :128 - spare] = r32[row, k * 128:]
                t[c, start + k, :, 128 - spare:] = jnp.zeros((rows, spare), F32)
            row = at(idx[0, first + total * splits + spot + c], rows)
            for k in range(outs):
                t[c, near + k] = o32[row, k * 128:(k + 1) * 128]
            for k in range(outs * EXTRA // 8):
                block, low = divmod(8 * k, rows)
                lane, high = divmod(8 * k, EXTRA)
                t[c, near + outs + block, low:low + 8, :] = vec[high:high + 8, lane * 128:(lane + 1) * 128]
            return 0

        lax.fori_loop(0, t.shape[0], one, 0)
        spot += t.shape[0]


def hidden_kernel(idx, small, base, keep, core, far, mg, out):
    tokens = mg.shape[0]
    xhat, inverse = norm(base[at(idx[0, 0] * tokens, tokens), :])
    out[...] = mg[...] + norm_back(keep[0] + core[0] + far[...], small[4:5, :], xhat, inverse)


def fold_kernel(count, *refs):
    keeps, gots, outs = refs[:count], refs[count:2 * count], refs[2 * count:]
    for i in range(count):
        stay, go = outs[2 * i:2 * i + 2]
        half = stay.shape[0]
        stay[...] = keeps[i][:half] + gots[i][:half]
        go[...] = keeps[i][half:] + gots[i][half:]


def fold(keeps, gots, marks=()):
    outs = []
    for keep in keeps:
        outs += [arr((keep.shape[0] // 2,) + keep.shape[1:])] * 2
    got = call(functools.partial(fold_kernel, len(keeps)), "fold", outs, [*keeps, *gots], smem=0, marks=marks)
    return got[::2], got[1::2]


def message_kernel(near, stop, vecs, part, far, out):
    blocks = near // 2
    out[:blocks] = part[blocks:near]
    out[blocks:blocks + vecs] = part[stop:stop + vecs] + far[:vecs]
    out[blocks + vecs:] = far[vecs + blocks:]


def place_kernel(splits, first, rows, idx, *refs):
    pieces, (gq, gk, gv, go) = refs[:-4], refs[-4:]
    part = gq.shape[1] // splits
    for z, piece in enumerate(pieces):
        row = at(idx[0, first + z] * rows, rows)
        count = gq.shape[1] // 128
        for k in range(count):
            go[row, k * 128:(k + 1) * 128] = piece[5 * splits + k]
        for i in range(splits):
            whole = jnp.concatenate([piece[5 * idx[0, i] + k] for k in range(5)], axis=1)
            for n, out in enumerate((gq, gk, gv)):
                out[row, i * part:(i + 1) * part] = whole[:, n * part:(n + 1) * part]


def place_feed_kernel(splits, blocks, unit, first, idx, *refs):
    pieces, (gd, gu) = refs[:-2], refs[-2:]
    downs, ups = pieces[:len(pieces) // 2], pieces[len(pieces) // 2:]
    for z, (down, up) in enumerate(zip(downs, ups)):
        gd[at(idx[0, first + z] * down.shape[0], down.shape[0]), :] = down[...]
        rows = up.shape[1]
        row = at(idx[0, first + z] * rows, rows)
        for i in range(splits):
            for n in range(blocks):
                start = (n * splits + i) * unit
                gu[row, start:start + unit] = up[idx[0, i], :, n * unit:(n + 1) * unit]


def swap(value, axis, mask):
    count = lax.axis_size(axis)
    return lax.ppermute(value, axis, [(i, i ^ mask) for i in range(count)])


def across(value):
    return swap(value, "ulys", 2)


def beside(value):
    return swap(value, "ulys", 1)


def over(value):
    return swap(value, "blk", 1)


def gather_splits(value):
    far = across(value)
    return [value, beside(value), far, beside(far)]


def collect(value):
    near = swap(value, "dp", 3)
    return [value, near, swap(value, "dp", 1), swap(near, "dp", 1)]


def halo_moves(group, reach, blocks):
    moves = []
    shift = 1
    while reach > 0 and shift < blocks:
        rows = min(group, reach)
        moves.append((rows, True, [(i, i - shift) for i in range(shift, blocks)]))
        moves.append((rows, False, [(i, i + shift) for i in range(blocks - shift)]))
        reach -= rows
        shift += 1
    return moves


def halo_get(value, reach, axis=0):
    blocks, group = lax.axis_size("blk"), value.shape[axis]
    parts = []
    for rows, right, moves in halo_moves(group, reach, blocks):
        start = 0 if right else group - rows
        parts.append(lax.ppermute(lax.slice_in_dim(value, start, start + rows, axis=axis), "blk", moves))
    return jnp.concatenate(parts, axis=axis)


def halo_add(value, halo, reach):
    blocks, group = lax.axis_size("blk"), value.shape[0]
    start = 0
    for rows, right, moves in halo_moves(group, reach, blocks):
        back = lax.ppermute(halo[start:start + rows], "blk", [(j, i) for i, j in moves])
        start += rows
        room = group - rows
        value = value + jnp.pad(back, ((0, room), (0, 0)) if right else ((room, 0), (0, 0)))
    return value


def local(
    hidden,
    time_embed,
    segment_ids,
    key_valid,
    out_grad,
    w_query,
    b_query,
    w_key,
    w_value,
    b_value,
    w_out,
    b_out,
    w_up,
    b_up,
    w_down,
    b_down,
    pre_gain,
    pre_shift,
    mlp_gain,
    mlp_shift,
):
    blocks, splits = lax.axis_size("blk"), lax.axis_size("ulys")
    b, u, d = (lax.axis_index(name) for name in ("blk", "ulys", "dp"))
    both = ("blk", "ulys")
    owners = blocks * splits
    tokens, width = hidden.shape
    group = tokens * splits
    part = width // splits
    rows = w_query.shape[0]
    unit = w_down.shape[0]
    units = unit * owners
    share = units // splits
    reach = group * blocks // 4
    fast = blocks == 2 and splits == 4 and lax.axis_size("dp") == 4 and reach <= group and group == width

    if fast:
        f1, f3 = (d ^ (d >> 1)) & 1, d >> 1
        quarters = [2 * (f1 ^ s) + (f3 ^ t) for s in range(2) for t in range(2)]
        owner_list = [(b ^ x) * splits + (u ^ r) for x in range(2) for r in range(4)]
        block_list = [b, b ^ 1]
        edge_row = jnp.where(b == 0, group - reach, 0)
        down_rows, up_rows, tail_rows = unit // 4, rows // 4, rows // 4
        down_table = [(b ^ x) * unit + q * down_rows for x in range(2) for q in quarters]
        up_table = [
            ((b ^ x) * splits + (u ^ r)) * rows + q * up_rows for q in quarters for x in range(2) for r in range(4)
        ]
        tail_table = [
            ((b ^ x) * splits + (u ^ r)) * rows + q * tail_rows for x in range(2) for q in quarters for r in range(4)
        ] + [(b ^ x) * rows + q * tail_rows for x in range(2) for q in quarters]
        chunks = 8
    else:
        quarters = []
        owner_list = list(range(owners))
        block_list = list(range(blocks))
        edge_row = 0
        down_rows, up_rows, tail_rows = unit, rows, rows
        down_table = [i * unit for i in range(blocks)]
        up_table = [i * rows for i in range(owners)]
        tail_table = up_table + [i * rows for i in range(blocks)]
        chunks = blocks
    entries, spots = [], []
    for values in (
        [u ^ r for r in range(splits)], owner_list, block_list, [d], [edge_row], down_table + up_table, tail_table,
        quarters,
    ):
        spots.append(len(entries))
        entries += values
    _, _, at_block, at_d, at_edge, at_feed, at_tail, at_quarter = spots
    idx = jnp.stack([jnp.asarray(v, jnp.int32) for v in entries]).reshape(1, -1)

    segments = segment_ids[0] + 1
    codes = jnp.stack([segments, jnp.where(key_valid[0] == 1, segments, 0)]).astype(F32)
    small = jnp.stack([b_query, b_value, b_out, b_down, pre_gain, pre_shift, mlp_gain, mlp_shift])
    small = lax.dynamic_update_slice(jnp.zeros((EXTRA, width), F32), small, (0, (b * splits + u) * rows))
    small = lax.dynamic_update_slice(small, b_up[None], (8 + u, b * unit))
    if fast:
        small = lax.dynamic_update_slice(small, codes, (12, 0))
        other = over(small)
        small = small + other
        halo_codes = jnp.where(b == 0, other[12:14, :reach], other[12:14, group - reach:group])
    else:
        small = lax.psum(small, "blk")
        halo_codes = halo_get(codes, reach, axis=1)
    tiles = codes[0].reshape(-1, TILE)
    edges = halo_codes[0].reshape(-1, EDGE)
    bounds = jnp.concatenate(
        [
            jnp.stack([tiles[:, 0], tiles[:, -1]], axis=1).reshape(-1),
            jnp.stack([jnp.min(jnp.where(edges == 0, 1e6, edges), axis=1), jnp.max(edges, axis=1)], axis=1).reshape(-1),
        ]
    ).astype(jnp.int32).reshape(1, -1)
    def make_base(marks):
        return call(
            base_kernel, "base", [arr((tokens + EXTRA, width))], [hidden, time_embed, small], smem=0, marks=marks)[0]

    if fast:
        tables = [idx, bounds, codes, halo_codes, small]
        near, far, *tables = call(
            pack_qkv_kernel, "pack_qkv",
            [arr((2, rows, 3 * part))] * 2 + [arr(x.shape, x.dtype) for x in tables],
            [*tables, w_query, w_key, w_value], smem=2)
        idx, bounds, codes, halo_codes, small = tables
        pieces = [(i, i % 2) for i in range(8)]
        far = across(far)
        near_over = over(near)
        base = make_base([far, near_over])
        far_base = across(base)
        qkv_arrays = [near, beside(near), far, beside(far)]
        near = near_over
        far = over(far)
        qkv_arrays += [near, beside(near), far, beside(far)]
        base_all = [base, beside(base), far_base, beside(far_base)]
        near2, far2, down_quarter = call(
            functools.partial(pack_feed_kernel, splits, blocks, at_d), "pack_feed",
            [arr((3, rows, share))] * 2 + [arr((unit // 4, width))],
            [idx, w_up, w_out, w_down], marks=[far])
        down_quarter = over(down_quarter)
        far2 = across(far2)
        feed_arrays = [near2, beside(near2), far2, beside(far2)]
        near2 = over(near2)
        feed_arrays += [near2, beside(near2)]
        whole = 1
    else:
        cut = jnp.stack([w_query, w_key, w_value], axis=1).reshape(rows, 3, splits, part)
        cut = cut.transpose(2, 0, 1, 3).reshape(splits, rows, 3 * part)
        cut = jnp.broadcast_to(cut[None], (blocks,) + cut.shape).reshape(owners, rows, 3 * part)
        got = lax.all_to_all(cut, both, 0, 0, tiled=True)
        qkv_arrays = [got[i:i + 1] for i in range(owners)]
        cut = w_up.reshape(rows, blocks, splits, unit).transpose(2, 0, 1, 3).reshape(splits, rows, share)
        cut = jnp.broadcast_to(cut[None], (blocks,) + cut.shape).reshape(owners, rows, share)
        got = lax.all_to_all(cut, both, 0, 0, tiled=True)
        outs = lax.all_gather(w_out, both, axis=0, tiled=False)
        feed_arrays = [jnp.stack([got[i], got[i], outs[i]]) for i in range(owners)]
        pieces = [(i, 0) for i in range(owners)]
        whole = blocks
        base = make_base([])
        base_all = gather_splits(base)
        gathered = lax.all_gather(w_down, "blk", axis=0, tiled=False)
        down = [gathered[i] for i in range(blocks)]

    query_codes, key_codes, edge_codes = codes, codes, halo_codes
    query, key_value, edge_kv, base, small, qkv_hi, qkv_lo, own_grad = call(
        functools.partial(qkv_kernel, pieces, splits, at_edge), "qkv",
        [arr((group, part)), arr((group, 2 * part)), arr((reach if fast else 8, 2 * part)), arr((group, width)),
         arr((EXTRA, width)), arr((width, 3 * part), BF), arr((width, 3 * part), BF), arr((tokens, width))],
        [idx, out_grad, *base_all, *qkv_arrays],
        [pltpu.VMEM((width, 3 * part), F32), pltpu.VMEM((group, width), BF), pltpu.VMEM((group, width), BF)],
        flops=2 * group * width * 3 * part)
    halo = over(edge_kv) if fast else halo_get(key_value, reach)
    state = attend_own(bounds, query_codes, key_codes, query, key_value)
    grads = gather_splits(own_grad)
    if fast:
        down = [w_down, down_quarter] + [swap(down_quarter, "dp", mask) for mask in (3, 1, 2)]
        attended, attended_wide, lse, far2 = attend_edge(bounds, query_codes, edge_codes, halo, state, (far2,), [*down[2:], grads[2], near2])
        far2 = over(far2)
        feed_arrays += [far2, beside(far2)]
    else:
        attended, attended_wide, lse = attend_edge(bounds, query_codes, edge_codes, halo, state)
    attended_all = gather_splits(attended_wide)
    og_hi, og_lo, down_hi, down_lo, act_grad = call(
        functools.partial(act_kernel, splits, whole, at_block, at_d), "act",
        [arr((group, width), BF)] * 2 + [arr((share, width), BF)] * 2 + [arr((group, share))],
        [idx, *grads, *down],
        flops=2 * group * width * share, marks=[attended_all[2]])
    up_hi, up_lo, out_hi, out_lo = call(
        functools.partial(weights_kernel, pieces, splits), "weights",
        [arr((width, share), BF)] * 2 + [arr((width, width), BF)] * 2,
        [idx, *feed_arrays],
        [pltpu.VMEM((width, share), F32), pltpu.VMEM((width, width), F32)], marks=[act_grad])

    pair = [arr((group, share), BF)] * 2
    keep, send, mine, inverse2, act_hi, act_lo, pre_hi, pre_lo, in_hi, in_lo, vec_feed = call(
        functools.partial(feed_kernel, splits), "feed",
        [arr((2, tokens, width))] * 2 + [arr((2, tokens, width)), arr((tokens, 128))] + pair * 2
        + [arr((group, width), BF)] * 2 + [arr((8, width))],
        [idx, small, base, *attended_all, out_hi, out_lo, up_hi, up_lo, act_grad],
        [pltpu.VMEM((group, width), F32), pltpu.VMEM((group, width), F32), pltpu.VMEM((group, 128), F32),
         pltpu.VMEM((group, width), F32)],
        flops=2 * group * width * (width + 2 * share))
    core = beside(send)
    near_sum = keep[1] + core[1]
    far_sum = across(near_sum)

    if fast:
        feed_outs = [arr((4, down_rows, width))] * 2 + [arr((8 * splits // 2, up_rows, share))] * 2
    else:
        feed_outs = [arr((blocks, down_rows, width)), arr((owners, up_rows, share))]
    keep_out, send_out, *feed_grads = call(
        functools.partial(feed_grads_kernel, splits, at_feed, down_rows, up_rows), "feed_grads",
        [arr((2, tokens, width))] * 2 + feed_outs,
        [idx, act_hi, act_lo, pre_hi, pre_lo, in_hi, in_lo, og_hi, og_lo, down_hi, down_lo],
        [pltpu.VMEM((group, width), F32)],
        flops=6 * group * width * share, marks=[near_sum])
    if fast:
        down_keep, down_send, up_keep, up_send = feed_grads
        down_got = over(down_send)
        up_got = swap(up_send, "dp", 1)

    middle_grad, vec_middle = call(
        middle_kernel, "middle",
        [arr((tokens, width)), arr((8, width))],
        [small, keep, core, far_sum, out_grad, mine, inverse2], smem=0, marks=[keep_out])
    middle_all = gather_splits(middle_grad)

    halo_grad, q2, dc, d2, dots, dq_part, mg_hi, mg_lo = attend_back_edge(
        idx, bounds, query_codes, edge_codes, query, halo, attended, lse, state[0], out_hi, out_lo, middle_all)
    if fast:
        returned = over(halo_grad)
        (down_keep, up_keep), (down_send, up_send) = fold((down_keep, up_keep), (down_got, up_got), [halo_grad])
        down_got = swap(down_send, "dp", 1)
        up_got = swap(up_send, "dp", 3)
        own_marks = [down_keep]
    else:
        own_marks = []
    query_grad, kv_grad = attend_back_own(
        bounds, query_codes, key_codes, key_value, lse, state[0], q2, dc, d2, dots, dq_part, own_marks)
    if not fast:
        kv_grad = halo_add(kv_grad, halo_grad, reach)
        returned = jnp.zeros((8, 2 * part), F32)

    core_out = beside(send_out)
    far_out = across(keep_out[1] + core_out[1])
    lane_blocks = -(-3 * part // 128)
    outs, vecs = width // 128, width // 128 * EXTRA // tail_rows
    total_blocks = splits * lane_blocks + outs + vecs
    tail_outs = [arr((2, total_blocks, tail_rows, 128))] * 4 if fast else [arr((blocks, total_blocks, tail_rows, 128))]
    keep_in, send_in, *tail = call(
        functools.partial(last_grads_kernel, splits, at_tail, at_edge, tail_rows), "last_grads",
        [arr((2, tokens, width))] * 2 + tail_outs,
        [idx, small, query_grad, kv_grad, returned, base, attended, vec_feed, vec_middle, mg_hi, mg_lo, qkv_hi, qkv_lo],
        [pltpu.VMEM((group, 3 * part), BF), pltpu.VMEM((group, 3 * part), BF), pltpu.VMEM((group, width), F32),
         pltpu.VMEM((width, 3 * part), F32), pltpu.VMEM((part, width), F32), pltpu.VMEM((group, 3 * part), F32),
         pltpu.VMEM((group, width), F32), pltpu.VMEM((EXTRA, width), F32)],
        flops=2 * group * width * 7 * part, marks=[far_out])
    to_owner = [(i * splits + j, j * blocks + i) for i in range(blocks) for j in range(splits)]
    near = 2 * lane_blocks
    if fast:
        tail_near, tail_far, send_near, send_far = tail
        got_far = over(send_far)
        got_near = over(send_near)
        core_in = beside(send_in)
        far_in = across(keep_in[1] + core_in[1])

        (down_keep, up_keep), (down_send, up_send) = fold((down_keep, up_keep), (down_got, up_got), [keep_in])
        down_got = swap(down_send, "dp", 3)
        up_got = over(up_send)
        tail_got = swap(tail_far + got_far, "dp", 1)
        tail_near = tail_near + got_near
        part_down = (down_keep + down_got)[0]
        part_up = up_keep + up_got
        far_up = across(part_up[2:])
        core_up = beside(jnp.stack([part_up[1], far_up[1]]))
        part_up = jnp.stack([part_up[0], core_up[0], far_up[0], core_up[1]])
        all_down = collect(part_down)
        all_up = collect(part_up)
        (tail_keep,), (tail_send,) = fold((tail_near,), (tail_got,), [*all_down, far_in])
        part_tail = (tail_keep + swap(tail_send, "dp", 3))[0]

        far_tail = across(part_tail[near + outs:])
        message, = call(
            functools.partial(message_kernel, near, near + outs, vecs), "message", [arr(far_tail.shape)],
            [part_tail, far_tail], smem=0, marks=all_up)
        core_tail = beside(message)
        vec = part_tail[near + outs:near + outs + vecs] + far_tail[:vecs] + core_tail[lane_blocks:lane_blocks + vecs]
        owned = lax.ppermute(part_tail[near:near + outs], both, to_owner)
        part_tail = jnp.concatenate([
            part_tail[:lane_blocks], core_tail[:lane_blocks], far_tail[vecs:vecs + lane_blocks],
            core_tail[lane_blocks + vecs:], owned])
        all_tail = collect(part_tail)
        total_down, total_up = call(
            functools.partial(place_feed_kernel, splits, blocks, unit, at_quarter), "place_feed",
            [arr((unit, width)), arr((rows, units))],
            [idx, *all_down, *all_up])
        total_query, total_key, total_value, total_out = call(
            functools.partial(place_kernel, splits, at_quarter, tail_rows), "place",
            [arr((rows, width))] * 4,
            [idx, *all_tail])
    else:
        core_in = beside(send_in)
        far_in = across(keep_in[1] + core_in[1])
        total_down, total_up, tail = [
            lax.psum(lax.psum_scatter(g.reshape((blocks, -1) + g.shape[1:]), "blk", scatter_dimension=0, tiled=False), "dp")
            for g in (*feed_grads, *tail)
        ]
        total_down = total_down.reshape(unit, width)
        total_up = lax.all_to_all(total_up, "ulys", 0, 0, tiled=True)
        total_up = total_up.reshape(splits, rows, blocks, unit).transpose(1, 2, 0, 3).reshape(rows, units)
        tail = tail[0]
        total_out = lax.ppermute(tail[near:near + outs], both, to_owner).transpose(1, 0, 2).reshape(rows, width)
        vec = lax.psum(tail[near + outs:near + outs + vecs], "ulys")
        got = jnp.concatenate([tail[:near], tail[near + outs + vecs:]]).reshape(splits, lane_blocks, rows, 128)
        got = lax.all_to_all(got, "ulys", 0, 0, tiled=True).transpose(2, 0, 1, 3).reshape(rows, splits, lane_blocks * 128)
        total_query, total_key, total_value = (
            got[:, :, i * part:(i + 1) * part].reshape(rows, width) for i in range(3)
        )
    (hidden_grad,) = call(
        hidden_kernel, "hidden",
        [arr((tokens, width))],
        [idx, small, base, keep_in, core_in, far_in, middle_grad])

    output = mine[0] + small[3:4] + keep_out[0] + core_out[0] + far_out

    vec = vec.reshape(outs, EXTRA, 128).transpose(1, 0, 2).reshape(EXTRA, width)
    vector = lax.dynamic_slice(vec, (0, (b * splits + u) * rows), (8, rows))
    up_vector = lax.dynamic_slice(vec, (8 + u, b * unit), (1, unit))[0]
    return (
        output,
        hidden_grad,
        total_query,
        vector[0],
        total_key,
        total_value,
        vector[1],
        total_out,
        vector[2],
        total_up,
        up_vector,
        total_down,
        vector[3],
        vector[4],
        vector[5],
        vector[6],
        vector[7],
    )


def solution(mesh):
    tokens = P(("dp", "blk", "ulys"), None)
    matrix = P(("blk", "ulys"), None)
    vector = P(("blk", "ulys"))
    return jax.shard_map(
        local,
        mesh=mesh,
        in_specs=(
            tokens,
            P("dp", None),
            P("dp", "blk"),
            P("dp", "blk"),
            tokens,
            matrix,
            vector,
            matrix,
            matrix,
            vector,
            matrix,
            vector,
            matrix,
            vector,
            matrix,
            vector,
            vector,
            vector,
            vector,
            vector,
        ),
        out_specs=(
            tokens,
            tokens,
            matrix,
            vector,
            matrix,
            matrix,
            vector,
            matrix,
            vector,
            matrix,
            vector,
            matrix,
            vector,
            vector,
            vector,
            vector,
            vector,
        ),
        check_vma=False,
    )
```

```python
import functools
import math

import jax
import jax.numpy as jnp
from jax import lax
from jax.experimental import pallas as pl
from jax.experimental.pallas import tpu as pltpu
from jax.sharding import PartitionSpec as P

HEAD_DIM = 64
FLOOR = -1e30
SQRT_2_PI = 0.7978845608028654
CUBIC = 0.044715
EXTRA = 16
TILE = 256
EDGE = 128
BF = jnp.bfloat16
F32 = jnp.float32
NN = (((1,), (0,)), ((), ()))
NT = (((1,), (1,)), ((), ()))
TN = (((0,), (0,)), ((), ()))
VM = pl.BlockSpec(memory_space=pltpu.VMEM)
SM = pl.BlockSpec(memory_space=pltpu.SMEM)
LIMITS = {"attend_own": 10, "attend_edge": 10, "back_edge": 12, "back_own": 12, "act": 14, "weights": 16, "feed_grads": 12, "place": 8, "hidden": 6, "middle": 6, "last_grads": 16, "fold": 10, "base": 6, "pack_qkv": 8, "pack_feed": 10}


def split(x):
    hi = x.astype(BF)
    return hi, (x - hi.astype(F32)).astype(BF)


def mm(a, b, dims=NN):
    return lax.dot_general(a, b, dims, preferred_element_type=F32)


def mm3(a, b, dims=NN):
    return mm(a[0], b[0], dims) + (mm(a[0], b[1], dims) + mm(a[1], b[0], dims))


def at(start, size, step=8):
    return pl.ds(pl.multiple_of(start, step), size)


def call(kernel, name, outs, ins, scratch=(), flops=0, smem=1, limit=16, wide=False, marks=()):
    inner, count, ins = kernel, len(ins), list(ins) + list(marks)

    def kernel(*refs):
        return inner(*refs[:count], *refs[len(ins):])

    size = sum(math.prod(x.shape) * x.dtype.itemsize for x in list(outs) + list(ins[smem:count]))
    return pl.pallas_call(
        kernel,
        out_shape=tuple(outs),
        in_specs=[SM] * smem + [VM] * (count - smem) + [pl.BlockSpec(memory_space=pl.ANY)] * len(marks),
        out_specs=tuple(SM if x.dtype == jnp.int32 else VM for x in outs),
        scratch_shapes=list(scratch),
        compiler_params=pltpu.CompilerParams(vmem_limit_bytes=(48 if wide else LIMITS.get(name, limit)) << 20),
        cost_estimate=pl.CostEstimate(flops=1, bytes_accessed=1, transcendentals=0),
        name=name,
    )(*ins)


def arr(shape, dtype=F32):
    return jax.ShapeDtypeStruct(tuple(shape), dtype)


def norm(x):
    centred = x - jnp.mean(x, axis=-1, keepdims=True)
    inverse = lax.rsqrt(jnp.mean(centred * centred, axis=-1, keepdims=True) + 1e-05)
    return centred * inverse, inverse


def norm_back(grad, gain, xhat, inverse):
    scaled = grad * gain
    mean = jnp.mean(scaled, axis=-1, keepdims=True)
    lean = jnp.mean(scaled * xhat, axis=-1, keepdims=True)
    return (scaled - mean - xhat * lean) * inverse


def pick(index, choices):
    value = choices[0]
    for i in range(1, len(choices)):
        value = jnp.where(index == i, choices[i], value)
    return value


def first_kernel(count, numbers, *refs):
    for source, target in zip((numbers,) + refs[:count], refs[count:]):
        if target.dtype == jnp.int32:
            for i in range(target.shape[1]):
                target[0, i] = source[0, i]
        else:
            target[...] = source[...]


def pack_qkv_kernel(idx, bounds, codes, halo_codes, small, wq, wk, wv, near, far, *outs):
    first_kernel(4, idx, bounds, codes, halo_codes, small, *outs)
    part = near.shape[2] // 3
    splits = wq.shape[1] // part
    for r in range(splits):
        target, k = (near, r) if r < 2 else (far, r - 2)
        for u in range(splits):

            @pl.when(idx[0, r] == u)
            def _():
                for i, w in enumerate((wq, wk, wv)):
                    target[k, :, i * part:(i + 1) * part] = w[:, u * part:(u + 1) * part]


def pack_feed_kernel(splits, blocks, place, idx, wup, wout, wdown, near, far, down_quarter):
    unit = near.shape[2] // blocks
    for r in range(splits):
        target, k = (near, r) if r < 2 else (far, r - 2)
        for u in range(splits):

            @pl.when(idx[0, r] == u)
            def _():
                for b in range(blocks):
                    lane = (b * splits + u) * unit
                    target[k, :, b * unit:(b + 1) * unit] = wup[:, lane:lane + unit]
    near[2] = wout[...]
    far[2] = wout[...]
    size = down_quarter.shape[0]
    down_quarter[...] = wdown[at(idx[0, place] * size, size), :]


def base_kernel(hidden, embed, small, out):
    tokens = hidden.shape[0]
    out[:tokens, :] = hidden[...] + embed[...]
    out[tokens:, :] = small[...]


def qkv_kernel(pieces, splits, edge, idx, og, *refs):
    base, rest = refs[:splits], refs[splits:]
    count = max(p[0] for p in pieces) + 1
    weights = rest[:count]
    (q_ref, kv_ref, edge_ref, base_ref, small_ref, wh, wl, og_ref, w32, nh, nl) = rest[count:count + 11]
    got = base + weights
    tokens = base[0].shape[0] - EXTRA
    part = q_ref.shape[1]
    rows = w32.shape[0] // len(pieces)
    small = None
    for r in range(splits):
        rest = got[r][tokens:, :]
        small = rest if small is None else small + rest
    small_ref[...] = small
    gain, shift = small[4:5], small[5:6]
    for r in range(splits):
        row = at(idx[0, r] * tokens, tokens, 16)
        x = got[r][:tokens, :]
        base_ref[row, :] = x
        xhat, _ = norm(x)
        nh[row, :], nl[row, :] = split(xhat * gain + shift)
    for i, (n, lead) in enumerate(pieces):
        w32[at(idx[0, splits + i] * rows, rows), :] = got[splits + n][lead, :rows, :]
    wh[...], wl[...] = split(w32[...])
    u = idx[0, 0]
    qb = pick(u, [small[0:1, i * part:(i + 1) * part] for i in range(splits)])
    vb = pick(u, [small[1:2, i * part:(i + 1) * part] for i in range(splits)])
    bias = jnp.concatenate([qb, jnp.zeros_like(qb), vb], axis=1)
    step = nh.shape[0] // 2

    def rows_of(i, _):
        row = at(i * step, step, 16)
        out = mm3((nh[row, :], nl[row, :]), (wh[...], wl[...])) + bias
        q_ref[row, :] = out[:, :part]
        kv_ref[row, :] = out[:, part:]
        return 0

    lax.fori_loop(0, 2, rows_of, 0)
    reach = edge_ref.shape[0]
    edge_ref[...] = kv_ref[at(idx[0, edge], reach), :]
    og_ref[...] = og[...]


def span_hits(seg, i, j):
    return (seg[0, 2 * j + 1] >= seg[0, 2 * i]) & (seg[0, 2 * j] <= seg[0, 2 * i + 1])


def prepare(src, width, first, count, size, pairs, flipped):
    heads = width // HEAD_DIM
    for scratch, start in pairs:
        for h in range(heads):
            hi, lo = split(src[:, start + h * HEAD_DIM:start + (h + 1) * HEAD_DIM])
            scratch[h] = jnp.concatenate([hi, lo, hi], axis=1)
    for j in range(count):
        turned = src[j * size:(j + 1) * size, first:first + width].T
        for h in range(heads):
            hi, lo = split(turned[h * HEAD_DIM:(h + 1) * HEAD_DIM])
            flipped[h, j] = jnp.concatenate([hi, lo], axis=0)


def columns(codes, out, size):
    for j in range(out.shape[0] // size):
        row = codes[1:2, j * size:(j + 1) * size]
        out[j * size:(j + 1) * size, :] = jnp.broadcast_to(row, (128, size)).T


def same_row(i, j):
    return (lax.broadcasted_iota(jnp.int32, (TILE, TILE), 0)
            - lax.broadcasted_iota(jnp.int32, (TILE, TILE), 1)) == (i - j) * TILE


def attend_add(heads, qc, keys, flipped, m_s, l_s, acc, i, j, size, allowed):
    qrow = at(i * TILE, TILE, TILE)
    krow = at(j * size, size, size)
    for h in range(heads):
        s = jnp.where(allowed, mm(keys[h, krow, :], qc[h, qrow, :], NT), FLOOR)
        m_old = m_s[h, i]
        m_new = jnp.maximum(m_old, jnp.max(s, axis=0, keepdims=True))
        p = jnp.where(allowed, jnp.exp(s - m_new), 0.0)
        factor = jnp.exp(m_old - m_new)
        m_s[h, i] = m_new
        l_s[h, i] = l_s[h, i] * factor + jnp.sum(p, axis=0, keepdims=True)
        hi, lo = split(p)
        v128 = flipped[h, j]
        acc[h, i] = acc[h, i] * factor + mm(v128, hi) + mm(v128, lo)


def attend_own_kernel(heads, seg_ref, qcode_ref, kcode_ref, q_ref, kv_ref, qc, m_s, l_s, acc, kc, vt, kcol):
    group, width = q_ref.shape
    nq = group // TILE
    for h in range(heads):
        hi, lo = split(q_ref[:, h * HEAD_DIM:(h + 1) * HEAD_DIM] * HEAD_DIM ** -0.5)
        qc[h] = jnp.concatenate([hi, hi, lo], axis=1)
    prepare(kv_ref, width, width, nq, TILE, [(kc, 0)], vt)
    columns(kcode_ref, kcol, TILE)
    m_s[...] = jnp.full_like(m_s, FLOOR)
    l_s[...] = jnp.zeros_like(l_s)
    acc[...] = jnp.zeros_like(acc)

    def per_q(i, _):
        def per_k(j, _):
            @pl.when(span_hits(seg_ref, i, j))
            def _():
                allowed = kcol[at(j * TILE, TILE, TILE), :1] == qcode_ref[:1, at(i * TILE, TILE, TILE)]
                attend_add(heads, qc, kc, vt, m_s, l_s, acc, i, j, TILE, allowed | same_row(i, j))
            return 0

        lax.fori_loop(0, nq, per_k, 0)
        return 0

    lax.fori_loop(0, nq, per_q, 0)


def attend_edge_kernel(heads, extra, seg_ref, qcode_ref, hcode_ref, halo_ref, qc, m_in, l_in, acc_in, *refs):
    out_ref, wide_ref, lse_ref = refs[extra:extra + 3]
    for source, target in zip(refs[:extra], refs[extra + 3:2 * extra + 3]):
        target[...] = source[...]
    kh, vh, hcol, m_s, l_s, acc = refs[2 * extra + 3:]
    group, width = out_ref.shape
    nq, nh = group // TILE, halo_ref.shape[0] // EDGE
    m_s[...] = m_in[...]
    l_s[...] = l_in[...]
    acc[...] = acc_in[...]
    if nh:
        prepare(halo_ref, width, width, nh, EDGE, [(kh, 0)], vh)
        columns(hcode_ref, hcol, EDGE)

    def per_q(i, _):
        qrow = at(i * TILE, TILE, TILE)

        def per_edge(j, _):
            @pl.when(span_hits(seg_ref, i, nq + j))
            def _():
                allowed = hcol[at(j * EDGE, EDGE, EDGE), :1] == qcode_ref[:1, qrow]
                attend_add(heads, qc, kh, vh, m_s, l_s, acc, i, j, EDGE, allowed)
            return 0

        if nh:
            lax.fori_loop(0, nh, per_edge, 0)
        parts = []
        for h in range(heads):
            total = l_s[h, i]
            parts.append((acc[h, i, :HEAD_DIM] + acc[h, i, HEAD_DIM:]) / total)
            lse_ref[h:h + 1, qrow] = m_s[h, i] + jnp.log(total)
        out_ref[qrow, :] = jnp.concatenate(parts, axis=0).T
        return 0

    lax.fori_loop(0, nq, per_q, 0)
    wide_ref[:, :width] = out_ref[:group // 2, :]
    wide_ref[:, width:] = out_ref[group // 2:, :]


def attend_own(segs, qcode, kcode, q, kv):
    group, width = q.shape
    heads, nq = width // HEAD_DIM, group // TILE
    return call(
        functools.partial(attend_own_kernel, heads), "attend_own",
        [arr((heads, group, 3 * HEAD_DIM), BF), arr((heads, nq, 1, TILE)), arr((heads, nq, 1, TILE)),
         arr((heads, nq, 2 * HEAD_DIM, TILE))],
        [segs, qcode, kcode, q, kv],
        [pltpu.VMEM((heads, group, 3 * HEAD_DIM), BF), pltpu.VMEM((heads, nq, 2 * HEAD_DIM, TILE), BF),
         pltpu.VMEM((group, 128), F32)],
        flops=4 * group * group * width)


def attend_edge(segs, qcode, hcode, halo, state, passed=(), marks=()):
    heads, group, _ = state[0].shape
    reach, width = halo.shape[0], halo.shape[1] // 2
    nq, nh = group // TILE, reach // EDGE
    return call(
        functools.partial(attend_edge_kernel, heads, len(passed)), "attend_edge",
        [arr((group, width)), arr((group // 2, 2 * width)), arr((8, group))] + [arr(x.shape) for x in passed],
        [segs, qcode, hcode, halo, *state, *passed],
        [pltpu.VMEM((heads, reach, 3 * HEAD_DIM), BF), pltpu.VMEM((heads, nh, 2 * HEAD_DIM, EDGE), BF),
         pltpu.VMEM((reach, 128), F32)]
        + [pltpu.VMEM(x.shape, x.dtype) for x in state[1:]],
        flops=2 * group * reach * width, wide=reach > group, marks=marks)


def back_add(heads, qc, q2, dc, d2, dot_s, lse_ref, keys, values, flipped, dqa, dka, dva, i, j, size, allowed):
    qrow = at(i * TILE, TILE, TILE)
    krow = at(j * size, size, size)
    for h in range(heads):
        s = mm(keys[h, krow, :], qc[h, qrow, :], NT)
        p = jnp.exp(jnp.where(allowed, s - lse_ref[h:h + 1, qrow], FLOOR))
        dp = mm(values[h, krow, :], dc[h, qrow, :], NT)
        ds = p * (dp - dot_s[h, :, qrow])
        hi, lo = split(p)
        d128 = d2[h, qrow, :]
        dva[h] += mm(hi, d128) + mm(lo, d128)
        hi, lo = split(ds)
        q128 = q2[h, qrow, :]
        dka[h] += mm(hi, q128) + mm(lo, q128)
        k128 = flipped[h, j]
        dqa[h, i] += mm(k128, hi) + mm(k128, lo)


def back_over(heads, seg_ref, nq, count, size, first, out, dka, dva, visit):
    width = heads * HEAD_DIM

    def folded(acc):
        return jnp.concatenate([acc[h, :, :HEAD_DIM] + acc[h, :, HEAD_DIM:] for h in range(heads)], axis=1)

    def per_k(j, _):
        dka[...] = jnp.zeros_like(dka)
        dva[...] = jnp.zeros_like(dva)

        def per_q(i, _):
            @pl.when(span_hits(seg_ref, i, first + j))
            def _():
                visit(i, j)
            return 0

        lax.fori_loop(0, nq, per_q, 0)
        krow = at(j * size, size, size)
        out[krow, :width] = folded(dka)
        out[krow, width:] = folded(dva)
        return 0

    lax.fori_loop(0, count, per_k, 0)


def back_edge_kernel(heads, splits, idx, seg_ref, qcode_ref, hcode_ref, q_ref, halo_ref, o_ref, lse_ref, qc,
                     oh_ref, ol_ref, *refs):
    mg, (dhalo_ref, q2, dc, d2, dot_s, dqa, gh, gl, kh, vh, kth, hcol, prod_s, dka, dva) = (
        refs[:splits], refs[splits:])
    group, width = q_ref.shape
    nq, nh = group // TILE, halo_ref.shape[0] // EDGE
    tokens = group // splits
    if nh:
        prepare(halo_ref, width, 0, nh, EDGE, [(kh, 0), (vh, width)], kth)
        columns(hcode_ref, hcol, EDGE)
    for h in range(heads):
        hi, lo = split(q_ref[:, h * HEAD_DIM:(h + 1) * HEAD_DIM] * HEAD_DIM ** -0.5)
        q2[h] = jnp.concatenate([hi, lo], axis=1)
    dqa[...] = jnp.zeros_like(dqa)
    wrow = at(idx[0, 0] * width, width, 16)
    w_pair = (oh_ref[wrow, :], ol_ref[wrow, :])
    for r in range(splits):
        row = at(idx[0, r] * tokens, tokens, 16)
        gh[row, :], gl[row, :] = split(mg[r][...])
    step = group // 3

    def rows_of(i, _):
        row = at(i * step, step, 16)
        grad = mm3((gh[row, :], gl[row, :]), w_pair, NT)
        prod_s[row, :] = grad * o_ref[row, :]
        for h in range(heads):
            hi, lo = split(grad[:, h * HEAD_DIM:(h + 1) * HEAD_DIM])
            dc[h, row, :] = jnp.concatenate([hi, hi, lo], axis=1)
            d2[h, row, :] = jnp.concatenate([hi, lo], axis=1)
        return 0

    lax.fori_loop(0, 3, rows_of, 0)
    for i in range(nq):
        rows = slice(i * TILE, (i + 1) * TILE)
        prod = prod_s[rows, :].T
        for h in range(heads):
            dot_s[h, :, rows] = jnp.sum(prod[h * HEAD_DIM:(h + 1) * HEAD_DIM], axis=0, keepdims=True)

    def visit(i, j):
        allowed = hcol[at(j * EDGE, EDGE, EDGE), :1] == qcode_ref[:1, at(i * TILE, TILE, TILE)]
        back_add(heads, qc, q2, dc, d2, dot_s, lse_ref, kh, vh, kth, dqa, dka, dva, i, j, EDGE, allowed)

    if nh:
        back_over(heads, seg_ref, nq, nh, EDGE, nq, dhalo_ref, dka, dva, visit)


def back_own_kernel(heads, seg_ref, qcode_ref, kcode_ref, kv_ref, lse_ref, qc, q2, dc, d2, dot_s, dq_in,
                    dq_ref, dkv_ref, kc, vc, kt, kcol, dqa, dka, dva):
    group, width = dq_ref.shape
    nq = group // TILE
    prepare(kv_ref, width, 0, nq, TILE, [(kc, 0), (vc, width)], kt)
    columns(kcode_ref, kcol, TILE)
    dqa[...] = dq_in[...]

    def visit(i, j):
        allowed = kcol[at(j * TILE, TILE, TILE), :1] == qcode_ref[:1, at(i * TILE, TILE, TILE)]
        back_add(heads, qc, q2, dc, d2, dot_s, lse_ref, kc, vc, kt, dqa, dka, dva, i, j, TILE, allowed | same_row(i, j))

    back_over(heads, seg_ref, nq, nq, TILE, 0, dkv_ref, dka, dva, visit)
    for i in range(nq):
        parts = [(dqa[h, i, :HEAD_DIM] + dqa[h, i, HEAD_DIM:]) * HEAD_DIM ** -0.5 for h in range(heads)]
        dq_ref[i * TILE:(i + 1) * TILE, :] = jnp.concatenate(parts, axis=0).T


def attend_back_edge(idx, segs, qcode, hcode, q, halo, o, lse, qc, oh, ol, mg):
    group, width = q.shape
    reach = halo.shape[0]
    heads = width // HEAD_DIM
    nq, nh = group // TILE, reach // EDGE
    full = oh.shape[1]
    H3, H2 = 3 * HEAD_DIM, 2 * HEAD_DIM
    return call(
        functools.partial(back_edge_kernel, heads, len(mg)), "back_edge",
        [arr((reach, 2 * width)), arr((heads, group, H2), BF), arr((heads, group, H3), BF), arr((heads, group, H2), BF),
         arr((heads, 1, group)), arr((heads, nq, H2, TILE)), arr((group, full), BF), arr((group, full), BF)],
        [idx, segs, qcode, hcode, q, halo, o, lse, qc, oh, ol, *mg],
        [
            pltpu.VMEM((heads, reach, H3), BF),
            pltpu.VMEM((heads, reach, H3), BF),
            pltpu.VMEM((heads, nh, H2, EDGE), BF),
            pltpu.VMEM((reach, 128), F32),
            pltpu.VMEM((group, width), F32),
            pltpu.VMEM((heads, EDGE, H2), F32),
            pltpu.VMEM((heads, EDGE, H2), F32),
        ],
        flops=2 * group * full * width, smem=2, wide=reach > group)


def attend_back_own(segs, qcode, kcode, kv, lse, qc, q2, dc, d2, dot_s, dqa, marks):
    heads, group, _ = qc.shape
    width = kv.shape[1] // 2
    nq = group // TILE
    H3, H2 = 3 * HEAD_DIM, 2 * HEAD_DIM
    return call(
        functools.partial(back_own_kernel, heads), "back_own",
        [arr((group, width)), arr((group, 2 * width))],
        [segs, qcode, kcode, kv, lse, qc, q2, dc, d2, dot_s, dqa],
        [
            pltpu.VMEM((heads, group, H3), BF),
            pltpu.VMEM((heads, group, H3), BF),
            pltpu.VMEM((heads, nq, H2, TILE), BF),
            pltpu.VMEM((group, 128), F32),
            pltpu.VMEM((heads, nq, H2, TILE), F32),
            pltpu.VMEM((heads, TILE, H2), F32),
            pltpu.VMEM((heads, TILE, H2), F32),
        ],
        flops=10 * group * group * width, marks=marks)


def weights_kernel(full, splits, idx, *refs):
    count = max([p[0] for p in full]) + 1
    weights, (uh, ul, oh, ol, u32, o32) = refs[:count], refs[count:count + 6]
    got = weights
    owners = len(full)
    rows = u32.shape[0] // owners
    for i, (n, lead) in enumerate(full):
        row = at(idx[0, splits + i] * rows, rows)
        u32[row, :] = got[n][lead]
        o32[row, :] = got[n][2]
    uh[...], ul[...] = split(u32[...])
    oh[...], ol[...] = split(o32[...])


def act_kernel(splits, whole, first, place, idx, *refs):
    got, (gh, gl, dh, dl, act_ref) = refs[:-5], refs[-5:]
    tokens = got[0].shape[0]
    down = got[splits:]
    unit = down[0].shape[0]
    blocks = dh.shape[0] // unit
    for r in range(splits):
        row = at(idx[0, r] * tokens, tokens, 16)
        gh[row, :], gl[row, :] = split(got[r][...])
    for i in range(blocks):
        if i < whole:
            row = at(idx[0, first + i] * unit, unit, 16)
            dh[row, :], dl[row, :] = split(down[i][...])
            continue
        size = unit // 4
        for z in range(4):
            quarter = idx[0, place] ^ (0, 3, 1, 2)[z]
            row = at(idx[0, first + i] * unit + quarter * size, size, 16)
            dh[row, :], dl[row, :] = split(down[whole + 4 * (i - whole) + z][...])
    step = gh.shape[0] // 2

    def rows_of(i, _):
        row = at(i * step, step, 16)
        act_ref[row, :] = mm3((gh[row, :], gl[row, :]), (dh[...], dl[...]), NT)
        return 0

    lax.fori_loop(0, 2, rows_of, 0)


def feed_kernel(splits, idx, small, base, *refs):
    (oh, ol, uh, ul, act, keep, send, mine, inv_ref, ah, al, ph, plo, mh, ml, vec, b32, x2, g32, r32) = (
        refs[splits:splits + 20])
    att = refs[:splits]
    tokens = keep.shape[1]
    group = b32.shape[0]
    part = att[0].shape[1] // 2
    gain, shift = small[6:7, :], small[7:8, :]
    up_bias = small[pl.ds(8 + idx[0, 0], 1), :]
    vec[...] = jnp.zeros_like(vec)
    step = group // 2

    def rows_of(i, _):
        row = at(i * step, step, 16)
        middle = base[row, :] + small[2:3, :]
        for s in range(splits):
            wrow = at(idx[0, s] * part, part, 16)
            piece = jnp.where(i == 0, att[s][:, :part], att[s][:, part:])
            middle = middle + mm3(split(piece), (oh[wrow, :], ol[wrow, :]))
        b32[row, :] = middle
        xhat, inverse = norm(middle)
        x2[row, :] = xhat
        g32[row, :] = jnp.broadcast_to(inverse, g32[row, :].shape)
        pair = split(xhat * gain + shift)
        mh[row, :], ml[row, :] = pair
        pre = mm3(pair, (uh[...], ul[...])) + up_bias
        square = pre * pre
        curve = jnp.tanh(SQRT_2_PI * (pre + CUBIC * square * pre))
        half = 0.5 * (1.0 + curve)
        ah[row, :], al[row, :] = split(pre * half)
        slope = half + 0.5 * pre * (1.0 - curve * curve) * SQRT_2_PI * (1.0 + 3.0 * CUBIC * square)
        grad = act[row, :] * slope
        pair = split(grad)
        ph[row, :], plo[row, :] = pair
        back = mm3(pair, (uh[...], ul[...]), NT)
        vec[0:1, :] += jnp.sum(grad, axis=0, keepdims=True)
        vec[1:2, :] += jnp.sum(back * xhat, axis=0, keepdims=True)
        vec[2:3, :] += jnp.sum(back, axis=0, keepdims=True)
        r32[row, :] = back
        return 0

    lax.fori_loop(0, 2, rows_of, 0)

    def pairs_of(h, _):
        keep[h] = r32[at(idx[0, 2 * h] * tokens, tokens), :]
        send[h] = r32[at(idx[0, 2 * h + 1] * tokens, tokens), :]
        return 0

    lax.fori_loop(0, splits // 2, pairs_of, 0)
    row = at(idx[0, 0] * tokens, tokens)
    mine[0] = b32[row, :]
    mine[1] = x2[row, :]
    inv_ref[...] = g32[row, :]


def feed_grads_kernel(splits, first, down_rows, up_rows, idx, ah, al, ph, plo, mh, ml, gh, gl, dh, dl,
                      keep, send, *refs):
    outs, r32 = refs[:-1], refs[-1]
    downs, ups = outs[:len(outs) // 2], outs[len(outs) // 2:]
    tokens = keep.shape[1]
    step = r32.shape[0] // 2

    third = r32.shape[0] // 3

    def left(a, b):
        def rows_of(i, _):
            lane = at(i * third, third, 128)
            r32[at(i * third, third), :] = mm3((a[0][:, lane], a[1][:, lane]), (b[0][...], b[1][...]), TN)
            return 0

        lax.fori_loop(0, 3, rows_of, 0)

    def deal(targets, rows, place):
        for target in targets:
            def one(c, _, target=target, place=place):
                target[c] = r32[at(idx[0, place + c], rows), :]
                return 0

            lax.fori_loop(0, target.shape[0], one, 0)
            place += target.shape[0]
        return place

    left((ah, al), (gh, gl))
    place = deal(downs, down_rows, first)
    left((mh, ml), (ph, plo))
    deal(ups, up_rows, place)

    def rows_of(i, _):
        row = at(i * step, step, 16)
        r32[row, :] = mm3((ah[row, :], al[row, :]), (dh[...], dl[...]))
        return 0

    lax.fori_loop(0, 2, rows_of, 0)

    def pairs_of(h, _):
        keep[h] = r32[at(idx[0, 2 * h] * tokens, tokens), :]
        send[h] = r32[at(idx[0, 2 * h + 1] * tokens, tokens), :]
        return 0

    lax.fori_loop(0, splits // 2, pairs_of, 0)


def middle_kernel(small, keep, core, far, og, mine, inv, mg_ref, vec_ref):
    grad = keep[0] + core[0] + far[...]
    out = og[...] + norm_back(grad, small[6:7, :], mine[1], inv[:, :1])
    mg_ref[...] = out
    vec_ref[...] = jnp.zeros_like(vec_ref)
    vec_ref[0:1, :] = jnp.sum(out, axis=0, keepdims=True)
    vec_ref[1:2, :] = jnp.sum(og[...], axis=0, keepdims=True)


def last_grads_kernel(splits, first, edge, rows, idx, small, dq, dkv, back, base, att, vec1, vec2, gh, gl, wh, wl,
                      keep, send, *refs):
    tails, (qh, ql, xhat, r32, o32, s32, n32, vec) = refs[:-8], refs[-8:]
    part = dq.shape[1]
    width = xhat.shape[1]
    tokens = keep.shape[1]
    u = idx[0, 0]
    s32[:, :part] = dq[...]
    s32[:, part:] = dkv[...]
    s32[at(idx[0, edge], back.shape[0]), part:] += back[...]
    qkv = s32[...]
    qh[...], ql[...] = split(qkv)
    sums = jnp.sum(qkv, axis=0, keepdims=True)
    xhat[...], _ = norm(base[...])
    vec[...] = jnp.zeros_like(vec)
    step = n32.shape[0] // 2

    def rows_of(i, _):
        row = at(i * step, step, 16)
        grad = mm3((qh[row, :], ql[row, :]), (wh[...], wl[...]), NT)
        n32[row, :] = grad
        vec[4:5, :] += jnp.sum(grad * xhat[row, :], axis=0, keepdims=True)
        vec[5:6, :] += jnp.sum(grad, axis=0, keepdims=True)
        return 0

    lax.fori_loop(0, 2, rows_of, 0)

    def pairs_of(h, _):
        keep[h] = n32[at(idx[0, 2 * h] * tokens, tokens), :]
        send[h] = n32[at(idx[0, 2 * h + 1] * tokens, tokens), :]
        return 0

    lax.fori_loop(0, splits // 2, pairs_of, 0)
    step = width // 3

    def lanes_of(i, _):
        lane = at(i * step, step, 128)
        pair = split(xhat[:, lane] * small[4:5, lane] + small[5:6, lane])
        r32[lane, :] = mm3(pair, (qh[...], ql[...]), TN)
        return 0

    lax.fori_loop(0, 3, lanes_of, 0)
    o32[...] = mm3(split(att[...]), (gh[...], gl[...]), TN)
    for i in range(splits):

        @pl.when(u == i)
        def _():
            vec[0:1, i * part:(i + 1) * part] = sums[:, :part]
            vec[1:2, i * part:(i + 1) * part] = sums[:, 2 * part:]

    vec[2:4, :] = vec2[0:2, :]
    vec[6:8, :] = vec1[1:3, :]
    vec[pl.ds(8 + u, 1), :] = vec1[0:1, :]
    wide = r32.shape[1]
    outs = width // 128
    vecs = outs * EXTRA // rows
    lane_blocks = -(-wide // 128)
    spare = lane_blocks * 128 - wide
    near = 2 * lane_blocks
    total = sum(t.shape[0] for t in tails)
    spot = 0
    for t in tails:
        def one(c, _, t=t, spot=spot):
            for j in range(splits):
                row = at(idx[0, first + (spot + c) * splits + j], rows)
                start = j * lane_blocks + (outs + vecs if j >= 2 else 0)
                for k in range(lane_blocks - 1):
                    t[c, start + k] = r32[row, k * 128:(k + 1) * 128]
                k = lane_blocks - 1
                t[c, start + k, :, :128 - spare] = r32[row, k * 128:]
                t[c, start + k, :, 128 - spare:] = jnp.zeros((rows, spare), F32)
            row = at(idx[0, first + total * splits + spot + c], rows)
            for k in range(outs):
                t[c, near + k] = o32[row, k * 128:(k + 1) * 128]
            for k in range(outs * EXTRA // 8):
                block, low = divmod(8 * k, rows)
                lane, high = divmod(8 * k, EXTRA)
                t[c, near + outs + block, low:low + 8, :] = vec[high:high + 8, lane * 128:(lane + 1) * 128]
            return 0

        lax.fori_loop(0, t.shape[0], one, 0)
        spot += t.shape[0]


def hidden_kernel(idx, small, base, keep, core, far, mg, out):
    tokens = mg.shape[0]
    xhat, inverse = norm(base[at(idx[0, 0] * tokens, tokens), :])
    out[...] = mg[...] + norm_back(keep[0] + core[0] + far[...], small[4:5, :], xhat, inverse)


def fold_kernel(count, *refs):
    keeps, gots, outs = refs[:count], refs[count:2 * count], refs[2 * count:]
    for i in range(count):
        stay, go = outs[2 * i:2 * i + 2]
        half = stay.shape[0]
        stay[...] = keeps[i][:half] + gots[i][:half]
        go[...] = keeps[i][half:] + gots[i][half:]


def fold(keeps, gots, marks=()):
    outs = []
    for keep in keeps:
        outs += [arr((keep.shape[0] // 2,) + keep.shape[1:])] * 2
    got = call(functools.partial(fold_kernel, len(keeps)), "fold", outs, [*keeps, *gots], smem=0, marks=marks)
    return got[::2], got[1::2]


def message_kernel(near, stop, vecs, part, far, out):
    blocks = near // 2
    out[:blocks] = part[blocks:near]
    out[blocks:blocks + vecs] = part[stop:stop + vecs] + far[:vecs]
    out[blocks + vecs:] = far[vecs + blocks:]


def place_kernel(splits, first, rows, idx, *refs):
    pieces, (gq, gk, gv, go) = refs[:-4], refs[-4:]
    part = gq.shape[1] // splits
    for z, piece in enumerate(pieces):
        row = at(idx[0, first + z] * rows, rows)
        count = gq.shape[1] // 128
        for k in range(count):
            go[row, k * 128:(k + 1) * 128] = piece[5 * splits + k]
        for i in range(splits):
            whole = jnp.concatenate([piece[5 * idx[0, i] + k] for k in range(5)], axis=1)
            for n, out in enumerate((gq, gk, gv)):
                out[row, i * part:(i + 1) * part] = whole[:, n * part:(n + 1) * part]


def place_feed_kernel(splits, blocks, unit, first, idx, *refs):
    pieces, (gd, gu) = refs[:-2], refs[-2:]
    downs, ups = pieces[:len(pieces) // 2], pieces[len(pieces) // 2:]
    for z, (down, up) in enumerate(zip(downs, ups)):
        gd[at(idx[0, first + z] * down.shape[0], down.shape[0]), :] = down[...]
        rows = up.shape[1]
        row = at(idx[0, first + z] * rows, rows)
        for i in range(splits):
            for n in range(blocks):
                start = (n * splits + i) * unit
                gu[row, start:start + unit] = up[idx[0, i], :, n * unit:(n + 1) * unit]


def swap(value, axis, mask):
    count = lax.axis_size(axis)
    return lax.ppermute(value, axis, [(i, i ^ mask) for i in range(count)])


def across(value):
    return swap(value, "ulys", 2)


def beside(value):
    return swap(value, "ulys", 1)


def over(value):
    return swap(value, "blk", 1)


def gather_splits(value):
    far = across(value)
    return [value, beside(value), far, beside(far)]


def collect(value):
    near = swap(value, "dp", 3)
    return [value, near, swap(value, "dp", 1), swap(near, "dp", 1)]


def halo_moves(group, reach, blocks):
    moves = []
    shift = 1
    while reach > 0 and shift < blocks:
        rows = min(group, reach)
        moves.append((rows, True, [(i, i - shift) for i in range(shift, blocks)]))
        moves.append((rows, False, [(i, i + shift) for i in range(blocks - shift)]))
        reach -= rows
        shift += 1
    return moves


def halo_get(value, reach, axis=0):
    blocks, group = lax.axis_size("blk"), value.shape[axis]
    parts = []
    for rows, right, moves in halo_moves(group, reach, blocks):
        start = 0 if right else group - rows
        parts.append(lax.ppermute(lax.slice_in_dim(value, start, start + rows, axis=axis), "blk", moves))
    return jnp.concatenate(parts, axis=axis)


def halo_add(value, halo, reach):
    blocks, group = lax.axis_size("blk"), value.shape[0]
    start = 0
    for rows, right, moves in halo_moves(group, reach, blocks):
        back = lax.ppermute(halo[start:start + rows], "blk", [(j, i) for i, j in moves])
        start += rows
        room = group - rows
        value = value + jnp.pad(back, ((0, room), (0, 0)) if right else ((room, 0), (0, 0)))
    return value


def local(
    hidden,
    time_embed,
    segment_ids,
    key_valid,
    out_grad,
    w_query,
    b_query,
    w_key,
    w_value,
    b_value,
    w_out,
    b_out,
    w_up,
    b_up,
    w_down,
    b_down,
    pre_gain,
    pre_shift,
    mlp_gain,
    mlp_shift,
):
    blocks, splits = lax.axis_size("blk"), lax.axis_size("ulys")
    b, u, d = (lax.axis_index(name) for name in ("blk", "ulys", "dp"))
    both = ("blk", "ulys")
    owners = blocks * splits
    tokens, width = hidden.shape
    group = tokens * splits
    part = width // splits
    rows = w_query.shape[0]
    unit = w_down.shape[0]
    units = unit * owners
    share = units // splits
    reach = group * blocks // 4
    fast = blocks == 2 and splits == 4 and lax.axis_size("dp") == 4 and reach <= group and group == width

    if fast:
        f1, f3 = (d ^ (d >> 1)) & 1, d >> 1
        quarters = [2 * (f1 ^ s) + (f3 ^ t) for s in range(2) for t in range(2)]
        owner_list = [(b ^ x) * splits + (u ^ r) for x in range(2) for r in range(4)]
        block_list = [b, b ^ 1]
        edge_row = jnp.where(b == 0, group - reach, 0)
        down_rows, up_rows, tail_rows = unit // 4, rows // 4, rows // 4
        down_table = [(b ^ x) * unit + q * down_rows for x in range(2) for q in quarters]
        up_table = [
            ((b ^ x) * splits + (u ^ r)) * rows + q * up_rows for q in quarters for x in range(2) for r in range(4)
        ]
        tail_table = [
            ((b ^ x) * splits + (u ^ r)) * rows + q * tail_rows for x in range(2) for q in quarters for r in range(4)
        ] + [(b ^ x) * rows + q * tail_rows for x in range(2) for q in quarters]
        chunks = 8
    else:
        quarters = []
        owner_list = list(range(owners))
        block_list = list(range(blocks))
        edge_row = 0
        down_rows, up_rows, tail_rows = unit, rows, rows
        down_table = [i * unit for i in range(blocks)]
        up_table = [i * rows for i in range(owners)]
        tail_table = up_table + [i * rows for i in range(blocks)]
        chunks = blocks
    entries, spots = [], []
    for values in (
        [u ^ r for r in range(splits)], owner_list, block_list, [d], [edge_row], down_table + up_table, tail_table,
        quarters,
    ):
        spots.append(len(entries))
        entries += values
    _, _, at_block, at_d, at_edge, at_feed, at_tail, at_quarter = spots
    idx = jnp.stack([jnp.asarray(v, jnp.int32) for v in entries]).reshape(1, -1)

    segments = segment_ids[0] + 1
    codes = jnp.stack([segments, jnp.where(key_valid[0] == 1, segments, 0)]).astype(F32)
    small = jnp.stack([b_query, b_value, b_out, b_down, pre_gain, pre_shift, mlp_gain, mlp_shift])
    small = lax.dynamic_update_slice(jnp.zeros((EXTRA, width), F32), small, (0, (b * splits + u) * rows))
    small = lax.dynamic_update_slice(small, b_up[None], (8 + u, b * unit))
    if fast:
        small = lax.dynamic_update_slice(small, codes, (12, 0))
        other = over(small)
        small = small + other
        halo_codes = jnp.where(b == 0, other[12:14, :reach], other[12:14, group - reach:group])
    else:
        small = lax.psum(small, "blk")
        halo_codes = halo_get(codes, reach, axis=1)
    tiles = codes[0].reshape(-1, TILE)
    edges = halo_codes[0].reshape(-1, EDGE)
    bounds = jnp.concatenate(
        [
            jnp.stack([tiles[:, 0], tiles[:, -1]], axis=1).reshape(-1),
            jnp.stack([jnp.min(jnp.where(edges == 0, 1e6, edges), axis=1), jnp.max(edges, axis=1)], axis=1).reshape(-1),
        ]
    ).astype(jnp.int32).reshape(1, -1)
    def make_base(marks):
        return call(
            base_kernel, "base", [arr((tokens + EXTRA, width))], [hidden, time_embed, small], smem=0, marks=marks)[0]

    if fast:
        tables = [idx, bounds, codes, halo_codes, small]
        near, far, *tables = call(
            pack_qkv_kernel, "pack_qkv",
            [arr((2, rows, 3 * part))] * 2 + [arr(x.shape, x.dtype) for x in tables],
            [*tables, w_query, w_key, w_value], smem=2)
        idx, bounds, codes, halo_codes, small = tables
        pieces = [(i, i % 2) for i in range(8)]
        far = across(far)
        near_over = over(near)
        base = make_base([far, near_over])
        far_base = across(base)
        qkv_arrays = [near, beside(near), far, beside(far)]
        near = near_over
        far = over(far)
        qkv_arrays += [near, beside(near), far, beside(far)]
        base_all = [base, beside(base), far_base, beside(far_base)]
        near2, far2, down_quarter = call(
            functools.partial(pack_feed_kernel, splits, blocks, at_d), "pack_feed",
            [arr((3, rows, share))] * 2 + [arr((unit // 4, width))],
            [idx, w_up, w_out, w_down], marks=[far])
        down_quarter = over(down_quarter)
        far2 = across(far2)
        feed_arrays = [near2, beside(near2), far2, beside(far2)]
        near2 = over(near2)
        feed_arrays += [near2, beside(near2)]
        whole = 1
    else:
        cut = jnp.stack([w_query, w_key, w_value], axis=1).reshape(rows, 3, splits, part)
        cut = cut.transpose(2, 0, 1, 3).reshape(splits, rows, 3 * part)
        cut = jnp.broadcast_to(cut[None], (blocks,) + cut.shape).reshape(owners, rows, 3 * part)
        got = lax.all_to_all(cut, both, 0, 0, tiled=True)
        qkv_arrays = [got[i:i + 1] for i in range(owners)]
        cut = w_up.reshape(rows, blocks, splits, unit).transpose(2, 0, 1, 3).reshape(splits, rows, share)
        cut = jnp.broadcast_to(cut[None], (blocks,) + cut.shape).reshape(owners, rows, share)
        got = lax.all_to_all(cut, both, 0, 0, tiled=True)
        outs = lax.all_gather(w_out, both, axis=0, tiled=False)
        feed_arrays = [jnp.stack([got[i], got[i], outs[i]]) for i in range(owners)]
        pieces = [(i, 0) for i in range(owners)]
        whole = blocks
        base = make_base([])
        base_all = gather_splits(base)
        gathered = lax.all_gather(w_down, "blk", axis=0, tiled=False)
        down = [gathered[i] for i in range(blocks)]

    query_codes, key_codes, edge_codes = codes, codes, halo_codes
    query, key_value, edge_kv, base, small, qkv_hi, qkv_lo, own_grad = call(
        functools.partial(qkv_kernel, pieces, splits, at_edge), "qkv",
        [arr((group, part)), arr((group, 2 * part)), arr((reach if fast else 8, 2 * part)), arr((group, width)),
         arr((EXTRA, width)), arr((width, 3 * part), BF), arr((width, 3 * part), BF), arr((tokens, width))],
        [idx, out_grad, *base_all, *qkv_arrays],
        [pltpu.VMEM((width, 3 * part), F32), pltpu.VMEM((group, width), BF), pltpu.VMEM((group, width), BF)],
        flops=2 * group * width * 3 * part)
    halo = over(edge_kv) if fast else halo_get(key_value, reach)
    state = attend_own(bounds, query_codes, key_codes, query, key_value)
    grads = gather_splits(own_grad)
    if fast:
        down = [w_down, down_quarter] + [swap(down_quarter, "dp", mask) for mask in (3, 1, 2)]
        attended, attended_wide, lse, far2 = attend_edge(bounds, query_codes, edge_codes, halo, state, (far2,), [*down[2:], grads[2], near2])
        far2 = over(far2)
        feed_arrays += [far2, beside(far2)]
    else:
        attended, attended_wide, lse = attend_edge(bounds, query_codes, edge_codes, halo, state)
    attended_all = gather_splits(attended_wide)
    og_hi, og_lo, down_hi, down_lo, act_grad = call(
        functools.partial(act_kernel, splits, whole, at_block, at_d), "act",
        [arr((group, width), BF)] * 2 + [arr((share, width), BF)] * 2 + [arr((group, share))],
        [idx, *grads, *down],
        flops=2 * group * width * share, marks=[attended_all[2]])
    up_hi, up_lo, out_hi, out_lo = call(
        functools.partial(weights_kernel, pieces, splits), "weights",
        [arr((width, share), BF)] * 2 + [arr((width, width), BF)] * 2,
        [idx, *feed_arrays],
        [pltpu.VMEM((width, share), F32), pltpu.VMEM((width, width), F32)], marks=[act_grad])

    pair = [arr((group, share), BF)] * 2
    keep, send, mine, inverse2, act_hi, act_lo, pre_hi, pre_lo, in_hi, in_lo, vec_feed = call(
        functools.partial(feed_kernel, splits), "feed",
        [arr((2, tokens, width))] * 2 + [arr((2, tokens, width)), arr((tokens, 128))] + pair * 2
        + [arr((group, width), BF)] * 2 + [arr((8, width))],
        [idx, small, base, *attended_all, out_hi, out_lo, up_hi, up_lo, act_grad],
        [pltpu.VMEM((group, width), F32), pltpu.VMEM((group, width), F32), pltpu.VMEM((group, 128), F32),
         pltpu.VMEM((group, width), F32)],
        flops=2 * group * width * (width + 2 * share))
    core = beside(send)
    near_sum = keep[1] + core[1]
    far_sum = across(near_sum)

    if fast:
        feed_outs = [arr((4, down_rows, width))] * 2 + [arr((8 * splits // 2, up_rows, share))] * 2
    else:
        feed_outs = [arr((blocks, down_rows, width)), arr((owners, up_rows, share))]
    keep_out, send_out, *feed_grads = call(
        functools.partial(feed_grads_kernel, splits, at_feed, down_rows, up_rows), "feed_grads",
        [arr((2, tokens, width))] * 2 + feed_outs,
        [idx, act_hi, act_lo, pre_hi, pre_lo, in_hi, in_lo, og_hi, og_lo, down_hi, down_lo],
        [pltpu.VMEM((group, width), F32)],
        flops=6 * group * width * share, marks=[near_sum])
    if fast:
        down_keep, down_send, up_keep, up_send = feed_grads
        down_got = over(down_send)
        up_got = swap(up_send, "dp", 1)

    middle_grad, vec_middle = call(
        middle_kernel, "middle",
        [arr((tokens, width)), arr((8, width))],
        [small, keep, core, far_sum, out_grad, mine, inverse2], smem=0, marks=[keep_out])
    middle_all = gather_splits(middle_grad)

    halo_grad, q2, dc, d2, dots, dq_part, mg_hi, mg_lo = attend_back_edge(
        idx, bounds, query_codes, edge_codes, query, halo, attended, lse, state[0], out_hi, out_lo, middle_all)
    if fast:
        returned = over(halo_grad)
        (down_keep, up_keep), (down_send, up_send) = fold((down_keep, up_keep), (down_got, up_got), [halo_grad])
        down_got = swap(down_send, "dp", 1)
        up_got = swap(up_send, "dp", 3)
        own_marks = [down_keep]
    else:
        own_marks = []
    query_grad, kv_grad = attend_back_own(
        bounds, query_codes, key_codes, key_value, lse, state[0], q2, dc, d2, dots, dq_part, own_marks)
    if not fast:
        kv_grad = halo_add(kv_grad, halo_grad, reach)
        returned = jnp.zeros((8, 2 * part), F32)

    core_out = beside(send_out)
    far_out = across(keep_out[1] + core_out[1])
    lane_blocks = -(-3 * part // 128)
    outs, vecs = width // 128, width // 128 * EXTRA // tail_rows
    total_blocks = splits * lane_blocks + outs + vecs
    tail_outs = [arr((2, total_blocks, tail_rows, 128))] * 4 if fast else [arr((blocks, total_blocks, tail_rows, 128))]
    keep_in, send_in, *tail = call(
        functools.partial(last_grads_kernel, splits, at_tail, at_edge, tail_rows), "last_grads",
        [arr((2, tokens, width))] * 2 + tail_outs,
        [idx, small, query_grad, kv_grad, returned, base, attended, vec_feed, vec_middle, mg_hi, mg_lo, qkv_hi, qkv_lo],
        [pltpu.VMEM((group, 3 * part), BF), pltpu.VMEM((group, 3 * part), BF), pltpu.VMEM((group, width), F32),
         pltpu.VMEM((width, 3 * part), F32), pltpu.VMEM((part, width), F32), pltpu.VMEM((group, 3 * part), F32),
         pltpu.VMEM((group, width), F32), pltpu.VMEM((EXTRA, width), F32)],
        flops=2 * group * width * 7 * part, marks=[far_out])
    to_owner = [(i * splits + j, j * blocks + i) for i in range(blocks) for j in range(splits)]
    near = 2 * lane_blocks
    if fast:
        tail_near, tail_far, send_near, send_far = tail
        got_far = over(send_far)
        got_near = over(send_near)
        core_in = beside(send_in)
        far_in = across(keep_in[1] + core_in[1])

        (down_keep, up_keep), (down_send, up_send) = fold((down_keep, up_keep), (down_got, up_got), [keep_in])
        down_got = swap(down_send, "dp", 3)
        up_got = over(up_send)
        tail_got = swap(tail_far + got_far, "dp", 1)
        tail_near = tail_near + got_near
        part_down = (down_keep + down_got)[0]
        part_up = up_keep + up_got
        far_up = across(part_up[2:])
        core_up = beside(jnp.stack([part_up[1], far_up[1]]))
        part_up = jnp.stack([part_up[0], core_up[0], far_up[0], core_up[1]])
        all_down = collect(part_down)
        all_up = collect(part_up)
        (tail_keep,), (tail_send,) = fold((tail_near,), (tail_got,), [*all_down, all_up[1], far_in])
        part_tail = (tail_keep + swap(tail_send, "dp", 3))[0]

        far_tail = across(part_tail[near + outs:])
        message, = call(
            functools.partial(message_kernel, near, near + outs, vecs), "message", [arr(far_tail.shape)],
            [part_tail, far_tail], smem=0, marks=[])
        core_tail = beside(message)
        vec = part_tail[near + outs:near + outs + vecs] + far_tail[:vecs] + core_tail[lane_blocks:lane_blocks + vecs]
        owned = lax.ppermute(part_tail[near:near + outs], both, to_owner)
        part_tail = jnp.concatenate([
            part_tail[:lane_blocks], core_tail[:lane_blocks], far_tail[vecs:vecs + lane_blocks],
            core_tail[lane_blocks + vecs:], owned])
        all_tail = collect(part_tail)
        total_down, total_up = call(
            functools.partial(place_feed_kernel, splits, blocks, unit, at_quarter), "place_feed",
            [arr((unit, width)), arr((rows, units))],
            [idx, *all_down, *all_up])
        total_query, total_key, total_value, total_out = call(
            functools.partial(place_kernel, splits, at_quarter, tail_rows), "place",
            [arr((rows, width))] * 4,
            [idx, *all_tail])
    else:
        core_in = beside(send_in)
        far_in = across(keep_in[1] + core_in[1])
        total_down, total_up, tail = [
            lax.psum(lax.psum_scatter(g.reshape((blocks, -1) + g.shape[1:]), "blk", scatter_dimension=0, tiled=False), "dp")
            for g in (*feed_grads, *tail)
        ]
        total_down = total_down.reshape(unit, width)
        total_up = lax.all_to_all(total_up, "ulys", 0, 0, tiled=True)
        total_up = total_up.reshape(splits, rows, blocks, unit).transpose(1, 2, 0, 3).reshape(rows, units)
        tail = tail[0]
        total_out = lax.ppermute(tail[near:near + outs], both, to_owner).transpose(1, 0, 2).reshape(rows, width)
        vec = lax.psum(tail[near + outs:near + outs + vecs], "ulys")
        got = jnp.concatenate([tail[:near], tail[near + outs + vecs:]]).reshape(splits, lane_blocks, rows, 128)
        got = lax.all_to_all(got, "ulys", 0, 0, tiled=True).transpose(2, 0, 1, 3).reshape(rows, splits, lane_blocks * 128)
        total_query, total_key, total_value = (
            got[:, :, i * part:(i + 1) * part].reshape(rows, width) for i in range(3)
        )
    (hidden_grad,) = call(
        hidden_kernel, "hidden",
        [arr((tokens, width))],
        [idx, small, base, keep_in, core_in, far_in, middle_grad])

    output = mine[0] + small[3:4] + keep_out[0] + core_out[0] + far_out

    vec = vec.reshape(outs, EXTRA, 128).transpose(1, 0, 2).reshape(EXTRA, width)
    vector = lax.dynamic_slice(vec, (0, (b * splits + u) * rows), (8, rows))
    up_vector = lax.dynamic_slice(vec, (8 + u, b * unit), (1, unit))[0]
    return (
        output,
        hidden_grad,
        total_query,
        vector[0],
        total_key,
        total_value,
        vector[1],
        total_out,
        vector[2],
        total_up,
        up_vector,
        total_down,
        vector[3],
        vector[4],
        vector[5],
        vector[6],
        vector[7],
    )


def solution(mesh):
    tokens = P(("dp", "blk", "ulys"), None)
    matrix = P(("blk", "ulys"), None)
    vector = P(("blk", "ulys"))
    return jax.shard_map(
        local,
        mesh=mesh,
        in_specs=(
            tokens,
            P("dp", None),
            P("dp", "blk"),
            P("dp", "blk"),
            tokens,
            matrix,
            vector,
            matrix,
            matrix,
            vector,
            matrix,
            vector,
            matrix,
            vector,
            matrix,
            vector,
            vector,
            vector,
            vector,
            vector,
        ),
        out_specs=(
            tokens,
            tokens,
            matrix,
            vector,
            matrix,
            matrix,
            vector,
            matrix,
            vector,
            matrix,
            vector,
            matrix,
            vector,
            vector,
            vector,
            vector,
            vector,
        ),
        check_vma=False,
    )
```

```python
import functools
import math

import jax
import jax.numpy as jnp
from jax import lax
from jax.experimental import pallas as pl
from jax.experimental.pallas import tpu as pltpu
from jax.sharding import PartitionSpec as P

HEAD_DIM = 64
FLOOR = -1e30
SQRT_2_PI = 0.7978845608028654
CUBIC = 0.044715
EXTRA = 16
TILE = 256
EDGE = 128
BF = jnp.bfloat16
F32 = jnp.float32
NN = (((1,), (0,)), ((), ()))
NT = (((1,), (1,)), ((), ()))
TN = (((0,), (0,)), ((), ()))
VM = pl.BlockSpec(memory_space=pltpu.VMEM)
SM = pl.BlockSpec(memory_space=pltpu.SMEM)
LIMITS = {"attend_own": 10, "attend_edge": 10, "back_edge": 12, "back_own": 12, "act": 14, "weights": 16, "feed_grads": 12, "place": 8, "hidden": 6, "middle": 6, "last_grads": 16, "fold": 10, "base": 6, "pack_qkv": 8, "pack_feed": 10}


def split(x):
    hi = x.astype(BF)
    return hi, (x - hi.astype(F32)).astype(BF)


def mm(a, b, dims=NN):
    return lax.dot_general(a, b, dims, preferred_element_type=F32)


def mm3(a, b, dims=NN):
    return mm(a[0], b[0], dims) + (mm(a[0], b[1], dims) + mm(a[1], b[0], dims))


def at(start, size, step=8):
    return pl.ds(pl.multiple_of(start, step), size)


def call(kernel, name, outs, ins, scratch=(), flops=0, smem=1, limit=16, wide=False, marks=()):
    inner, count, ins = kernel, len(ins), list(ins) + list(marks)

    def kernel(*refs):
        return inner(*refs[:count], *refs[len(ins):])

    size = sum(math.prod(x.shape) * x.dtype.itemsize for x in list(outs) + list(ins[smem:count]))
    return pl.pallas_call(
        kernel,
        out_shape=tuple(outs),
        in_specs=[SM] * smem + [VM] * (count - smem) + [pl.BlockSpec(memory_space=pl.ANY)] * len(marks),
        out_specs=tuple(SM if x.dtype == jnp.int32 else VM for x in outs),
        scratch_shapes=list(scratch),
        compiler_params=pltpu.CompilerParams(vmem_limit_bytes=(48 if wide else LIMITS.get(name, limit)) << 20),
        cost_estimate=pl.CostEstimate(flops=1, bytes_accessed=1, transcendentals=0),
        name=name,
    )(*ins)


def arr(shape, dtype=F32):
    return jax.ShapeDtypeStruct(tuple(shape), dtype)


def norm(x):
    centred = x - jnp.mean(x, axis=-1, keepdims=True)
    inverse = lax.rsqrt(jnp.mean(centred * centred, axis=-1, keepdims=True) + 1e-05)
    return centred * inverse, inverse


def norm_back(grad, gain, xhat, inverse):
    scaled = grad * gain
    mean = jnp.mean(scaled, axis=-1, keepdims=True)
    lean = jnp.mean(scaled * xhat, axis=-1, keepdims=True)
    return (scaled - mean - xhat * lean) * inverse


def pick(index, choices):
    value = choices[0]
    for i in range(1, len(choices)):
        value = jnp.where(index == i, choices[i], value)
    return value


def first_kernel(count, numbers, *refs):
    for source, target in zip((numbers,) + refs[:count], refs[count:]):
        if target.dtype == jnp.int32:
            for i in range(target.shape[1]):
                target[0, i] = source[0, i]
        else:
            target[...] = source[...]


def pack_qkv_kernel(idx, bounds, codes, halo_codes, small, wq, wk, wv, near, far, *outs):
    first_kernel(4, idx, bounds, codes, halo_codes, small, *outs)
    part = near.shape[2] // 3
    splits = wq.shape[1] // part
    for r in range(splits):
        target, k = (near, r) if r < 2 else (far, r - 2)
        for u in range(splits):

            @pl.when(idx[0, r] == u)
            def _():
                for i, w in enumerate((wq, wk, wv)):
                    target[k, :, i * part:(i + 1) * part] = w[:, u * part:(u + 1) * part]


def pack_feed_kernel(splits, blocks, place, idx, wup, wout, wdown, near, far, down_quarter):
    unit = near.shape[2] // blocks
    for r in range(splits):
        target, k = (near, r) if r < 2 else (far, r - 2)
        for u in range(splits):

            @pl.when(idx[0, r] == u)
            def _():
                for b in range(blocks):
                    lane = (b * splits + u) * unit
                    target[k, :, b * unit:(b + 1) * unit] = wup[:, lane:lane + unit]
    near[2] = wout[...]
    far[2] = wout[...]
    size = down_quarter.shape[0]
    down_quarter[...] = wdown[at(idx[0, place] * size, size), :]


def base_kernel(hidden, embed, small, out):
    tokens = hidden.shape[0]
    out[:tokens, :] = hidden[...] + embed[...]
    out[tokens:, :] = small[...]


def qkv_kernel(pieces, splits, edge, idx, og, *refs):
    base, rest = refs[:splits], refs[splits:]
    count = max(p[0] for p in pieces) + 1
    weights = rest[:count]
    (q_ref, kv_ref, edge_ref, base_ref, small_ref, wh, wl, og_ref, w32, nh, nl) = rest[count:count + 11]
    got = base + weights
    tokens = base[0].shape[0] - EXTRA
    part = q_ref.shape[1]
    rows = w32.shape[0] // len(pieces)
    small = None
    for r in range(splits):
        rest = got[r][tokens:, :]
        small = rest if small is None else small + rest
    small_ref[...] = small
    gain, shift = small[4:5], small[5:6]
    for r in range(splits):
        row = at(idx[0, r] * tokens, tokens, 16)
        x = got[r][:tokens, :]
        base_ref[row, :] = x
        xhat, _ = norm(x)
        nh[row, :], nl[row, :] = split(xhat * gain + shift)
    for i, (n, lead) in enumerate(pieces):
        w32[at(idx[0, splits + i] * rows, rows), :] = got[splits + n][lead, :rows, :]
    wh[...], wl[...] = split(w32[...])
    u = idx[0, 0]
    qb = pick(u, [small[0:1, i * part:(i + 1) * part] for i in range(splits)])
    vb = pick(u, [small[1:2, i * part:(i + 1) * part] for i in range(splits)])
    bias = jnp.concatenate([qb, jnp.zeros_like(qb), vb], axis=1)
    step = nh.shape[0] // 2

    def rows_of(i, _):
        row = at(i * step, step, 16)
        out = mm3((nh[row, :], nl[row, :]), (wh[...], wl[...])) + bias
        q_ref[row, :] = out[:, :part]
        kv_ref[row, :] = out[:, part:]
        return 0

    lax.fori_loop(0, 2, rows_of, 0)
    reach = edge_ref.shape[0]
    edge_ref[...] = kv_ref[at(idx[0, edge], reach), :]
    og_ref[...] = og[...]


def span_hits(seg, i, j):
    return (seg[0, 2 * j + 1] >= seg[0, 2 * i]) & (seg[0, 2 * j] <= seg[0, 2 * i + 1])


def prepare(src, width, first, count, size, pairs, flipped):
    heads = width // HEAD_DIM
    for scratch, start in pairs:
        for h in range(heads):
            hi, lo = split(src[:, start + h * HEAD_DIM:start + (h + 1) * HEAD_DIM])
            scratch[h] = jnp.concatenate([hi, lo, hi], axis=1)
    for j in range(count):
        turned = src[j * size:(j + 1) * size, first:first + width].T
        for h in range(heads):
            hi, lo = split(turned[h * HEAD_DIM:(h + 1) * HEAD_DIM])
            flipped[h, j] = jnp.concatenate([hi, lo], axis=0)


def columns(codes, out, size):
    for j in range(out.shape[0] // size):
        row = codes[1:2, j * size:(j + 1) * size]
        out[j * size:(j + 1) * size, :] = jnp.broadcast_to(row, (128, size)).T


def same_row(i, j):
    return (lax.broadcasted_iota(jnp.int32, (TILE, TILE), 0)
            - lax.broadcasted_iota(jnp.int32, (TILE, TILE), 1)) == (i - j) * TILE


def attend_add(heads, qc, keys, flipped, m_s, l_s, acc, i, j, size, allowed):
    qrow = at(i * TILE, TILE, TILE)
    krow = at(j * size, size, size)
    for h in range(heads):
        s = jnp.where(allowed, mm(keys[h, krow, :], qc[h, qrow, :], NT), FLOOR)
        m_old = m_s[h, i]
        m_new = jnp.maximum(m_old, jnp.max(s, axis=0, keepdims=True))
        p = jnp.where(allowed, jnp.exp(s - m_new), 0.0)
        factor = jnp.exp(m_old - m_new)
        m_s[h, i] = m_new
        l_s[h, i] = l_s[h, i] * factor + jnp.sum(p, axis=0, keepdims=True)
        hi, lo = split(p)
        v128 = flipped[h, j]
        acc[h, i] = acc[h, i] * factor + mm(v128, hi) + mm(v128, lo)


def attend_own_kernel(heads, seg_ref, qcode_ref, kcode_ref, q_ref, kv_ref, qc, m_s, l_s, acc, kc, vt, kcol):
    group, width = q_ref.shape
    nq = group // TILE
    for h in range(heads):
        hi, lo = split(q_ref[:, h * HEAD_DIM:(h + 1) * HEAD_DIM] * HEAD_DIM ** -0.5)
        qc[h] = jnp.concatenate([hi, hi, lo], axis=1)
    prepare(kv_ref, width, width, nq, TILE, [(kc, 0)], vt)
    columns(kcode_ref, kcol, TILE)
    m_s[...] = jnp.full_like(m_s, FLOOR)
    l_s[...] = jnp.zeros_like(l_s)
    acc[...] = jnp.zeros_like(acc)

    def per_q(i, _):
        def per_k(j, _):
            @pl.when(span_hits(seg_ref, i, j))
            def _():
                allowed = kcol[at(j * TILE, TILE, TILE), :1] == qcode_ref[:1, at(i * TILE, TILE, TILE)]
                attend_add(heads, qc, kc, vt, m_s, l_s, acc, i, j, TILE, allowed | same_row(i, j))
            return 0

        lax.fori_loop(0, nq, per_k, 0)
        return 0

    lax.fori_loop(0, nq, per_q, 0)


def attend_edge_kernel(heads, extra, seg_ref, qcode_ref, hcode_ref, halo_ref, qc, m_in, l_in, acc_in, *refs):
    out_ref, wide_ref, lse_ref = refs[extra:extra + 3]
    for source, target in zip(refs[:extra], refs[extra + 3:2 * extra + 3]):
        target[...] = source[...]
    kh, vh, hcol, m_s, l_s, acc = refs[2 * extra + 3:]
    group, width = out_ref.shape
    nq, nh = group // TILE, halo_ref.shape[0] // EDGE
    m_s[...] = m_in[...]
    l_s[...] = l_in[...]
    acc[...] = acc_in[...]
    if nh:
        prepare(halo_ref, width, width, nh, EDGE, [(kh, 0)], vh)
        columns(hcode_ref, hcol, EDGE)

    def per_q(i, _):
        qrow = at(i * TILE, TILE, TILE)

        def per_edge(j, _):
            @pl.when(span_hits(seg_ref, i, nq + j))
            def _():
                allowed = hcol[at(j * EDGE, EDGE, EDGE), :1] == qcode_ref[:1, qrow]
                attend_add(heads, qc, kh, vh, m_s, l_s, acc, i, j, EDGE, allowed)
            return 0

        if nh:
            lax.fori_loop(0, nh, per_edge, 0)
        parts = []
        for h in range(heads):
            total = l_s[h, i]
            parts.append((acc[h, i, :HEAD_DIM] + acc[h, i, HEAD_DIM:]) / total)
            lse_ref[h:h + 1, qrow] = m_s[h, i] + jnp.log(total)
        out_ref[qrow, :] = jnp.concatenate(parts, axis=0).T
        return 0

    lax.fori_loop(0, nq, per_q, 0)
    wide_ref[:, :width] = out_ref[:group // 2, :]
    wide_ref[:, width:] = out_ref[group // 2:, :]


def attend_own(segs, qcode, kcode, q, kv):
    group, width = q.shape
    heads, nq = width // HEAD_DIM, group // TILE
    return call(
        functools.partial(attend_own_kernel, heads), "attend_own",
        [arr((heads, group, 3 * HEAD_DIM), BF), arr((heads, nq, 1, TILE)), arr((heads, nq, 1, TILE)),
         arr((heads, nq, 2 * HEAD_DIM, TILE))],
        [segs, qcode, kcode, q, kv],
        [pltpu.VMEM((heads, group, 3 * HEAD_DIM), BF), pltpu.VMEM((heads, nq, 2 * HEAD_DIM, TILE), BF),
         pltpu.VMEM((group, 128), F32)],
        flops=4 * group * group * width)


def attend_edge(segs, qcode, hcode, halo, state, passed=(), marks=()):
    heads, group, _ = state[0].shape
    reach, width = halo.shape[0], halo.shape[1] // 2
    nq, nh = group // TILE, reach // EDGE
    return call(
        functools.partial(attend_edge_kernel, heads, len(passed)), "attend_edge",
        [arr((group, width)), arr((group // 2, 2 * width)), arr((8, group))] + [arr(x.shape) for x in passed],
        [segs, qcode, hcode, halo, *state, *passed],
        [pltpu.VMEM((heads, reach, 3 * HEAD_DIM), BF), pltpu.VMEM((heads, nh, 2 * HEAD_DIM, EDGE), BF),
         pltpu.VMEM((reach, 128), F32)]
        + [pltpu.VMEM(x.shape, x.dtype) for x in state[1:]],
        flops=2 * group * reach * width, wide=reach > group, marks=marks)


def back_add(heads, qc, q2, dc, d2, dot_s, lse_ref, keys, values, flipped, dqa, dka, dva, i, j, size, allowed):
    qrow = at(i * TILE, TILE, TILE)
    krow = at(j * size, size, size)
    for h in range(heads):
        s = mm(keys[h, krow, :], qc[h, qrow, :], NT)
        p = jnp.exp(jnp.where(allowed, s - lse_ref[h:h + 1, qrow], FLOOR))
        dp = mm(values[h, krow, :], dc[h, qrow, :], NT)
        ds = p * (dp - dot_s[h, :, qrow])
        hi, lo = split(p)
        d128 = d2[h, qrow, :]
        dva[h] += mm(hi, d128) + mm(lo, d128)
        hi, lo = split(ds)
        q128 = q2[h, qrow, :]
        dka[h] += mm(hi, q128) + mm(lo, q128)
        k128 = flipped[h, j]
        dqa[h, i] += mm(k128, hi) + mm(k128, lo)


def back_over(heads, seg_ref, nq, count, size, first, out, dka, dva, visit):
    width = heads * HEAD_DIM

    def folded(acc):
        return jnp.concatenate([acc[h, :, :HEAD_DIM] + acc[h, :, HEAD_DIM:] for h in range(heads)], axis=1)

    def per_k(j, _):
        dka[...] = jnp.zeros_like(dka)
        dva[...] = jnp.zeros_like(dva)

        def per_q(i, _):
            @pl.when(span_hits(seg_ref, i, first + j))
            def _():
                visit(i, j)
            return 0

        lax.fori_loop(0, nq, per_q, 0)
        krow = at(j * size, size, size)
        out[krow, :width] = folded(dka)
        out[krow, width:] = folded(dva)
        return 0

    lax.fori_loop(0, count, per_k, 0)


def back_edge_kernel(heads, splits, idx, seg_ref, qcode_ref, hcode_ref, q_ref, halo_ref, o_ref, lse_ref, qc,
                     oh_ref, ol_ref, *refs):
    mg, (dhalo_ref, q2, dc, d2, dot_s, dqa, gh, gl, kh, vh, kth, hcol, prod_s, dka, dva) = (
        refs[:splits], refs[splits:])
    group, width = q_ref.shape
    nq, nh = group // TILE, halo_ref.shape[0] // EDGE
    tokens = group // splits
    if nh:
        prepare(halo_ref, width, 0, nh, EDGE, [(kh, 0), (vh, width)], kth)
        columns(hcode_ref, hcol, EDGE)
    for h in range(heads):
        hi, lo = split(q_ref[:, h * HEAD_DIM:(h + 1) * HEAD_DIM] * HEAD_DIM ** -0.5)
        q2[h] = jnp.concatenate([hi, lo], axis=1)
    dqa[...] = jnp.zeros_like(dqa)
    wrow = at(idx[0, 0] * width, width, 16)
    w_pair = (oh_ref[wrow, :], ol_ref[wrow, :])
    for r in range(splits):
        row = at(idx[0, r] * tokens, tokens, 16)
        gh[row, :], gl[row, :] = split(mg[r][...])
    step = group // 3

    def rows_of(i, _):
        row = at(i * step, step, 16)
        grad = mm3((gh[row, :], gl[row, :]), w_pair, NT)
        prod_s[row, :] = grad * o_ref[row, :]
        for h in range(heads):
            hi, lo = split(grad[:, h * HEAD_DIM:(h + 1) * HEAD_DIM])
            dc[h, row, :] = jnp.concatenate([hi, hi, lo], axis=1)
            d2[h, row, :] = jnp.concatenate([hi, lo], axis=1)
        return 0

    lax.fori_loop(0, 3, rows_of, 0)
    for i in range(nq):
        rows = slice(i * TILE, (i + 1) * TILE)
        prod = prod_s[rows, :].T
        for h in range(heads):
            dot_s[h, :, rows] = jnp.sum(prod[h * HEAD_DIM:(h + 1) * HEAD_DIM], axis=0, keepdims=True)

    def visit(i, j):
        allowed = hcol[at(j * EDGE, EDGE, EDGE), :1] == qcode_ref[:1, at(i * TILE, TILE, TILE)]
        back_add(heads, qc, q2, dc, d2, dot_s, lse_ref, kh, vh, kth, dqa, dka, dva, i, j, EDGE, allowed)

    if nh:
        back_over(heads, seg_ref, nq, nh, EDGE, nq, dhalo_ref, dka, dva, visit)


def back_own_kernel(heads, seg_ref, qcode_ref, kcode_ref, kv_ref, lse_ref, qc, q2, dc, d2, dot_s, dq_in,
                    dq_ref, dkv_ref, kc, vc, kt, kcol, dqa, dka, dva):
    group, width = dq_ref.shape
    nq = group // TILE
    prepare(kv_ref, width, 0, nq, TILE, [(kc, 0), (vc, width)], kt)
    columns(kcode_ref, kcol, TILE)
    dqa[...] = dq_in[...]

    def visit(i, j):
        allowed = kcol[at(j * TILE, TILE, TILE), :1] == qcode_ref[:1, at(i * TILE, TILE, TILE)]
        back_add(heads, qc, q2, dc, d2, dot_s, lse_ref, kc, vc, kt, dqa, dka, dva, i, j, TILE, allowed | same_row(i, j))

    back_over(heads, seg_ref, nq, nq, TILE, 0, dkv_ref, dka, dva, visit)
    for i in range(nq):
        parts = [(dqa[h, i, :HEAD_DIM] + dqa[h, i, HEAD_DIM:]) * HEAD_DIM ** -0.5 for h in range(heads)]
        dq_ref[i * TILE:(i + 1) * TILE, :] = jnp.concatenate(parts, axis=0).T


def attend_back_edge(idx, segs, qcode, hcode, q, halo, o, lse, qc, oh, ol, mg):
    group, width = q.shape
    reach = halo.shape[0]
    heads = width // HEAD_DIM
    nq, nh = group // TILE, reach // EDGE
    full = oh.shape[1]
    H3, H2 = 3 * HEAD_DIM, 2 * HEAD_DIM
    return call(
        functools.partial(back_edge_kernel, heads, len(mg)), "back_edge",
        [arr((reach, 2 * width)), arr((heads, group, H2), BF), arr((heads, group, H3), BF), arr((heads, group, H2), BF),
         arr((heads, 1, group)), arr((heads, nq, H2, TILE)), arr((group, full), BF), arr((group, full), BF)],
        [idx, segs, qcode, hcode, q, halo, o, lse, qc, oh, ol, *mg],
        [
            pltpu.VMEM((heads, reach, H3), BF),
            pltpu.VMEM((heads, reach, H3), BF),
            pltpu.VMEM((heads, nh, H2, EDGE), BF),
            pltpu.VMEM((reach, 128), F32),
            pltpu.VMEM((group, width), F32),
            pltpu.VMEM((heads, EDGE, H2), F32),
            pltpu.VMEM((heads, EDGE, H2), F32),
        ],
        flops=2 * group * full * width, smem=2, wide=reach > group)


def attend_back_own(segs, qcode, kcode, kv, lse, qc, q2, dc, d2, dot_s, dqa, marks):
    heads, group, _ = qc.shape
    width = kv.shape[1] // 2
    nq = group // TILE
    H3, H2 = 3 * HEAD_DIM, 2 * HEAD_DIM
    return call(
        functools.partial(back_own_kernel, heads), "back_own",
        [arr((group, width)), arr((group, 2 * width))],
        [segs, qcode, kcode, kv, lse, qc, q2, dc, d2, dot_s, dqa],
        [
            pltpu.VMEM((heads, group, H3), BF),
            pltpu.VMEM((heads, group, H3), BF),
            pltpu.VMEM((heads, nq, H2, TILE), BF),
            pltpu.VMEM((group, 128), F32),
            pltpu.VMEM((heads, nq, H2, TILE), F32),
            pltpu.VMEM((heads, TILE, H2), F32),
            pltpu.VMEM((heads, TILE, H2), F32),
        ],
        flops=10 * group * group * width, marks=marks)


def weights_kernel(full, splits, idx, *refs):
    count = max([p[0] for p in full]) + 1
    weights, (uh, ul, oh, ol, u32, o32) = refs[:count], refs[count:count + 6]
    got = weights
    owners = len(full)
    rows = u32.shape[0] // owners
    for i, (n, lead) in enumerate(full):
        row = at(idx[0, splits + i] * rows, rows)
        u32[row, :] = got[n][lead]
        o32[row, :] = got[n][2]
    uh[...], ul[...] = split(u32[...])
    oh[...], ol[...] = split(o32[...])


def act_kernel(splits, whole, first, place, idx, *refs):
    got, (gh, gl, dh, dl, act_ref) = refs[:-5], refs[-5:]
    tokens = got[0].shape[0]
    down = got[splits:]
    unit = down[0].shape[0]
    blocks = dh.shape[0] // unit
    for r in range(splits):
        row = at(idx[0, r] * tokens, tokens, 16)
        gh[row, :], gl[row, :] = split(got[r][...])
    for i in range(blocks):
        if i < whole:
            row = at(idx[0, first + i] * unit, unit, 16)
            dh[row, :], dl[row, :] = split(down[i][...])
            continue
        size = unit // 4
        for z in range(4):
            quarter = idx[0, place] ^ (0, 3, 1, 2)[z]
            row = at(idx[0, first + i] * unit + quarter * size, size, 16)
            dh[row, :], dl[row, :] = split(down[whole + 4 * (i - whole) + z][...])
    step = gh.shape[0] // 2

    def rows_of(i, _):
        row = at(i * step, step, 16)
        act_ref[row, :] = mm3((gh[row, :], gl[row, :]), (dh[...], dl[...]), NT)
        return 0

    lax.fori_loop(0, 2, rows_of, 0)


def feed_kernel(splits, idx, small, base, *refs):
    (oh, ol, uh, ul, act, keep, send, mine, inv_ref, ah, al, ph, plo, mh, ml, vec, b32, x2, g32, r32) = (
        refs[splits:splits + 20])
    att = refs[:splits]
    tokens = keep.shape[1]
    group = b32.shape[0]
    part = att[0].shape[1] // 2
    gain, shift = small[6:7, :], small[7:8, :]
    up_bias = small[pl.ds(8 + idx[0, 0], 1), :]
    vec[...] = jnp.zeros_like(vec)
    step = group // 2

    def rows_of(i, _):
        row = at(i * step, step, 16)
        middle = base[row, :] + small[2:3, :]
        for s in range(splits):
            wrow = at(idx[0, s] * part, part, 16)
            piece = jnp.where(i == 0, att[s][:, :part], att[s][:, part:])
            middle = middle + mm3(split(piece), (oh[wrow, :], ol[wrow, :]))
        b32[row, :] = middle
        xhat, inverse = norm(middle)
        x2[row, :] = xhat
        g32[row, :] = jnp.broadcast_to(inverse, g32[row, :].shape)
        pair = split(xhat * gain + shift)
        mh[row, :], ml[row, :] = pair
        pre = mm3(pair, (uh[...], ul[...])) + up_bias
        square = pre * pre
        curve = jnp.tanh(SQRT_2_PI * (pre + CUBIC * square * pre))
        half = 0.5 * (1.0 + curve)
        ah[row, :], al[row, :] = split(pre * half)
        slope = half + 0.5 * pre * (1.0 - curve * curve) * SQRT_2_PI * (1.0 + 3.0 * CUBIC * square)
        grad = act[row, :] * slope
        pair = split(grad)
        ph[row, :], plo[row, :] = pair
        back = mm3(pair, (uh[...], ul[...]), NT)
        vec[0:1, :] += jnp.sum(grad, axis=0, keepdims=True)
        vec[1:2, :] += jnp.sum(back * xhat, axis=0, keepdims=True)
        vec[2:3, :] += jnp.sum(back, axis=0, keepdims=True)
        r32[row, :] = back
        return 0

    lax.fori_loop(0, 2, rows_of, 0)

    def pairs_of(h, _):
        keep[h] = r32[at(idx[0, 2 * h] * tokens, tokens), :]
        send[h] = r32[at(idx[0, 2 * h + 1] * tokens, tokens), :]
        return 0

    lax.fori_loop(0, splits // 2, pairs_of, 0)
    row = at(idx[0, 0] * tokens, tokens)
    mine[0] = b32[row, :]
    mine[1] = x2[row, :]
    inv_ref[...] = g32[row, :]


def feed_grads_kernel(splits, first, down_rows, up_rows, idx, ah, al, ph, plo, mh, ml, gh, gl, dh, dl,
                      keep, send, *refs):
    outs, r32 = refs[:-1], refs[-1]
    downs, ups = outs[:len(outs) // 2], outs[len(outs) // 2:]
    tokens = keep.shape[1]
    step = r32.shape[0] // 2

    third = r32.shape[0] // 3

    def left(a, b):
        def rows_of(i, _):
            lane = at(i * third, third, 128)
            r32[at(i * third, third), :] = mm3((a[0][:, lane], a[1][:, lane]), (b[0][...], b[1][...]), TN)
            return 0

        lax.fori_loop(0, 3, rows_of, 0)

    def deal(targets, rows, place):
        for target in targets:
            def one(c, _, target=target, place=place):
                target[c] = r32[at(idx[0, place + c], rows), :]
                return 0

            lax.fori_loop(0, target.shape[0], one, 0)
            place += target.shape[0]
        return place

    left((ah, al), (gh, gl))
    place = deal(downs, down_rows, first)
    left((mh, ml), (ph, plo))
    deal(ups, up_rows, place)

    def rows_of(i, _):
        row = at(i * step, step, 16)
        r32[row, :] = mm3((ah[row, :], al[row, :]), (dh[...], dl[...]))
        return 0

    lax.fori_loop(0, 2, rows_of, 0)

    def pairs_of(h, _):
        keep[h] = r32[at(idx[0, 2 * h] * tokens, tokens), :]
        send[h] = r32[at(idx[0, 2 * h + 1] * tokens, tokens), :]
        return 0

    lax.fori_loop(0, splits // 2, pairs_of, 0)


def middle_kernel(small, keep, core, far, og, mine, inv, mg_ref, vec_ref):
    grad = keep[0] + core[0] + far[...]
    out = og[...] + norm_back(grad, small[6:7, :], mine[1], inv[:, :1])
    mg_ref[...] = out
    vec_ref[...] = jnp.zeros_like(vec_ref)
    vec_ref[0:1, :] = jnp.sum(out, axis=0, keepdims=True)
    vec_ref[1:2, :] = jnp.sum(og[...], axis=0, keepdims=True)


def last_grads_kernel(splits, first, edge, rows, idx, small, dq, dkv, back, base, att, vec1, vec2, gh, gl, wh, wl,
                      keep, send, *refs):
    tails, (qh, ql, xhat, r32, o32, s32, n32, vec) = refs[:-8], refs[-8:]
    part = dq.shape[1]
    width = xhat.shape[1]
    tokens = keep.shape[1]
    u = idx[0, 0]
    s32[:, :part] = dq[...]
    s32[:, part:] = dkv[...]
    s32[at(idx[0, edge], back.shape[0]), part:] += back[...]
    qkv = s32[...]
    qh[...], ql[...] = split(qkv)
    sums = jnp.sum(qkv, axis=0, keepdims=True)
    xhat[...], _ = norm(base[...])
    vec[...] = jnp.zeros_like(vec)
    step = n32.shape[0] // 2

    def rows_of(i, _):
        row = at(i * step, step, 16)
        grad = mm3((qh[row, :], ql[row, :]), (wh[...], wl[...]), NT)
        n32[row, :] = grad
        vec[4:5, :] += jnp.sum(grad * xhat[row, :], axis=0, keepdims=True)
        vec[5:6, :] += jnp.sum(grad, axis=0, keepdims=True)
        return 0

    lax.fori_loop(0, 2, rows_of, 0)

    def pairs_of(h, _):
        keep[h] = n32[at(idx[0, 2 * h] * tokens, tokens), :]
        send[h] = n32[at(idx[0, 2 * h + 1] * tokens, tokens), :]
        return 0

    lax.fori_loop(0, splits // 2, pairs_of, 0)
    step = width // 3

    def lanes_of(i, _):
        lane = at(i * step, step, 128)
        pair = split(xhat[:, lane] * small[4:5, lane] + small[5:6, lane])
        r32[lane, :] = mm3(pair, (qh[...], ql[...]), TN)
        return 0

    lax.fori_loop(0, 3, lanes_of, 0)
    o32[...] = mm3(split(att[...]), (gh[...], gl[...]), TN)
    for i in range(splits):

        @pl.when(u == i)
        def _():
            vec[0:1, i * part:(i + 1) * part] = sums[:, :part]
            vec[1:2, i * part:(i + 1) * part] = sums[:, 2 * part:]

    vec[2:4, :] = vec2[0:2, :]
    vec[6:8, :] = vec1[1:3, :]
    vec[pl.ds(8 + u, 1), :] = vec1[0:1, :]
    wide = r32.shape[1]
    outs = width // 128
    vecs = outs * EXTRA // rows
    lane_blocks = -(-wide // 128)
    spare = lane_blocks * 128 - wide
    near = 2 * lane_blocks
    total = sum(t.shape[0] for t in tails)
    spot = 0
    for t in tails:
        def one(c, _, t=t, spot=spot):
            for j in range(splits):
                row = at(idx[0, first + (spot + c) * splits + j], rows)
                start = j * lane_blocks + (outs + vecs if j >= 2 else 0)
                for k in range(lane_blocks - 1):
                    t[c, start + k] = r32[row, k * 128:(k + 1) * 128]
                k = lane_blocks - 1
                t[c, start + k, :, :128 - spare] = r32[row, k * 128:]
                t[c, start + k, :, 128 - spare:] = jnp.zeros((rows, spare), F32)
            row = at(idx[0, first + total * splits + spot + c], rows)
            for k in range(outs):
                t[c, near + k] = o32[row, k * 128:(k + 1) * 128]
            for k in range(outs * EXTRA // 8):
                block, low = divmod(8 * k, rows)
                lane, high = divmod(8 * k, EXTRA)
                t[c, near + outs + block, low:low + 8, :] = vec[high:high + 8, lane * 128:(lane + 1) * 128]
            return 0

        lax.fori_loop(0, t.shape[0], one, 0)
        spot += t.shape[0]


def hidden_kernel(idx, small, base, keep, core, far, mg, out):
    tokens = mg.shape[0]
    xhat, inverse = norm(base[at(idx[0, 0] * tokens, tokens), :])
    out[...] = mg[...] + norm_back(keep[0] + core[0] + far[...], small[4:5, :], xhat, inverse)


def fold_kernel(count, *refs):
    keeps, gots, outs = refs[:count], refs[count:2 * count], refs[2 * count:]
    for i in range(count):
        stay, go = outs[2 * i:2 * i + 2]
        half = stay.shape[0]
        stay[...] = keeps[i][:half] + gots[i][:half]
        go[...] = keeps[i][half:] + gots[i][half:]


def fold(keeps, gots, marks=()):
    outs = []
    for keep in keeps:
        outs += [arr((keep.shape[0] // 2,) + keep.shape[1:])] * 2
    got = call(functools.partial(fold_kernel, len(keeps)), "fold", outs, [*keeps, *gots], smem=0, marks=marks)
    return got[::2], got[1::2]


def message_kernel(near, stop, vecs, part, far, out):
    blocks = near // 2
    out[:blocks] = part[blocks:near]
    out[blocks:blocks + vecs] = part[stop:stop + vecs] + far[:vecs]
    out[blocks + vecs:] = far[vecs + blocks:]


def place_kernel(splits, first, rows, idx, *refs):
    pieces, (gq, gk, gv, go) = refs[:-4], refs[-4:]
    part = gq.shape[1] // splits
    for z, piece in enumerate(pieces):
        row = at(idx[0, first + z] * rows, rows)
        count = gq.shape[1] // 128
        for k in range(count):
            go[row, k * 128:(k + 1) * 128] = piece[5 * splits + k]
        for i in range(splits):
            whole = jnp.concatenate([piece[5 * idx[0, i] + k] for k in range(5)], axis=1)
            for n, out in enumerate((gq, gk, gv)):
                out[row, i * part:(i + 1) * part] = whole[:, n * part:(n + 1) * part]


def place_feed_kernel(splits, blocks, unit, first, idx, *refs):
    pieces, (gd, gu) = refs[:-2], refs[-2:]
    downs, ups = pieces[:len(pieces) // 2], pieces[len(pieces) // 2:]
    for z, (down, up) in enumerate(zip(downs, ups)):
        gd[at(idx[0, first + z] * down.shape[0], down.shape[0]), :] = down[...]
        rows = up.shape[1]
        row = at(idx[0, first + z] * rows, rows)
        for i in range(splits):
            for n in range(blocks):
                start = (n * splits + i) * unit
                gu[row, start:start + unit] = up[idx[0, i], :, n * unit:(n + 1) * unit]


def swap(value, axis, mask):
    count = lax.axis_size(axis)
    return lax.ppermute(value, axis, [(i, i ^ mask) for i in range(count)])


def across(value):
    return swap(value, "ulys", 2)


def beside(value):
    return swap(value, "ulys", 1)


def over(value):
    return swap(value, "blk", 1)


def gather_splits(value):
    far = across(value)
    return [value, beside(value), far, beside(far)]


def collect(value):
    near = swap(value, "dp", 3)
    return [value, near, swap(value, "dp", 1), swap(near, "dp", 1)]


def halo_moves(group, reach, blocks):
    moves = []
    shift = 1
    while reach > 0 and shift < blocks:
        rows = min(group, reach)
        moves.append((rows, True, [(i, i - shift) for i in range(shift, blocks)]))
        moves.append((rows, False, [(i, i + shift) for i in range(blocks - shift)]))
        reach -= rows
        shift += 1
    return moves


def halo_get(value, reach, axis=0):
    blocks, group = lax.axis_size("blk"), value.shape[axis]
    parts = []
    for rows, right, moves in halo_moves(group, reach, blocks):
        start = 0 if right else group - rows
        parts.append(lax.ppermute(lax.slice_in_dim(value, start, start + rows, axis=axis), "blk", moves))
    return jnp.concatenate(parts, axis=axis)


def halo_add(value, halo, reach):
    blocks, group = lax.axis_size("blk"), value.shape[0]
    start = 0
    for rows, right, moves in halo_moves(group, reach, blocks):
        back = lax.ppermute(halo[start:start + rows], "blk", [(j, i) for i, j in moves])
        start += rows
        room = group - rows
        value = value + jnp.pad(back, ((0, room), (0, 0)) if right else ((room, 0), (0, 0)))
    return value


def local(
    hidden,
    time_embed,
    segment_ids,
    key_valid,
    out_grad,
    w_query,
    b_query,
    w_key,
    w_value,
    b_value,
    w_out,
    b_out,
    w_up,
    b_up,
    w_down,
    b_down,
    pre_gain,
    pre_shift,
    mlp_gain,
    mlp_shift,
):
    blocks, splits = lax.axis_size("blk"), lax.axis_size("ulys")
    b, u, d = (lax.axis_index(name) for name in ("blk", "ulys", "dp"))
    both = ("blk", "ulys")
    owners = blocks * splits
    tokens, width = hidden.shape
    group = tokens * splits
    part = width // splits
    rows = w_query.shape[0]
    unit = w_down.shape[0]
    units = unit * owners
    share = units // splits
    reach = group * blocks // 4
    fast = blocks == 2 and splits == 4 and lax.axis_size("dp") == 4 and reach <= group and group == width

    if fast:
        f1, f3 = (d ^ (d >> 1)) & 1, d >> 1
        quarters = [2 * (f1 ^ s) + (f3 ^ t) for s in range(2) for t in range(2)]
        owner_list = [(b ^ x) * splits + (u ^ r) for x in range(2) for r in range(4)]
        block_list = [b, b ^ 1]
        edge_row = jnp.where(b == 0, group - reach, 0)
        down_rows, up_rows, tail_rows = unit // 4, rows // 4, rows // 4
        down_table = [(b ^ x) * unit + q * down_rows for x in range(2) for q in quarters]
        up_table = [
            ((b ^ x) * splits + (u ^ r)) * rows + q * up_rows for q in quarters for x in range(2) for r in range(4)
        ]
        tail_table = [
            ((b ^ x) * splits + (u ^ r)) * rows + q * tail_rows for x in range(2) for q in quarters for r in range(4)
        ] + [(b ^ x) * rows + q * tail_rows for x in range(2) for q in quarters]
        chunks = 8
    else:
        quarters = []
        owner_list = list(range(owners))
        block_list = list(range(blocks))
        edge_row = 0
        down_rows, up_rows, tail_rows = unit, rows, rows
        down_table = [i * unit for i in range(blocks)]
        up_table = [i * rows for i in range(owners)]
        tail_table = up_table + [i * rows for i in range(blocks)]
        chunks = blocks
    entries, spots = [], []
    for values in (
        [u ^ r for r in range(splits)], owner_list, block_list, [d], [edge_row], down_table + up_table, tail_table,
        quarters,
    ):
        spots.append(len(entries))
        entries += values
    _, _, at_block, at_d, at_edge, at_feed, at_tail, at_quarter = spots
    idx = jnp.stack([jnp.asarray(v, jnp.int32) for v in entries]).reshape(1, -1)

    segments = segment_ids[0] + 1
    codes = jnp.stack([segments, jnp.where(key_valid[0] == 1, segments, 0)]).astype(F32)
    small = jnp.stack([b_query, b_value, b_out, b_down, pre_gain, pre_shift, mlp_gain, mlp_shift])
    small = lax.dynamic_update_slice(jnp.zeros((EXTRA, width), F32), small, (0, (b * splits + u) * rows))
    small = lax.dynamic_update_slice(small, b_up[None], (8 + u, b * unit))
    if fast:
        small = lax.dynamic_update_slice(small, codes, (12, 0))
        other = over(small)
        small = small + other
        halo_codes = jnp.where(b == 0, other[12:14, :reach], other[12:14, group - reach:group])
    else:
        small = lax.psum(small, "blk")
        halo_codes = halo_get(codes, reach, axis=1)
    tiles = codes[0].reshape(-1, TILE)
    edges = halo_codes[0].reshape(-1, EDGE)
    bounds = jnp.concatenate(
        [
            jnp.stack([tiles[:, 0], tiles[:, -1]], axis=1).reshape(-1),
            jnp.stack([jnp.min(jnp.where(edges == 0, 1e6, edges), axis=1), jnp.max(edges, axis=1)], axis=1).reshape(-1),
        ]
    ).astype(jnp.int32).reshape(1, -1)
    def make_base(marks):
        return call(
            base_kernel, "base", [arr((tokens + EXTRA, width))], [hidden, time_embed, small], smem=0, marks=marks)[0]

    if fast:
        tables = [idx, bounds, codes, halo_codes, small]
        near, far, *tables = call(
            pack_qkv_kernel, "pack_qkv",
            [arr((2, rows, 3 * part))] * 2 + [arr(x.shape, x.dtype) for x in tables],
            [*tables, w_query, w_key, w_value], smem=2)
        idx, bounds, codes, halo_codes, small = tables
        pieces = [(i, i % 2) for i in range(8)]
        far = across(far)
        near_over = over(near)
        base = make_base([far, near_over])
        far_base = across(base)
        qkv_arrays = [near, beside(near), far, beside(far)]
        near = near_over
        far = over(far)
        qkv_arrays += [near, beside(near), far, beside(far)]
        base_all = [base, beside(base), far_base, beside(far_base)]
        near2, far2, down_quarter = call(
            functools.partial(pack_feed_kernel, splits, blocks, at_d), "pack_feed",
            [arr((3, rows, share))] * 2 + [arr((unit // 4, width))],
            [idx, w_up, w_out, w_down], marks=[far])
        down_quarter = over(down_quarter)
        far2 = across(far2)
        feed_arrays = [near2, beside(near2), far2, beside(far2)]
        near2 = over(near2)
        feed_arrays += [near2, beside(near2)]
        whole = 1
    else:
        cut = jnp.stack([w_query, w_key, w_value], axis=1).reshape(rows, 3, splits, part)
        cut = cut.transpose(2, 0, 1, 3).reshape(splits, rows, 3 * part)
        cut = jnp.broadcast_to(cut[None], (blocks,) + cut.shape).reshape(owners, rows, 3 * part)
        got = lax.all_to_all(cut, both, 0, 0, tiled=True)
        qkv_arrays = [got[i:i + 1] for i in range(owners)]
        cut = w_up.reshape(rows, blocks, splits, unit).transpose(2, 0, 1, 3).reshape(splits, rows, share)
        cut = jnp.broadcast_to(cut[None], (blocks,) + cut.shape).reshape(owners, rows, share)
        got = lax.all_to_all(cut, both, 0, 0, tiled=True)
        outs = lax.all_gather(w_out, both, axis=0, tiled=False)
        feed_arrays = [jnp.stack([got[i], got[i], outs[i]]) for i in range(owners)]
        pieces = [(i, 0) for i in range(owners)]
        whole = blocks
        base = make_base([])
        base_all = gather_splits(base)
        gathered = lax.all_gather(w_down, "blk", axis=0, tiled=False)
        down = [gathered[i] for i in range(blocks)]

    query_codes, key_codes, edge_codes = codes, codes, halo_codes
    query, key_value, edge_kv, base, small, qkv_hi, qkv_lo, own_grad = call(
        functools.partial(qkv_kernel, pieces, splits, at_edge), "qkv",
        [arr((group, part)), arr((group, 2 * part)), arr((reach if fast else 8, 2 * part)), arr((group, width)),
         arr((EXTRA, width)), arr((width, 3 * part), BF), arr((width, 3 * part), BF), arr((tokens, width))],
        [idx, out_grad, *base_all, *qkv_arrays],
        [pltpu.VMEM((width, 3 * part), F32), pltpu.VMEM((group, width), BF), pltpu.VMEM((group, width), BF)],
        flops=2 * group * width * 3 * part)
    halo = over(edge_kv) if fast else halo_get(key_value, reach)
    state = attend_own(bounds, query_codes, key_codes, query, key_value)
    grads = gather_splits(own_grad)
    if fast:
        down = [w_down, down_quarter] + [swap(down_quarter, "dp", mask) for mask in (3, 1, 2)]
        attended, attended_wide, lse, far2 = attend_edge(bounds, query_codes, edge_codes, halo, state, (far2,), [*down[2:], grads[2], near2])
        far2 = over(far2)
        feed_arrays += [far2, beside(far2)]
    else:
        attended, attended_wide, lse = attend_edge(bounds, query_codes, edge_codes, halo, state)
    attended_all = gather_splits(attended_wide)
    og_hi, og_lo, down_hi, down_lo, act_grad = call(
        functools.partial(act_kernel, splits, whole, at_block, at_d), "act",
        [arr((group, width), BF)] * 2 + [arr((share, width), BF)] * 2 + [arr((group, share))],
        [idx, *grads, *down],
        flops=2 * group * width * share, marks=[attended_all[2]])
    up_hi, up_lo, out_hi, out_lo = call(
        functools.partial(weights_kernel, pieces, splits), "weights",
        [arr((width, share), BF)] * 2 + [arr((width, width), BF)] * 2,
        [idx, *feed_arrays],
        [pltpu.VMEM((width, share), F32), pltpu.VMEM((width, width), F32)], marks=[act_grad])

    pair = [arr((group, share), BF)] * 2
    keep, send, mine, inverse2, act_hi, act_lo, pre_hi, pre_lo, in_hi, in_lo, vec_feed = call(
        functools.partial(feed_kernel, splits), "feed",
        [arr((2, tokens, width))] * 2 + [arr((2, tokens, width)), arr((tokens, 128))] + pair * 2
        + [arr((group, width), BF)] * 2 + [arr((8, width))],
        [idx, small, base, *attended_all, out_hi, out_lo, up_hi, up_lo, act_grad],
        [pltpu.VMEM((group, width), F32), pltpu.VMEM((group, width), F32), pltpu.VMEM((group, 128), F32),
         pltpu.VMEM((group, width), F32)],
        flops=2 * group * width * (width + 2 * share))
    core = beside(send)
    near_sum = keep[1] + core[1]
    far_sum = across(near_sum)

    if fast:
        feed_outs = [arr((4, down_rows, width))] * 2 + [arr((8 * splits // 2, up_rows, share))] * 2
    else:
        feed_outs = [arr((blocks, down_rows, width)), arr((owners, up_rows, share))]
    keep_out, send_out, *feed_grads = call(
        functools.partial(feed_grads_kernel, splits, at_feed, down_rows, up_rows), "feed_grads",
        [arr((2, tokens, width))] * 2 + feed_outs,
        [idx, act_hi, act_lo, pre_hi, pre_lo, in_hi, in_lo, og_hi, og_lo, down_hi, down_lo],
        [pltpu.VMEM((group, width), F32)],
        flops=6 * group * width * share, marks=[near_sum])
    if fast:
        down_keep, down_send, up_keep, up_send = feed_grads
        down_got = over(down_send)
        up_got = swap(up_send, "dp", 1)

    middle_grad, vec_middle = call(
        middle_kernel, "middle",
        [arr((tokens, width)), arr((8, width))],
        [small, keep, core, far_sum, out_grad, mine, inverse2], smem=0, marks=[keep_out])
    middle_all = gather_splits(middle_grad)

    halo_grad, q2, dc, d2, dots, dq_part, mg_hi, mg_lo = attend_back_edge(
        idx, bounds, query_codes, edge_codes, query, halo, attended, lse, state[0], out_hi, out_lo, middle_all)
    if fast:
        returned = over(halo_grad)
        (down_keep, up_keep), (down_send, up_send) = fold((down_keep, up_keep), (down_got, up_got), [halo_grad])
        down_got = swap(down_send, "dp", 1)
        up_got = swap(up_send, "dp", 3)
        own_marks = [down_keep]
    else:
        own_marks = []
    query_grad, kv_grad = attend_back_own(
        bounds, query_codes, key_codes, key_value, lse, state[0], q2, dc, d2, dots, dq_part, own_marks)
    if not fast:
        kv_grad = halo_add(kv_grad, halo_grad, reach)
        returned = jnp.zeros((8, 2 * part), F32)

    core_out = beside(send_out)
    far_out = across(keep_out[1] + core_out[1])
    lane_blocks = -(-3 * part // 128)
    outs, vecs = width // 128, width // 128 * EXTRA // tail_rows
    total_blocks = splits * lane_blocks + outs + vecs
    tail_outs = [arr((2, total_blocks, tail_rows, 128))] * 4 if fast else [arr((blocks, total_blocks, tail_rows, 128))]
    keep_in, send_in, *tail = call(
        functools.partial(last_grads_kernel, splits, at_tail, at_edge, tail_rows), "last_grads",
        [arr((2, tokens, width))] * 2 + tail_outs,
        [idx, small, query_grad, kv_grad, returned, base, attended, vec_feed, vec_middle, mg_hi, mg_lo, qkv_hi, qkv_lo],
        [pltpu.VMEM((group, 3 * part), BF), pltpu.VMEM((group, 3 * part), BF), pltpu.VMEM((group, width), F32),
         pltpu.VMEM((width, 3 * part), F32), pltpu.VMEM((part, width), F32), pltpu.VMEM((group, 3 * part), F32),
         pltpu.VMEM((group, width), F32), pltpu.VMEM((EXTRA, width), F32)],
        flops=2 * group * width * 7 * part, marks=[far_out])
    to_owner = [(i * splits + j, j * blocks + i) for i in range(blocks) for j in range(splits)]
    near = 2 * lane_blocks
    if fast:
        tail_near, tail_far, send_near, send_far = tail
        got_far = over(send_far)
        got_near = over(send_near)
        core_in = beside(send_in)
        far_in = across(keep_in[1] + core_in[1])

        (down_keep, up_keep), (down_send, up_send) = fold((down_keep, up_keep), (down_got, up_got), [keep_in])
        down_got = swap(down_send, "dp", 3)
        up_got = over(up_send)
        tail_got = swap(tail_far + got_far, "dp", 1)
        tail_near = tail_near + got_near
        part_down = (down_keep + down_got)[0]
        part_up = up_keep + up_got
        far_up = across(part_up[2:])
        core_up = beside(jnp.stack([part_up[1], far_up[1]]))
        part_up = jnp.stack([part_up[0], core_up[0], far_up[0], core_up[1]])
        all_down = collect(part_down)
        all_up = collect(part_up)
        (tail_keep,), (tail_send,) = fold((tail_near,), (tail_got,), [all_down[1], all_down[2], all_up[1], far_in])
        part_tail = (tail_keep + swap(tail_send, "dp", 3))[0]

        far_tail = across(part_tail[near + outs:])
        message, = call(
            functools.partial(message_kernel, near, near + outs, vecs), "message", [arr(far_tail.shape)],
            [part_tail, far_tail], smem=0, marks=[])
        core_tail = beside(message)
        vec = part_tail[near + outs:near + outs + vecs] + far_tail[:vecs] + core_tail[lane_blocks:lane_blocks + vecs]
        owned = lax.ppermute(part_tail[near:near + outs], both, to_owner)
        part_tail = jnp.concatenate([
            part_tail[:lane_blocks], core_tail[:lane_blocks], far_tail[vecs:vecs + lane_blocks],
            core_tail[lane_blocks + vecs:], owned])
        all_tail = collect(part_tail)
        total_down, total_up = call(
            functools.partial(place_feed_kernel, splits, blocks, unit, at_quarter), "place_feed",
            [arr((unit, width)), arr((rows, units))],
            [idx, *all_down, *all_up])
        total_query, total_key, total_value, total_out = call(
            functools.partial(place_kernel, splits, at_quarter, tail_rows), "place",
            [arr((rows, width))] * 4,
            [idx, *all_tail])
    else:
        core_in = beside(send_in)
        far_in = across(keep_in[1] + core_in[1])
        total_down, total_up, tail = [
            lax.psum(lax.psum_scatter(g.reshape((blocks, -1) + g.shape[1:]), "blk", scatter_dimension=0, tiled=False), "dp")
            for g in (*feed_grads, *tail)
        ]
        total_down = total_down.reshape(unit, width)
        total_up = lax.all_to_all(total_up, "ulys", 0, 0, tiled=True)
        total_up = total_up.reshape(splits, rows, blocks, unit).transpose(1, 2, 0, 3).reshape(rows, units)
        tail = tail[0]
        total_out = lax.ppermute(tail[near:near + outs], both, to_owner).transpose(1, 0, 2).reshape(rows, width)
        vec = lax.psum(tail[near + outs:near + outs + vecs], "ulys")
        got = jnp.concatenate([tail[:near], tail[near + outs + vecs:]]).reshape(splits, lane_blocks, rows, 128)
        got = lax.all_to_all(got, "ulys", 0, 0, tiled=True).transpose(2, 0, 1, 3).reshape(rows, splits, lane_blocks * 128)
        total_query, total_key, total_value = (
            got[:, :, i * part:(i + 1) * part].reshape(rows, width) for i in range(3)
        )
    (hidden_grad,) = call(
        hidden_kernel, "hidden",
        [arr((tokens, width))],
        [idx, small, base, keep_in, core_in, far_in, middle_grad])

    output = mine[0] + small[3:4] + keep_out[0] + core_out[0] + far_out

    vec = vec.reshape(outs, EXTRA, 128).transpose(1, 0, 2).reshape(EXTRA, width)
    vector = lax.dynamic_slice(vec, (0, (b * splits + u) * rows), (8, rows))
    up_vector = lax.dynamic_slice(vec, (8 + u, b * unit), (1, unit))[0]
    return (
        output,
        hidden_grad,
        total_query,
        vector[0],
        total_key,
        total_value,
        vector[1],
        total_out,
        vector[2],
        total_up,
        up_vector,
        total_down,
        vector[3],
        vector[4],
        vector[5],
        vector[6],
        vector[7],
    )


def solution(mesh):
    tokens = P(("dp", "blk", "ulys"), None)
    matrix = P(("blk", "ulys"), None)
    vector = P(("blk", "ulys"))
    return jax.shard_map(
        local,
        mesh=mesh,
        in_specs=(
            tokens,
            P("dp", None),
            P("dp", "blk"),
            P("dp", "blk"),
            tokens,
            matrix,
            vector,
            matrix,
            matrix,
            vector,
            matrix,
            vector,
            matrix,
            vector,
            matrix,
            vector,
            vector,
            vector,
            vector,
            vector,
        ),
        out_specs=(
            tokens,
            tokens,
            matrix,
            vector,
            matrix,
            matrix,
            vector,
            matrix,
            vector,
            matrix,
            vector,
            matrix,
            vector,
            vector,
            vector,
            vector,
            vector,
        ),
        check_vma=False,
    )
```

```python
import functools
import math

import jax
import jax.numpy as jnp
from jax import lax
from jax.experimental import pallas as pl
from jax.experimental.pallas import tpu as pltpu
from jax.sharding import PartitionSpec as P

HEAD_DIM = 64
FLOOR = -1e30
SQRT_2_PI = 0.7978845608028654
CUBIC = 0.044715
EXTRA = 16
TILE = 256
EDGE = 128
BF = jnp.bfloat16
F32 = jnp.float32
NN = (((1,), (0,)), ((), ()))
NT = (((1,), (1,)), ((), ()))
TN = (((0,), (0,)), ((), ()))
VM = pl.BlockSpec(memory_space=pltpu.VMEM)
SM = pl.BlockSpec(memory_space=pltpu.SMEM)
LIMITS = {"attend_own": 10, "attend_edge": 10, "back_edge": 12, "back_own": 12, "act": 14, "weights": 16, "feed_grads": 12, "place": 8, "hidden": 6, "middle": 6, "last_grads": 16, "fold": 10, "base": 6, "pack_qkv": 8, "pack_feed": 10}


def split(x):
    hi = x.astype(BF)
    return hi, (x - hi.astype(F32)).astype(BF)


def mm(a, b, dims=NN):
    return lax.dot_general(a, b, dims, preferred_element_type=F32)


def mm3(a, b, dims=NN):
    return mm(a[0], b[0], dims) + (mm(a[0], b[1], dims) + mm(a[1], b[0], dims))


def at(start, size, step=8):
    return pl.ds(pl.multiple_of(start, step), size)


def call(kernel, name, outs, ins, scratch=(), flops=0, smem=1, limit=16, wide=False, marks=()):
    inner, count, ins = kernel, len(ins), list(ins) + list(marks)

    def kernel(*refs):
        return inner(*refs[:count], *refs[len(ins):])

    size = sum(math.prod(x.shape) * x.dtype.itemsize for x in list(outs) + list(ins[smem:count]))
    return pl.pallas_call(
        kernel,
        out_shape=tuple(outs),
        in_specs=[SM] * smem + [VM] * (count - smem) + [pl.BlockSpec(memory_space=pl.ANY)] * len(marks),
        out_specs=tuple(SM if x.dtype == jnp.int32 else VM for x in outs),
        scratch_shapes=list(scratch),
        compiler_params=pltpu.CompilerParams(vmem_limit_bytes=(48 if wide else LIMITS.get(name, limit)) << 20),
        cost_estimate=pl.CostEstimate(flops=1, bytes_accessed=1, transcendentals=0),
        name=name,
    )(*ins)


def arr(shape, dtype=F32):
    return jax.ShapeDtypeStruct(tuple(shape), dtype)


def norm(x):
    centred = x - jnp.mean(x, axis=-1, keepdims=True)
    inverse = lax.rsqrt(jnp.mean(centred * centred, axis=-1, keepdims=True) + 1e-05)
    return centred * inverse, inverse


def norm_back(grad, gain, xhat, inverse):
    scaled = grad * gain
    mean = jnp.mean(scaled, axis=-1, keepdims=True)
    lean = jnp.mean(scaled * xhat, axis=-1, keepdims=True)
    return (scaled - mean - xhat * lean) * inverse


def pick(index, choices):
    value = choices[0]
    for i in range(1, len(choices)):
        value = jnp.where(index == i, choices[i], value)
    return value


def first_kernel(count, numbers, *refs):
    for source, target in zip((numbers,) + refs[:count], refs[count:]):
        if target.dtype == jnp.int32:
            for i in range(target.shape[1]):
                target[0, i] = source[0, i]
        else:
            target[...] = source[...]


def pack_qkv_kernel(idx, bounds, codes, halo_codes, small, wq, wk, wv, near, far, *outs):
    first_kernel(4, idx, bounds, codes, halo_codes, small, *outs)
    part = near.shape[2] // 3
    splits = wq.shape[1] // part
    for r in range(splits):
        target, k = (near, r) if r < 2 else (far, r - 2)
        for u in range(splits):

            @pl.when(idx[0, r] == u)
            def _():
                for i, w in enumerate((wq, wk, wv)):
                    target[k, :, i * part:(i + 1) * part] = w[:, u * part:(u + 1) * part]


def pack_feed_kernel(splits, blocks, place, idx, wup, wout, wdown, near, far, down_quarter):
    unit = near.shape[2] // blocks
    for r in range(splits):
        target, k = (near, r) if r < 2 else (far, r - 2)
        for u in range(splits):

            @pl.when(idx[0, r] == u)
            def _():
                for b in range(blocks):
                    lane = (b * splits + u) * unit
                    target[k, :, b * unit:(b + 1) * unit] = wup[:, lane:lane + unit]
    near[2] = wout[...]
    far[2] = wout[...]
    size = down_quarter.shape[0]
    down_quarter[...] = wdown[at(idx[0, place] * size, size), :]


def base_kernel(hidden, embed, small, out):
    tokens = hidden.shape[0]
    out[:tokens, :] = hidden[...] + embed[...]
    out[tokens:, :] = small[...]


def qkv_kernel(pieces, splits, edge, idx, og, *refs):
    base, rest = refs[:splits], refs[splits:]
    count = max(p[0] for p in pieces) + 1
    weights = rest[:count]
    (q_ref, kv_ref, edge_ref, base_ref, small_ref, wh, wl, og_ref, w32, nh, nl) = rest[count:count + 11]
    got = base + weights
    tokens = base[0].shape[0] - EXTRA
    part = q_ref.shape[1]
    rows = w32.shape[0] // len(pieces)
    small = None
    for r in range(splits):
        rest = got[r][tokens:, :]
        small = rest if small is None else small + rest
    small_ref[...] = small
    gain, shift = small[4:5], small[5:6]
    for r in range(splits):
        row = at(idx[0, r] * tokens, tokens, 16)
        x = got[r][:tokens, :]
        base_ref[row, :] = x
        xhat, _ = norm(x)
        nh[row, :], nl[row, :] = split(xhat * gain + shift)
    for i, (n, lead) in enumerate(pieces):
        w32[at(idx[0, splits + i] * rows, rows), :] = got[splits + n][lead, :rows, :]
    wh[...], wl[...] = split(w32[...])
    u = idx[0, 0]
    qb = pick(u, [small[0:1, i * part:(i + 1) * part] for i in range(splits)])
    vb = pick(u, [small[1:2, i * part:(i + 1) * part] for i in range(splits)])
    bias = jnp.concatenate([qb, jnp.zeros_like(qb), vb], axis=1)
    step = nh.shape[0] // 3

    def rows_of(i, _):
        row = at(i * step, step, 16)
        out = mm3((nh[row, :], nl[row, :]), (wh[...], wl[...])) + bias
        q_ref[row, :] = out[:, :part]
        kv_ref[row, :] = out[:, part:]
        return 0

    lax.fori_loop(0, 3, rows_of, 0)
    reach = edge_ref.shape[0]
    edge_ref[...] = kv_ref[at(idx[0, edge], reach), :]
    og_ref[...] = og[...]


def span_hits(seg, i, j):
    return (seg[0, 2 * j + 1] >= seg[0, 2 * i]) & (seg[0, 2 * j] <= seg[0, 2 * i + 1])


def prepare(src, width, first, count, size, pairs, flipped):
    heads = width // HEAD_DIM
    for scratch, start in pairs:
        for h in range(heads):
            hi, lo = split(src[:, start + h * HEAD_DIM:start + (h + 1) * HEAD_DIM])
            scratch[h] = jnp.concatenate([hi, lo, hi], axis=1)
    for j in range(count):
        turned = src[j * size:(j + 1) * size, first:first + width].T
        for h in range(heads):
            hi, lo = split(turned[h * HEAD_DIM:(h + 1) * HEAD_DIM])
            flipped[h, j] = jnp.concatenate([hi, lo], axis=0)


def columns(codes, out, size):
    for j in range(out.shape[0] // size):
        row = codes[1:2, j * size:(j + 1) * size]
        out[j * size:(j + 1) * size, :] = jnp.broadcast_to(row, (128, size)).T


def same_row(i, j):
    return (lax.broadcasted_iota(jnp.int32, (TILE, TILE), 0)
            - lax.broadcasted_iota(jnp.int32, (TILE, TILE), 1)) == (i - j) * TILE


def attend_add(heads, qc, keys, flipped, m_s, l_s, acc, i, j, size, allowed):
    qrow = at(i * TILE, TILE, TILE)
    krow = at(j * size, size, size)
    for h in range(heads):
        s = jnp.where(allowed, mm(keys[h, krow, :], qc[h, qrow, :], NT), FLOOR)
        m_old = m_s[h, i]
        m_new = jnp.maximum(m_old, jnp.max(s, axis=0, keepdims=True))
        p = jnp.where(allowed, jnp.exp(s - m_new), 0.0)
        factor = jnp.exp(m_old - m_new)
        m_s[h, i] = m_new
        l_s[h, i] = l_s[h, i] * factor + jnp.sum(p, axis=0, keepdims=True)
        hi, lo = split(p)
        v128 = flipped[h, j]
        acc[h, i] = acc[h, i] * factor + mm(v128, hi) + mm(v128, lo)


def attend_own_kernel(heads, seg_ref, qcode_ref, kcode_ref, q_ref, kv_ref, qc, m_s, l_s, acc, kc, vt, kcol):
    group, width = q_ref.shape
    nq = group // TILE
    for h in range(heads):
        hi, lo = split(q_ref[:, h * HEAD_DIM:(h + 1) * HEAD_DIM] * HEAD_DIM ** -0.5)
        qc[h] = jnp.concatenate([hi, hi, lo], axis=1)
    prepare(kv_ref, width, width, nq, TILE, [(kc, 0)], vt)
    columns(kcode_ref, kcol, TILE)
    m_s[...] = jnp.full_like(m_s, FLOOR)
    l_s[...] = jnp.zeros_like(l_s)
    acc[...] = jnp.zeros_like(acc)

    def per_q(i, _):
        def per_k(j, _):
            @pl.when(span_hits(seg_ref, i, j))
            def _():
                allowed = kcol[at(j * TILE, TILE, TILE), :1] == qcode_ref[:1, at(i * TILE, TILE, TILE)]
                attend_add(heads, qc, kc, vt, m_s, l_s, acc, i, j, TILE, allowed | same_row(i, j))
            return 0

        lax.fori_loop(0, nq, per_k, 0)
        return 0

    lax.fori_loop(0, nq, per_q, 0)


def attend_edge_kernel(heads, extra, seg_ref, qcode_ref, hcode_ref, halo_ref, qc, m_in, l_in, acc_in, *refs):
    out_ref, wide_ref, lse_ref = refs[extra:extra + 3]
    for source, target in zip(refs[:extra], refs[extra + 3:2 * extra + 3]):
        target[...] = source[...]
    kh, vh, hcol, m_s, l_s, acc = refs[2 * extra + 3:]
    group, width = out_ref.shape
    nq, nh = group // TILE, halo_ref.shape[0] // EDGE
    m_s[...] = m_in[...]
    l_s[...] = l_in[...]
    acc[...] = acc_in[...]
    if nh:
        prepare(halo_ref, width, width, nh, EDGE, [(kh, 0)], vh)
        columns(hcode_ref, hcol, EDGE)

    def per_q(i, _):
        qrow = at(i * TILE, TILE, TILE)

        def per_edge(j, _):
            @pl.when(span_hits(seg_ref, i, nq + j))
            def _():
                allowed = hcol[at(j * EDGE, EDGE, EDGE), :1] == qcode_ref[:1, qrow]
                attend_add(heads, qc, kh, vh, m_s, l_s, acc, i, j, EDGE, allowed)
            return 0

        if nh:
            lax.fori_loop(0, nh, per_edge, 0)
        parts = []
        for h in range(heads):
            total = l_s[h, i]
            parts.append((acc[h, i, :HEAD_DIM] + acc[h, i, HEAD_DIM:]) / total)
            lse_ref[h:h + 1, qrow] = m_s[h, i] + jnp.log(total)
        out_ref[qrow, :] = jnp.concatenate(parts, axis=0).T
        return 0

    lax.fori_loop(0, nq, per_q, 0)
    wide_ref[:, :width] = out_ref[:group // 2, :]
    wide_ref[:, width:] = out_ref[group // 2:, :]


def attend_own(segs, qcode, kcode, q, kv):
    group, width = q.shape
    heads, nq = width // HEAD_DIM, group // TILE
    return call(
        functools.partial(attend_own_kernel, heads), "attend_own",
        [arr((heads, group, 3 * HEAD_DIM), BF), arr((heads, nq, 1, TILE)), arr((heads, nq, 1, TILE)),
         arr((heads, nq, 2 * HEAD_DIM, TILE))],
        [segs, qcode, kcode, q, kv],
        [pltpu.VMEM((heads, group, 3 * HEAD_DIM), BF), pltpu.VMEM((heads, nq, 2 * HEAD_DIM, TILE), BF),
         pltpu.VMEM((group, 128), F32)],
        flops=4 * group * group * width)


def attend_edge(segs, qcode, hcode, halo, state, passed=(), marks=()):
    heads, group, _ = state[0].shape
    reach, width = halo.shape[0], halo.shape[1] // 2
    nq, nh = group // TILE, reach // EDGE
    return call(
        functools.partial(attend_edge_kernel, heads, len(passed)), "attend_edge",
        [arr((group, width)), arr((group // 2, 2 * width)), arr((8, group))] + [arr(x.shape) for x in passed],
        [segs, qcode, hcode, halo, *state, *passed],
        [pltpu.VMEM((heads, reach, 3 * HEAD_DIM), BF), pltpu.VMEM((heads, nh, 2 * HEAD_DIM, EDGE), BF),
         pltpu.VMEM((reach, 128), F32)]
        + [pltpu.VMEM(x.shape, x.dtype) for x in state[1:]],
        flops=2 * group * reach * width, wide=reach > group, marks=marks)


def back_add(heads, qc, q2, dc, d2, dot_s, lse_ref, keys, values, flipped, dqa, dka, dva, i, j, size, allowed):
    qrow = at(i * TILE, TILE, TILE)
    krow = at(j * size, size, size)
    for h in range(heads):
        s = mm(keys[h, krow, :], qc[h, qrow, :], NT)
        p = jnp.exp(jnp.where(allowed, s - lse_ref[h:h + 1, qrow], FLOOR))
        dp = mm(values[h, krow, :], dc[h, qrow, :], NT)
        ds = p * (dp - dot_s[h, :, qrow])
        hi, lo = split(p)
        d128 = d2[h, qrow, :]
        dva[h] += mm(hi, d128) + mm(lo, d128)
        hi, lo = split(ds)
        q128 = q2[h, qrow, :]
        dka[h] += mm(hi, q128) + mm(lo, q128)
        k128 = flipped[h, j]
        dqa[h, i] += mm(k128, hi) + mm(k128, lo)


def back_over(heads, seg_ref, nq, count, size, first, out, dka, dva, visit):
    width = heads * HEAD_DIM

    def folded(acc):
        return jnp.concatenate([acc[h, :, :HEAD_DIM] + acc[h, :, HEAD_DIM:] for h in range(heads)], axis=1)

    def per_k(j, _):
        dka[...] = jnp.zeros_like(dka)
        dva[...] = jnp.zeros_like(dva)

        def per_q(i, _):
            @pl.when(span_hits(seg_ref, i, first + j))
            def _():
                visit(i, j)
            return 0

        lax.fori_loop(0, nq, per_q, 0)
        krow = at(j * size, size, size)
        out[krow, :width] = folded(dka)
        out[krow, width:] = folded(dva)
        return 0

    lax.fori_loop(0, count, per_k, 0)


def back_edge_kernel(heads, splits, idx, seg_ref, qcode_ref, hcode_ref, q_ref, halo_ref, o_ref, lse_ref, qc,
                     oh_ref, ol_ref, *refs):
    mg, (dhalo_ref, q2, dc, d2, dot_s, dqa, gh, gl, kh, vh, kth, hcol, prod_s, dka, dva) = (
        refs[:splits], refs[splits:])
    group, width = q_ref.shape
    nq, nh = group // TILE, halo_ref.shape[0] // EDGE
    tokens = group // splits
    if nh:
        prepare(halo_ref, width, 0, nh, EDGE, [(kh, 0), (vh, width)], kth)
        columns(hcode_ref, hcol, EDGE)
    for h in range(heads):
        hi, lo = split(q_ref[:, h * HEAD_DIM:(h + 1) * HEAD_DIM] * HEAD_DIM ** -0.5)
        q2[h] = jnp.concatenate([hi, lo], axis=1)
    dqa[...] = jnp.zeros_like(dqa)
    wrow = at(idx[0, 0] * width, width, 16)
    w_pair = (oh_ref[wrow, :], ol_ref[wrow, :])
    for r in range(splits):
        row = at(idx[0, r] * tokens, tokens, 16)
        gh[row, :], gl[row, :] = split(mg[r][...])
    step = group // 3

    def rows_of(i, _):
        row = at(i * step, step, 16)
        grad = mm3((gh[row, :], gl[row, :]), w_pair, NT)
        prod_s[row, :] = grad * o_ref[row, :]
        for h in range(heads):
            hi, lo = split(grad[:, h * HEAD_DIM:(h + 1) * HEAD_DIM])
            dc[h, row, :] = jnp.concatenate([hi, hi, lo], axis=1)
            d2[h, row, :] = jnp.concatenate([hi, lo], axis=1)
        return 0

    lax.fori_loop(0, 3, rows_of, 0)
    for i in range(nq):
        rows = slice(i * TILE, (i + 1) * TILE)
        prod = prod_s[rows, :].T
        for h in range(heads):
            dot_s[h, :, rows] = jnp.sum(prod[h * HEAD_DIM:(h + 1) * HEAD_DIM], axis=0, keepdims=True)

    def visit(i, j):
        allowed = hcol[at(j * EDGE, EDGE, EDGE), :1] == qcode_ref[:1, at(i * TILE, TILE, TILE)]
        back_add(heads, qc, q2, dc, d2, dot_s, lse_ref, kh, vh, kth, dqa, dka, dva, i, j, EDGE, allowed)

    if nh:
        back_over(heads, seg_ref, nq, nh, EDGE, nq, dhalo_ref, dka, dva, visit)


def back_own_kernel(heads, seg_ref, qcode_ref, kcode_ref, kv_ref, lse_ref, qc, q2, dc, d2, dot_s, dq_in,
                    dq_ref, dkv_ref, kc, vc, kt, kcol, dqa, dka, dva):
    group, width = dq_ref.shape
    nq = group // TILE
    prepare(kv_ref, width, 0, nq, TILE, [(kc, 0), (vc, width)], kt)
    columns(kcode_ref, kcol, TILE)
    dqa[...] = dq_in[...]

    def visit(i, j):
        allowed = kcol[at(j * TILE, TILE, TILE), :1] == qcode_ref[:1, at(i * TILE, TILE, TILE)]
        back_add(heads, qc, q2, dc, d2, dot_s, lse_ref, kc, vc, kt, dqa, dka, dva, i, j, TILE, allowed | same_row(i, j))

    back_over(heads, seg_ref, nq, nq, TILE, 0, dkv_ref, dka, dva, visit)
    for i in range(nq):
        parts = [(dqa[h, i, :HEAD_DIM] + dqa[h, i, HEAD_DIM:]) * HEAD_DIM ** -0.5 for h in range(heads)]
        dq_ref[i * TILE:(i + 1) * TILE, :] = jnp.concatenate(parts, axis=0).T


def attend_back_edge(idx, segs, qcode, hcode, q, halo, o, lse, qc, oh, ol, mg):
    group, width = q.shape
    reach = halo.shape[0]
    heads = width // HEAD_DIM
    nq, nh = group // TILE, reach // EDGE
    full = oh.shape[1]
    H3, H2 = 3 * HEAD_DIM, 2 * HEAD_DIM
    return call(
        functools.partial(back_edge_kernel, heads, len(mg)), "back_edge",
        [arr((reach, 2 * width)), arr((heads, group, H2), BF), arr((heads, group, H3), BF), arr((heads, group, H2), BF),
         arr((heads, 1, group)), arr((heads, nq, H2, TILE)), arr((group, full), BF), arr((group, full), BF)],
        [idx, segs, qcode, hcode, q, halo, o, lse, qc, oh, ol, *mg],
        [
            pltpu.VMEM((heads, reach, H3), BF),
            pltpu.VMEM((heads, reach, H3), BF),
            pltpu.VMEM((heads, nh, H2, EDGE), BF),
            pltpu.VMEM((reach, 128), F32),
            pltpu.VMEM((group, width), F32),
            pltpu.VMEM((heads, EDGE, H2), F32),
            pltpu.VMEM((heads, EDGE, H2), F32),
        ],
        flops=2 * group * full * width, smem=2, wide=reach > group)


def attend_back_own(segs, qcode, kcode, kv, lse, qc, q2, dc, d2, dot_s, dqa, marks):
    heads, group, _ = qc.shape
    width = kv.shape[1] // 2
    nq = group // TILE
    H3, H2 = 3 * HEAD_DIM, 2 * HEAD_DIM
    return call(
        functools.partial(back_own_kernel, heads), "back_own",
        [arr((group, width)), arr((group, 2 * width))],
        [segs, qcode, kcode, kv, lse, qc, q2, dc, d2, dot_s, dqa],
        [
            pltpu.VMEM((heads, group, H3), BF),
            pltpu.VMEM((heads, group, H3), BF),
            pltpu.VMEM((heads, nq, H2, TILE), BF),
            pltpu.VMEM((group, 128), F32),
            pltpu.VMEM((heads, nq, H2, TILE), F32),
            pltpu.VMEM((heads, TILE, H2), F32),
            pltpu.VMEM((heads, TILE, H2), F32),
        ],
        flops=10 * group * group * width, marks=marks)


def weights_kernel(full, splits, idx, *refs):
    count = max([p[0] for p in full]) + 1
    weights, (uh, ul, oh, ol, u32, o32) = refs[:count], refs[count:count + 6]
    got = weights
    owners = len(full)
    rows = u32.shape[0] // owners
    for i, (n, lead) in enumerate(full):
        row = at(idx[0, splits + i] * rows, rows)
        u32[row, :] = got[n][lead]
        o32[row, :] = got[n][2]
    uh[...], ul[...] = split(u32[...])
    oh[...], ol[...] = split(o32[...])


def act_kernel(splits, whole, first, place, idx, *refs):
    got, (gh, gl, dh, dl, act_ref) = refs[:-5], refs[-5:]
    tokens = got[0].shape[0]
    down = got[splits:]
    unit = down[0].shape[0]
    blocks = dh.shape[0] // unit
    for r in range(splits):
        row = at(idx[0, r] * tokens, tokens, 16)
        gh[row, :], gl[row, :] = split(got[r][...])
    for i in range(blocks):
        if i < whole:
            row = at(idx[0, first + i] * unit, unit, 16)
            dh[row, :], dl[row, :] = split(down[i][...])
            continue
        size = unit // 4
        for z in range(4):
            quarter = idx[0, place] ^ (0, 3, 1, 2)[z]
            row = at(idx[0, first + i] * unit + quarter * size, size, 16)
            dh[row, :], dl[row, :] = split(down[whole + 4 * (i - whole) + z][...])
    step = gh.shape[0] // 3

    def rows_of(i, _):
        row = at(i * step, step, 16)
        act_ref[row, :] = mm3((gh[row, :], gl[row, :]), (dh[...], dl[...]), NT)
        return 0

    lax.fori_loop(0, 3, rows_of, 0)


def feed_kernel(splits, idx, small, base, *refs):
    (oh, ol, uh, ul, act, keep, send, mine, inv_ref, ah, al, ph, plo, mh, ml, vec, b32, x2, g32, r32) = (
        refs[splits:splits + 20])
    att = refs[:splits]
    tokens = keep.shape[1]
    group = b32.shape[0]
    part = att[0].shape[1] // 2
    gain, shift = small[6:7, :], small[7:8, :]
    up_bias = small[pl.ds(8 + idx[0, 0], 1), :]
    vec[...] = jnp.zeros_like(vec)
    step = group // 2

    def rows_of(i, _):
        row = at(i * step, step, 16)
        middle = base[row, :] + small[2:3, :]
        for s in range(splits):
            wrow = at(idx[0, s] * part, part, 16)
            piece = jnp.where(i == 0, att[s][:, :part], att[s][:, part:])
            middle = middle + mm3(split(piece), (oh[wrow, :], ol[wrow, :]))
        b32[row, :] = middle
        xhat, inverse = norm(middle)
        x2[row, :] = xhat
        g32[row, :] = jnp.broadcast_to(inverse, g32[row, :].shape)
        pair = split(xhat * gain + shift)
        mh[row, :], ml[row, :] = pair
        pre = mm3(pair, (uh[...], ul[...])) + up_bias
        square = pre * pre
        curve = jnp.tanh(SQRT_2_PI * (pre + CUBIC * square * pre))
        half = 0.5 * (1.0 + curve)
        ah[row, :], al[row, :] = split(pre * half)
        slope = half + 0.5 * pre * (1.0 - curve * curve) * SQRT_2_PI * (1.0 + 3.0 * CUBIC * square)
        grad = act[row, :] * slope
        pair = split(grad)
        ph[row, :], plo[row, :] = pair
        back = mm3(pair, (uh[...], ul[...]), NT)
        vec[0:1, :] += jnp.sum(grad, axis=0, keepdims=True)
        vec[1:2, :] += jnp.sum(back * xhat, axis=0, keepdims=True)
        vec[2:3, :] += jnp.sum(back, axis=0, keepdims=True)
        r32[row, :] = back
        return 0

    lax.fori_loop(0, 2, rows_of, 0)

    def pairs_of(h, _):
        keep[h] = r32[at(idx[0, 2 * h] * tokens, tokens), :]
        send[h] = r32[at(idx[0, 2 * h + 1] * tokens, tokens), :]
        return 0

    lax.fori_loop(0, splits // 2, pairs_of, 0)
    row = at(idx[0, 0] * tokens, tokens)
    mine[0] = b32[row, :]
    mine[1] = x2[row, :]
    inv_ref[...] = g32[row, :]


def feed_grads_kernel(splits, first, down_rows, up_rows, idx, ah, al, ph, plo, mh, ml, gh, gl, dh, dl,
                      keep, send, *refs):
    outs, r32 = refs[:-1], refs[-1]
    downs, ups = outs[:len(outs) // 2], outs[len(outs) // 2:]
    tokens = keep.shape[1]
    step = r32.shape[0] // 3

    third = r32.shape[0] // 3

    def left(a, b):
        def rows_of(i, _):
            lane = at(i * third, third, 128)
            r32[at(i * third, third), :] = mm3((a[0][:, lane], a[1][:, lane]), (b[0][...], b[1][...]), TN)
            return 0

        lax.fori_loop(0, 3, rows_of, 0)

    def deal(targets, rows, place):
        for target in targets:
            def one(c, _, target=target, place=place):
                target[c] = r32[at(idx[0, place + c], rows), :]
                return 0

            lax.fori_loop(0, target.shape[0], one, 0)
            place += target.shape[0]
        return place

    left((ah, al), (gh, gl))
    place = deal(downs, down_rows, first)
    left((mh, ml), (ph, plo))
    deal(ups, up_rows, place)

    def rows_of(i, _):
        row = at(i * step, step, 16)
        r32[row, :] = mm3((ah[row, :], al[row, :]), (dh[...], dl[...]))
        return 0

    lax.fori_loop(0, 3, rows_of, 0)

    def pairs_of(h, _):
        keep[h] = r32[at(idx[0, 2 * h] * tokens, tokens), :]
        send[h] = r32[at(idx[0, 2 * h + 1] * tokens, tokens), :]
        return 0

    lax.fori_loop(0, splits // 2, pairs_of, 0)


def middle_kernel(small, keep, core, far, og, mine, inv, mg_ref, vec_ref):
    grad = keep[0] + core[0] + far[...]
    out = og[...] + norm_back(grad, small[6:7, :], mine[1], inv[:, :1])
    mg_ref[...] = out
    vec_ref[...] = jnp.zeros_like(vec_ref)
    vec_ref[0:1, :] = jnp.sum(out, axis=0, keepdims=True)
    vec_ref[1:2, :] = jnp.sum(og[...], axis=0, keepdims=True)


def last_grads_kernel(splits, first, edge, rows, idx, small, dq, dkv, back, base, att, vec1, vec2, gh, gl, wh, wl,
                      keep, send, *refs):
    tails, (qh, ql, xhat, r32, o32, s32, n32, vec) = refs[:-8], refs[-8:]
    part = dq.shape[1]
    width = xhat.shape[1]
    tokens = keep.shape[1]
    u = idx[0, 0]
    s32[:, :part] = dq[...]
    s32[:, part:] = dkv[...]
    s32[at(idx[0, edge], back.shape[0]), part:] += back[...]
    qkv = s32[...]
    qh[...], ql[...] = split(qkv)
    sums = jnp.sum(qkv, axis=0, keepdims=True)
    xhat[...], _ = norm(base[...])
    vec[...] = jnp.zeros_like(vec)
    step = n32.shape[0] // 3

    def rows_of(i, _):
        row = at(i * step, step, 16)
        grad = mm3((qh[row, :], ql[row, :]), (wh[...], wl[...]), NT)
        n32[row, :] = grad
        vec[4:5, :] += jnp.sum(grad * xhat[row, :], axis=0, keepdims=True)
        vec[5:6, :] += jnp.sum(grad, axis=0, keepdims=True)
        return 0

    lax.fori_loop(0, 3, rows_of, 0)

    def pairs_of(h, _):
        keep[h] = n32[at(idx[0, 2 * h] * tokens, tokens), :]
        send[h] = n32[at(idx[0, 2 * h + 1] * tokens, tokens), :]
        return 0

    lax.fori_loop(0, splits // 2, pairs_of, 0)
    step = width // 3

    def lanes_of(i, _):
        lane = at(i * step, step, 128)
        pair = split(xhat[:, lane] * small[4:5, lane] + small[5:6, lane])
        r32[lane, :] = mm3(pair, (qh[...], ql[...]), TN)
        return 0

    lax.fori_loop(0, 3, lanes_of, 0)
    o32[...] = mm3(split(att[...]), (gh[...], gl[...]), TN)
    for i in range(splits):

        @pl.when(u == i)
        def _():
            vec[0:1, i * part:(i + 1) * part] = sums[:, :part]
            vec[1:2, i * part:(i + 1) * part] = sums[:, 2 * part:]

    vec[2:4, :] = vec2[0:2, :]
    vec[6:8, :] = vec1[1:3, :]
    vec[pl.ds(8 + u, 1), :] = vec1[0:1, :]
    wide = r32.shape[1]
    outs = width // 128
    vecs = outs * EXTRA // rows
    lane_blocks = -(-wide // 128)
    spare = lane_blocks * 128 - wide
    near = 2 * lane_blocks
    total = sum(t.shape[0] for t in tails)
    spot = 0
    for t in tails:
        def one(c, _, t=t, spot=spot):
            for j in range(splits):
                row = at(idx[0, first + (spot + c) * splits + j], rows)
                start = j * lane_blocks + (outs + vecs if j >= 2 else 0)
                for k in range(lane_blocks - 1):
                    t[c, start + k] = r32[row, k * 128:(k + 1) * 128]
                k = lane_blocks - 1
                t[c, start + k, :, :128 - spare] = r32[row, k * 128:]
                t[c, start + k, :, 128 - spare:] = jnp.zeros((rows, spare), F32)
            row = at(idx[0, first + total * splits + spot + c], rows)
            for k in range(outs):
                t[c, near + k] = o32[row, k * 128:(k + 1) * 128]
            for k in range(outs * EXTRA // 8):
                block, low = divmod(8 * k, rows)
                lane, high = divmod(8 * k, EXTRA)
                t[c, near + outs + block, low:low + 8, :] = vec[high:high + 8, lane * 128:(lane + 1) * 128]
            return 0

        lax.fori_loop(0, t.shape[0], one, 0)
        spot += t.shape[0]


def hidden_kernel(idx, small, base, keep, core, far, mg, out):
    tokens = mg.shape[0]
    xhat, inverse = norm(base[at(idx[0, 0] * tokens, tokens), :])
    out[...] = mg[...] + norm_back(keep[0] + core[0] + far[...], small[4:5, :], xhat, inverse)


def fold_kernel(count, *refs):
    keeps, gots, outs = refs[:count], refs[count:2 * count], refs[2 * count:]
    for i in range(count):
        stay, go = outs[2 * i:2 * i + 2]
        half = stay.shape[0]
        stay[...] = keeps[i][:half] + gots[i][:half]
        go[...] = keeps[i][half:] + gots[i][half:]


def fold(keeps, gots, marks=()):
    outs = []
    for keep in keeps:
        outs += [arr((keep.shape[0] // 2,) + keep.shape[1:])] * 2
    got = call(functools.partial(fold_kernel, len(keeps)), "fold", outs, [*keeps, *gots], smem=0, marks=marks)
    return got[::2], got[1::2]


def message_kernel(near, stop, vecs, part, far, out):
    blocks = near // 2
    out[:blocks] = part[blocks:near]
    out[blocks:blocks + vecs] = part[stop:stop + vecs] + far[:vecs]
    out[blocks + vecs:] = far[vecs + blocks:]


def place_kernel(splits, first, rows, idx, *refs):
    pieces, (gq, gk, gv, go) = refs[:-4], refs[-4:]
    part = gq.shape[1] // splits
    for z, piece in enumerate(pieces):
        row = at(idx[0, first + z] * rows, rows)
        count = gq.shape[1] // 128
        for k in range(count):
            go[row, k * 128:(k + 1) * 128] = piece[5 * splits + k]
        for i in range(splits):
            whole = jnp.concatenate([piece[5 * idx[0, i] + k] for k in range(5)], axis=1)
            for n, out in enumerate((gq, gk, gv)):
                out[row, i * part:(i + 1) * part] = whole[:, n * part:(n + 1) * part]


def place_feed_kernel(splits, blocks, unit, first, idx, *refs):
    pieces, (gd, gu) = refs[:-2], refs[-2:]
    downs, ups = pieces[:len(pieces) // 2], pieces[len(pieces) // 2:]
    for z, (down, up) in enumerate(zip(downs, ups)):
        gd[at(idx[0, first + z] * down.shape[0], down.shape[0]), :] = down[...]
        rows = up.shape[1]
        row = at(idx[0, first + z] * rows, rows)
        for i in range(splits):
            for n in range(blocks):
                start = (n * splits + i) * unit
                gu[row, start:start + unit] = up[idx[0, i], :, n * unit:(n + 1) * unit]


def swap(value, axis, mask):
    count = lax.axis_size(axis)
    return lax.ppermute(value, axis, [(i, i ^ mask) for i in range(count)])


def across(value):
    return swap(value, "ulys", 2)


def beside(value):
    return swap(value, "ulys", 1)


def over(value):
    return swap(value, "blk", 1)


def gather_splits(value):
    far = across(value)
    return [value, beside(value), far, beside(far)]


def collect(value):
    near = swap(value, "dp", 3)
    return [value, near, swap(value, "dp", 1), swap(near, "dp", 1)]


def halo_moves(group, reach, blocks):
    moves = []
    shift = 1
    while reach > 0 and shift < blocks:
        rows = min(group, reach)
        moves.append((rows, True, [(i, i - shift) for i in range(shift, blocks)]))
        moves.append((rows, False, [(i, i + shift) for i in range(blocks - shift)]))
        reach -= rows
        shift += 1
    return moves


def halo_get(value, reach, axis=0):
    blocks, group = lax.axis_size("blk"), value.shape[axis]
    parts = []
    for rows, right, moves in halo_moves(group, reach, blocks):
        start = 0 if right else group - rows
        parts.append(lax.ppermute(lax.slice_in_dim(value, start, start + rows, axis=axis), "blk", moves))
    return jnp.concatenate(parts, axis=axis)


def halo_add(value, halo, reach):
    blocks, group = lax.axis_size("blk"), value.shape[0]
    start = 0
    for rows, right, moves in halo_moves(group, reach, blocks):
        back = lax.ppermute(halo[start:start + rows], "blk", [(j, i) for i, j in moves])
        start += rows
        room = group - rows
        value = value + jnp.pad(back, ((0, room), (0, 0)) if right else ((room, 0), (0, 0)))
    return value


def local(
    hidden,
    time_embed,
    segment_ids,
    key_valid,
    out_grad,
    w_query,
    b_query,
    w_key,
    w_value,
    b_value,
    w_out,
    b_out,
    w_up,
    b_up,
    w_down,
    b_down,
    pre_gain,
    pre_shift,
    mlp_gain,
    mlp_shift,
):
    blocks, splits = lax.axis_size("blk"), lax.axis_size("ulys")
    b, u, d = (lax.axis_index(name) for name in ("blk", "ulys", "dp"))
    both = ("blk", "ulys")
    owners = blocks * splits
    tokens, width = hidden.shape
    group = tokens * splits
    part = width // splits
    rows = w_query.shape[0]
    unit = w_down.shape[0]
    units = unit * owners
    share = units // splits
    reach = group * blocks // 4
    fast = blocks == 2 and splits == 4 and lax.axis_size("dp") == 4 and reach <= group and group == width

    if fast:
        f1, f3 = (d ^ (d >> 1)) & 1, d >> 1
        quarters = [2 * (f1 ^ s) + (f3 ^ t) for s in range(2) for t in range(2)]
        owner_list = [(b ^ x) * splits + (u ^ r) for x in range(2) for r in range(4)]
        block_list = [b, b ^ 1]
        edge_row = jnp.where(b == 0, group - reach, 0)
        down_rows, up_rows, tail_rows = unit // 4, rows // 4, rows // 4
        down_table = [(b ^ x) * unit + q * down_rows for x in range(2) for q in quarters]
        up_table = [
            ((b ^ x) * splits + (u ^ r)) * rows + q * up_rows for q in quarters for x in range(2) for r in range(4)
        ]
        tail_table = [
            ((b ^ x) * splits + (u ^ r)) * rows + q * tail_rows for x in range(2) for q in quarters for r in range(4)
        ] + [(b ^ x) * rows + q * tail_rows for x in range(2) for q in quarters]
        chunks = 8
    else:
        quarters = []
        owner_list = list(range(owners))
        block_list = list(range(blocks))
        edge_row = 0
        down_rows, up_rows, tail_rows = unit, rows, rows
        down_table = [i * unit for i in range(blocks)]
        up_table = [i * rows for i in range(owners)]
        tail_table = up_table + [i * rows for i in range(blocks)]
        chunks = blocks
    entries, spots = [], []
    for values in (
        [u ^ r for r in range(splits)], owner_list, block_list, [d], [edge_row], down_table + up_table, tail_table,
        quarters,
    ):
        spots.append(len(entries))
        entries += values
    _, _, at_block, at_d, at_edge, at_feed, at_tail, at_quarter = spots
    idx = jnp.stack([jnp.asarray(v, jnp.int32) for v in entries]).reshape(1, -1)

    segments = segment_ids[0] + 1
    codes = jnp.stack([segments, jnp.where(key_valid[0] == 1, segments, 0)]).astype(F32)
    small = jnp.stack([b_query, b_value, b_out, b_down, pre_gain, pre_shift, mlp_gain, mlp_shift])
    small = lax.dynamic_update_slice(jnp.zeros((EXTRA, width), F32), small, (0, (b * splits + u) * rows))
    small = lax.dynamic_update_slice(small, b_up[None], (8 + u, b * unit))
    if fast:
        small = lax.dynamic_update_slice(small, codes, (12, 0))
        other = over(small)
        small = small + other
        halo_codes = jnp.where(b == 0, other[12:14, :reach], other[12:14, group - reach:group])
    else:
        small = lax.psum(small, "blk")
        halo_codes = halo_get(codes, reach, axis=1)
    tiles = codes[0].reshape(-1, TILE)
    edges = halo_codes[0].reshape(-1, EDGE)
    bounds = jnp.concatenate(
        [
            jnp.stack([tiles[:, 0], tiles[:, -1]], axis=1).reshape(-1),
            jnp.stack([jnp.min(jnp.where(edges == 0, 1e6, edges), axis=1), jnp.max(edges, axis=1)], axis=1).reshape(-1),
        ]
    ).astype(jnp.int32).reshape(1, -1)
    def make_base(marks):
        return call(
            base_kernel, "base", [arr((tokens + EXTRA, width))], [hidden, time_embed, small], smem=0, marks=marks)[0]

    if fast:
        tables = [idx, bounds, codes, halo_codes, small]
        near, far, *tables = call(
            pack_qkv_kernel, "pack_qkv",
            [arr((2, rows, 3 * part))] * 2 + [arr(x.shape, x.dtype) for x in tables],
            [*tables, w_query, w_key, w_value], smem=2)
        idx, bounds, codes, halo_codes, small = tables
        pieces = [(i, i % 2) for i in range(8)]
        far = across(far)
        near_over = over(near)
        base = make_base([far, near_over])
        far_base = across(base)
        qkv_arrays = [near, beside(near), far, beside(far)]
        near = near_over
        far = over(far)
        qkv_arrays += [near, beside(near), far, beside(far)]
        base_all = [base, beside(base), far_base, beside(far_base)]
        near2, far2, down_quarter = call(
            functools.partial(pack_feed_kernel, splits, blocks, at_d), "pack_feed",
            [arr((3, rows, share))] * 2 + [arr((unit // 4, width))],
            [idx, w_up, w_out, w_down], marks=[far])
        down_quarter = over(down_quarter)
        far2 = across(far2)
        feed_arrays = [near2, beside(near2), far2, beside(far2)]
        near2 = over(near2)
        feed_arrays += [near2, beside(near2)]
        whole = 1
    else:
        cut = jnp.stack([w_query, w_key, w_value], axis=1).reshape(rows, 3, splits, part)
        cut = cut.transpose(2, 0, 1, 3).reshape(splits, rows, 3 * part)
        cut = jnp.broadcast_to(cut[None], (blocks,) + cut.shape).reshape(owners, rows, 3 * part)
        got = lax.all_to_all(cut, both, 0, 0, tiled=True)
        qkv_arrays = [got[i:i + 1] for i in range(owners)]
        cut = w_up.reshape(rows, blocks, splits, unit).transpose(2, 0, 1, 3).reshape(splits, rows, share)
        cut = jnp.broadcast_to(cut[None], (blocks,) + cut.shape).reshape(owners, rows, share)
        got = lax.all_to_all(cut, both, 0, 0, tiled=True)
        outs = lax.all_gather(w_out, both, axis=0, tiled=False)
        feed_arrays = [jnp.stack([got[i], got[i], outs[i]]) for i in range(owners)]
        pieces = [(i, 0) for i in range(owners)]
        whole = blocks
        base = make_base([])
        base_all = gather_splits(base)
        gathered = lax.all_gather(w_down, "blk", axis=0, tiled=False)
        down = [gathered[i] for i in range(blocks)]

    query_codes, key_codes, edge_codes = codes, codes, halo_codes
    query, key_value, edge_kv, base, small, qkv_hi, qkv_lo, own_grad = call(
        functools.partial(qkv_kernel, pieces, splits, at_edge), "qkv",
        [arr((group, part)), arr((group, 2 * part)), arr((reach if fast else 8, 2 * part)), arr((group, width)),
         arr((EXTRA, width)), arr((width, 3 * part), BF), arr((width, 3 * part), BF), arr((tokens, width))],
        [idx, out_grad, *base_all, *qkv_arrays],
        [pltpu.VMEM((width, 3 * part), F32), pltpu.VMEM((group, width), BF), pltpu.VMEM((group, width), BF)],
        flops=2 * group * width * 3 * part)
    halo = over(edge_kv) if fast else halo_get(key_value, reach)
    state = attend_own(bounds, query_codes, key_codes, query, key_value)
    grads = gather_splits(own_grad)
    if fast:
        down = [w_down, down_quarter] + [swap(down_quarter, "dp", mask) for mask in (3, 1, 2)]
        attended, attended_wide, lse, far2 = attend_edge(bounds, query_codes, edge_codes, halo, state, (far2,), [*down[2:], grads[2], near2])
        far2 = over(far2)
        feed_arrays += [far2, beside(far2)]
    else:
        attended, attended_wide, lse = attend_edge(bounds, query_codes, edge_codes, halo, state)
    attended_all = gather_splits(attended_wide)
    og_hi, og_lo, down_hi, down_lo, act_grad = call(
        functools.partial(act_kernel, splits, whole, at_block, at_d), "act",
        [arr((group, width), BF)] * 2 + [arr((share, width), BF)] * 2 + [arr((group, share))],
        [idx, *grads, *down],
        flops=2 * group * width * share, marks=[attended_all[2]])
    up_hi, up_lo, out_hi, out_lo = call(
        functools.partial(weights_kernel, pieces, splits), "weights",
        [arr((width, share), BF)] * 2 + [arr((width, width), BF)] * 2,
        [idx, *feed_arrays],
        [pltpu.VMEM((width, share), F32), pltpu.VMEM((width, width), F32)], marks=[act_grad])

    pair = [arr((group, share), BF)] * 2
    keep, send, mine, inverse2, act_hi, act_lo, pre_hi, pre_lo, in_hi, in_lo, vec_feed = call(
        functools.partial(feed_kernel, splits), "feed",
        [arr((2, tokens, width))] * 2 + [arr((2, tokens, width)), arr((tokens, 128))] + pair * 2
        + [arr((group, width), BF)] * 2 + [arr((8, width))],
        [idx, small, base, *attended_all, out_hi, out_lo, up_hi, up_lo, act_grad],
        [pltpu.VMEM((group, width), F32), pltpu.VMEM((group, width), F32), pltpu.VMEM((group, 128), F32),
         pltpu.VMEM((group, width), F32)],
        flops=2 * group * width * (width + 2 * share))
    core = beside(send)
    near_sum = keep[1] + core[1]
    far_sum = across(near_sum)

    if fast:
        feed_outs = [arr((4, down_rows, width))] * 2 + [arr((8 * splits // 2, up_rows, share))] * 2
    else:
        feed_outs = [arr((blocks, down_rows, width)), arr((owners, up_rows, share))]
    keep_out, send_out, *feed_grads = call(
        functools.partial(feed_grads_kernel, splits, at_feed, down_rows, up_rows), "feed_grads",
        [arr((2, tokens, width))] * 2 + feed_outs,
        [idx, act_hi, act_lo, pre_hi, pre_lo, in_hi, in_lo, og_hi, og_lo, down_hi, down_lo],
        [pltpu.VMEM((group, width), F32)],
        flops=6 * group * width * share, marks=[near_sum])
    if fast:
        down_keep, down_send, up_keep, up_send = feed_grads
        down_got = over(down_send)
        up_got = swap(up_send, "dp", 1)

    middle_grad, vec_middle = call(
        middle_kernel, "middle",
        [arr((tokens, width)), arr((8, width))],
        [small, keep, core, far_sum, out_grad, mine, inverse2], smem=0, marks=[keep_out])
    middle_all = gather_splits(middle_grad)

    halo_grad, q2, dc, d2, dots, dq_part, mg_hi, mg_lo = attend_back_edge(
        idx, bounds, query_codes, edge_codes, query, halo, attended, lse, state[0], out_hi, out_lo, middle_all)
    if fast:
        returned = over(halo_grad)
        (down_keep, up_keep), (down_send, up_send) = fold((down_keep, up_keep), (down_got, up_got), [halo_grad])
        down_got = swap(down_send, "dp", 1)
        up_got = swap(up_send, "dp", 3)
        own_marks = [down_keep]
    else:
        own_marks = []
    query_grad, kv_grad = attend_back_own(
        bounds, query_codes, key_codes, key_value, lse, state[0], q2, dc, d2, dots, dq_part, own_marks)
    if not fast:
        kv_grad = halo_add(kv_grad, halo_grad, reach)
        returned = jnp.zeros((8, 2 * part), F32)

    core_out = beside(send_out)
    far_out = across(keep_out[1] + core_out[1])
    lane_blocks = -(-3 * part // 128)
    outs, vecs = width // 128, width // 128 * EXTRA // tail_rows
    total_blocks = splits * lane_blocks + outs + vecs
    tail_outs = [arr((2, total_blocks, tail_rows, 128))] * 4 if fast else [arr((blocks, total_blocks, tail_rows, 128))]
    keep_in, send_in, *tail = call(
        functools.partial(last_grads_kernel, splits, at_tail, at_edge, tail_rows), "last_grads",
        [arr((2, tokens, width))] * 2 + tail_outs,
        [idx, small, query_grad, kv_grad, returned, base, attended, vec_feed, vec_middle, mg_hi, mg_lo, qkv_hi, qkv_lo],
        [pltpu.VMEM((group, 3 * part), BF), pltpu.VMEM((group, 3 * part), BF), pltpu.VMEM((group, width), F32),
         pltpu.VMEM((width, 3 * part), F32), pltpu.VMEM((part, width), F32), pltpu.VMEM((group, 3 * part), F32),
         pltpu.VMEM((group, width), F32), pltpu.VMEM((EXTRA, width), F32)],
        flops=2 * group * width * 7 * part, marks=[far_out])
    to_owner = [(i * splits + j, j * blocks + i) for i in range(blocks) for j in range(splits)]
    near = 2 * lane_blocks
    if fast:
        tail_near, tail_far, send_near, send_far = tail
        got_far = over(send_far)
        got_near = over(send_near)
        core_in = beside(send_in)
        far_in = across(keep_in[1] + core_in[1])

        (down_keep, up_keep), (down_send, up_send) = fold((down_keep, up_keep), (down_got, up_got), [keep_in])
        down_got = swap(down_send, "dp", 3)
        up_got = over(up_send)
        tail_got = swap(tail_far + got_far, "dp", 1)
        tail_near = tail_near + got_near
        part_down = (down_keep + down_got)[0]
        part_up = up_keep + up_got
        far_up = across(part_up[2:])
        core_up = beside(jnp.stack([part_up[1], far_up[1]]))
        part_up = jnp.stack([part_up[0], core_up[0], far_up[0], core_up[1]])
        all_down = collect(part_down)
        all_up = collect(part_up)
        (tail_keep,), (tail_send,) = fold((tail_near,), (tail_got,), [all_down[1], all_down[2], all_up[1], far_in])
        part_tail = (tail_keep + swap(tail_send, "dp", 3))[0]

        far_tail = across(part_tail[near + outs:])
        message, = call(
            functools.partial(message_kernel, near, near + outs, vecs), "message", [arr(far_tail.shape)],
            [part_tail, far_tail], smem=0, marks=[])
        core_tail = beside(message)
        vec = part_tail[near + outs:near + outs + vecs] + far_tail[:vecs] + core_tail[lane_blocks:lane_blocks + vecs]
        owned = lax.ppermute(part_tail[near:near + outs], both, to_owner)
        part_tail = jnp.concatenate([
            part_tail[:lane_blocks], core_tail[:lane_blocks], far_tail[vecs:vecs + lane_blocks],
            core_tail[lane_blocks + vecs:], owned])
        all_tail = collect(part_tail)
        total_down, total_up = call(
            functools.partial(place_feed_kernel, splits, blocks, unit, at_quarter), "place_feed",
            [arr((unit, width)), arr((rows, units))],
            [idx, *all_down, *all_up])
        total_query, total_key, total_value, total_out = call(
            functools.partial(place_kernel, splits, at_quarter, tail_rows), "place",
            [arr((rows, width))] * 4,
            [idx, *all_tail])
    else:
        core_in = beside(send_in)
        far_in = across(keep_in[1] + core_in[1])
        total_down, total_up, tail = [
            lax.psum(lax.psum_scatter(g.reshape((blocks, -1) + g.shape[1:]), "blk", scatter_dimension=0, tiled=False), "dp")
            for g in (*feed_grads, *tail)
        ]
        total_down = total_down.reshape(unit, width)
        total_up = lax.all_to_all(total_up, "ulys", 0, 0, tiled=True)
        total_up = total_up.reshape(splits, rows, blocks, unit).transpose(1, 2, 0, 3).reshape(rows, units)
        tail = tail[0]
        total_out = lax.ppermute(tail[near:near + outs], both, to_owner).transpose(1, 0, 2).reshape(rows, width)
        vec = lax.psum(tail[near + outs:near + outs + vecs], "ulys")
        got = jnp.concatenate([tail[:near], tail[near + outs + vecs:]]).reshape(splits, lane_blocks, rows, 128)
        got = lax.all_to_all(got, "ulys", 0, 0, tiled=True).transpose(2, 0, 1, 3).reshape(rows, splits, lane_blocks * 128)
        total_query, total_key, total_value = (
            got[:, :, i * part:(i + 1) * part].reshape(rows, width) for i in range(3)
        )
    (hidden_grad,) = call(
        hidden_kernel, "hidden",
        [arr((tokens, width))],
        [idx, small, base, keep_in, core_in, far_in, middle_grad])

    output = mine[0] + small[3:4] + keep_out[0] + core_out[0] + far_out

    vec = vec.reshape(outs, EXTRA, 128).transpose(1, 0, 2).reshape(EXTRA, width)
    vector = lax.dynamic_slice(vec, (0, (b * splits + u) * rows), (8, rows))
    up_vector = lax.dynamic_slice(vec, (8 + u, b * unit), (1, unit))[0]
    return (
        output,
        hidden_grad,
        total_query,
        vector[0],
        total_key,
        total_value,
        vector[1],
        total_out,
        vector[2],
        total_up,
        up_vector,
        total_down,
        vector[3],
        vector[4],
        vector[5],
        vector[6],
        vector[7],
    )


def solution(mesh):
    tokens = P(("dp", "blk", "ulys"), None)
    matrix = P(("blk", "ulys"), None)
    vector = P(("blk", "ulys"))
    return jax.shard_map(
        local,
        mesh=mesh,
        in_specs=(
            tokens,
            P("dp", None),
            P("dp", "blk"),
            P("dp", "blk"),
            tokens,
            matrix,
            vector,
            matrix,
            matrix,
            vector,
            matrix,
            vector,
            matrix,
            vector,
            matrix,
            vector,
            vector,
            vector,
            vector,
            vector,
        ),
        out_specs=(
            tokens,
            tokens,
            matrix,
            vector,
            matrix,
            matrix,
            vector,
            matrix,
            vector,
            matrix,
            vector,
            matrix,
            vector,
            vector,
            vector,
            vector,
            vector,
        ),
        check_vma=False,
    )
```
